1024 devices in a mesh: lon: 64 (over z, y_hi, core), lat: 4 (over y_lo), segment: 4 (over x).
Axes of the slice: x: 4, y: 8 (y_hi: 2, y_lo: 4; y = y_hi * 4 + y_lo), z: 16, core: 2. Of those that a mesh axis runs over, the one named last changes fastest.
Arguments:
- inputs: bfloat16 [2, 64, 256, 512], P(None, 'lat', 'lon'), may hold values from -6 to 6
- cotangent: bfloat16 [2, 64, 256, 512], P(None, 'lat', 'lon'), may hold values from -6 to 6
- weights: bfloat16 [4, 3, 512, 512], P('segment'), may hold values from -0.15625 to 0.15625
- basis_values: float32 [64, 9, 3], replicated, may hold values from 0.05 to 0.5
- lat_step: int32 [64, 9], replicated, may hold values from -2 to 2, as said below
- lon_step: int32 [64, 9], replicated, may hold values from -2 to 2, as said below
Outputs:
- section_out: bfloat16 [4, 2, 64, 256, 512], P('segment', None, 'lat', 'lon')
- section_grad: bfloat16 [4, 2, 64, 256, 512], P('segment', None, 'lat', 'lon')
- weight_grad: float32 [4, 786432], P('segment', ('lon', 'lat'))
The draws below stay inside these ranges and needn't reach their ends.
Inputs may be any that keep to these rules, and one draw needn't show every extreme that they name: `lat_step`: row offsets of the support points; 2 and -2 each occur. `lon_step`: column offsets of the support points; 2 and -2 each occur.
All inputs are finite; a program needn't handle non-finite values.
Results may differ from the reference program's by a relative error of at most 0.017.
Values may be sent and summed in bfloat16 or wider, within the bound.
A program may use at most 32 MiB of HBM per device.

```python
import math
import jax
import jax.numpy as jnp
from jax import lax

C = 512
BASIS = 3
TAPS = 9
REACH = 2
MEMBERS = 2
SEGMENTS = 4
NLAT = 64
NLON = 256


def offsets(key):
    base_key, row_key = jax.random.split(key)
    offset_table = jax.random.randint(base_key, (NLAT, TAPS), -REACH, REACH + 1)
    picked = jax.random.randint(row_key, (2,), 0, NLAT)
    offset_table = offset_table.at[picked[0], 1].set(REACH)
    offset_table = offset_table.at[picked[1], 2].set(-REACH)
    return offset_table.astype(jnp.int32)


def draw_lat_step(key, part):
    return offsets(jax.random.fold_in(key, 11))


def draw_lon_step(key, part):
    return offsets(jax.random.fold_in(key, 23))


def levels(stream_key, extent, pieces, low, largest):
    def one(axis_at, parts):
        draws = jax.random.uniform(jax.random.fold_in(jax.random.fold_in(stream_key, 6), axis_at), (parts,), jnp.float32, low / len(pieces), largest / len(pieces))
        return jnp.repeat(jnp.exp(draws), extent[axis_at] // parts).reshape((-1,) + (1,) * (len(extent) - axis_at - 1))

    factor_of = one(*pieces[0])
    for cut in pieces[1:]:
        factor_of = factor_of * one(*cut)
    return factor_of


def gaussian(own_key, extent, scale, most, cuts=(), kind=jnp.bfloat16):
    values = jax.random.normal(own_key, extent, jnp.float32) * scale
    if len(cuts) > 0:
        values = levels(own_key, extent, cuts, -0.22, 0.18) * values
    return jnp.clip(values, min=-most, max=most).astype(kind)


def setup_inputs(seed: int = 0) -> dict:
    arg_keys = jax.random.split(jax.random.key(seed), 7)
    return {
        "inputs": gaussian(arg_keys[0], (MEMBERS, NLAT, NLON, C), 1.0, 6.0, ((1, 4), (2, 64))),
        "cotangent": gaussian(arg_keys[1], (MEMBERS, NLAT, NLON, C), 1.0, 6.0, ((1, 4), (2, 64))),
        "weights": gaussian(arg_keys[2], (SEGMENTS, BASIS, C, C), (BASIS * C) ** -0.5, 0.15625, ((0, 4),)),
        "basis_values": jnp.clip(jnp.exp(jax.random.uniform(arg_keys[3], (NLAT, TAPS, BASIS), jnp.float32, math.log(0.05), math.log(0.5))), 0.05, 0.5),
        "lat_step": draw_lat_step(jax.random.fold_in(arg_keys[6], 71), 0),
        "lon_step": draw_lon_step(jax.random.fold_in(arg_keys[6], 71), 0),
    }


def spread_taps(features, basis_values, lat_step, lon_step):
    lat_total = features.shape[1]
    lon_total = features.shape[2]
    row_ids = jnp.arange(lat_total, dtype=jnp.int32)
    col_ids = jnp.arange(lon_total, dtype=jnp.int32)
    summed = jnp.zeros((BASIS,) + features.shape, features.dtype)
    for tap_num in range(TAPS):
        source = row_ids + lat_step[:, tap_num].astype(jnp.int32)
        inside = (source >= 0) & (source < lat_total)
        source = jnp.clip(source, 0, lat_total - 1).astype(jnp.int32)
        column = ((col_ids[None, :] + lon_step[:, tap_num].astype(jnp.int32)[:, None]) % lon_total).astype(jnp.int32)
        picked = features[:, source[:, None], column, :]
        picked = jnp.where(inside[None, :, None, None], picked, jnp.zeros_like(picked))
        factor = jnp.transpose(basis_values[:, tap_num, :]).astype(features.dtype)
        summed = summed + factor[:, None, :, None, None] * picked[None]
    return summed

def reference(inputs, cotangent, weights, basis_values, lat_step, lon_step):
    depth_total = weights.shape[0]
    channels = inputs.shape[3]
    grad_scale = 1.0 / math.sqrt(inputs.shape[0] * inputs.shape[1] * inputs.shape[2])
    current = inputs
    stored = []
    section_outs = []
    for segment_num in range(depth_total):
        widened = current.astype(jnp.float32)
        spread = spread_taps(widened, basis_values, lat_step, lon_step).astype(jnp.bfloat16)
        mixed = jnp.zeros((spread.shape[1] * spread.shape[2] * spread.shape[3], channels), jnp.float32)
        for basis_num in range(BASIS):
            mixed = mixed + jnp.dot(spread[basis_num].reshape(-1, channels), weights[segment_num, basis_num], preferred_element_type=jnp.float32)
        mixed = mixed.reshape(widened.shape)
        result = (widened + jax.nn.silu(mixed)).astype(jnp.bfloat16)
        stored.append((widened, spread, mixed))
        section_outs.append(result)
        current = result
    grad = cotangent
    section_grads = [None] * depth_total
    weight_grads = [None] * depth_total
    for segment_num in reversed(range(depth_total)):
        widened, spread, mixed = stored[segment_num]
        sigma = jax.nn.sigmoid(mixed)
        gate_grad = (grad.astype(jnp.float32) * sigma * (1.0 + mixed * (1.0 - sigma))).astype(jnp.bfloat16)
        flat_gate = gate_grad.reshape(-1, channels)
        feature_grad = jnp.stack([jnp.dot(flat_gate, jnp.transpose(weights[segment_num, basis_num]), preferred_element_type=jnp.float32) for basis_num in range(BASIS)]).astype(jnp.bfloat16)
        feature_grad = lax.optimization_barrier(feature_grad).astype(jnp.float32).reshape(spread.shape)
        _, pull_back = jax.vjp(lambda values_in: spread_taps(values_in, basis_values, lat_step, lon_step), widened)
        pulled = pull_back(feature_grad)[0]
        new_grad = (grad.astype(jnp.float32) + pulled).astype(jnp.bfloat16)
        weight_grads[segment_num] = jnp.stack([jnp.dot(jnp.transpose(spread[basis_num].reshape(-1, channels)), flat_gate, preferred_element_type=jnp.float32) for basis_num in range(BASIS)]).reshape(-1) * grad_scale
        section_grads[segment_num] = new_grad
        grad = new_grad
    return (jnp.stack(section_outs), jnp.stack(section_grads), jnp.stack(weight_grads))
```

```python
import functools
import math

import jax
import jax.numpy as jnp
import numpy as np
from jax import lax
from jax.experimental import pallas as pl
from jax.experimental.pallas import tpu as pltpu
from jax.sharding import PartitionSpec as P

BASIS = 3
TAPS = 9
REACH = 2
LANES = 128
MESH = pl.DeviceIdType.MESH
F32 = jnp.float32
BF16 = jnp.bfloat16


def cell_index(row, col, rows, half):
    return (col // half) * (rows * half) + row * half + col % half


def halo_cells(rows, cols):
    cells = []
    for col in (-2, cols):
        cells += [(i, col + j) for i in range(rows) for j in range(2)]
    for row in (-2, rows):
        cells += [(row + i, j) for i in range(2) for j in range(cols)]
    for row in (-2, rows):
        for col in (-2, cols):
            cells += [(row + i, col + j) for i in range(2) for j in range(2)] + [None] * 4
    return cells


def static_tables(rows, cols, half):
    own = rows * cols
    cells = [None] * own
    for i in range(rows):
        for j in range(cols):
            cells[cell_index(i, j, rows, half)] = (i, j)
    halo = halo_cells(rows, cols)
    pick = np.zeros((len(halo), own), np.float32)
    for slot, cell in enumerate(halo):
        if cell is not None:
            pick[slot, cell_index(cell[0] % rows, cell[1] % cols, rows, half)] = 1
    near = rows + 8
    spots = cells + halo
    spot_rows = np.zeros((near, len(spots)), np.float32)
    spot_at = np.full((16, len(spots)), -100, np.int32)
    for s, cell in enumerate(spots):
        if cell is not None:
            spot_rows[cell[0] + REACH, s] = 1
            spot_at[0, s], spot_at[1, s] = cell
    own_rows = np.ascontiguousarray(spot_rows[:, :own].T)
    own_at = np.zeros((own, 2 * LANES), np.int32)
    own_at[:, :LANES] = spot_at[0, :own, None]
    own_at[:, LANES:] = spot_at[1, :own, None]
    return (
        pick.astype(jnp.bfloat16),
        own_rows.astype(jnp.bfloat16),
        own_at,
        spot_rows.astype(jnp.bfloat16),
        spot_at,
    )


def spot_of(row, col, rows, cols, half):
    own = rows * cols
    inner = (row >= 0) & (row < rows)
    mid = (col >= 0) & (col < cols)
    side = jnp.where(col < 0, col + 2, col - cols)
    far = jnp.where(row < 0, row + 2, row - rows)
    right = (col >= cols).astype(jnp.int32)
    down = (row >= rows).astype(jnp.int32)
    second = (col >= half).astype(jnp.int32)
    at_own = second * (rows * half) + row * half + col - second * half
    at_side = own + right * (2 * rows) + row * 2 + side
    base = own + 4 * rows
    at_far = base + down * (2 * cols) + far * cols + col
    at_corner = base + 4 * cols + (down * 2 + right) * 8 + far * 2 + side
    return jnp.where(
        inner, jnp.where(mid, at_own, at_side), jnp.where(mid, at_far, at_corner)
    )


def step_kernel(
    sizes,
    table_ref,
    pick_ref,
    own_rows_ref,
    own_at_ref,
    spot_rows_ref,
    spot_at_ref,
    in_ref,
    cot_ref,
    w_ref,
    out_ref,
    grad_ref,
    wg_ref,
    xp,
    gp,
    gown,
    hb,
    ahead,
    back,
    spread,
    spread_other,
    gate_other,
    slope,
    ob,
    gb,
    feat,
    product,
    blk,
    ysend,
    yrecv,
    acc,
    zsend,
    zrecv,
    fsend,
    frecv,
    cin_s,
    cin_r,
    hop_s,
    hop_r,
    halo_s,
    halo_r,
    oc_s,
    oc_r,
    pair_s,
    pair_r,
    y_s,
    y_r,
    z_s,
    z_r,
):
    n_seg, n_lat, n_z, scale = sizes
    half_cells, channels = in_ref.shape[1:]
    rows = table_ref.shape[0] - 16
    rows = rows // n_lat
    half = half_cells // rows
    cols = 2 * half
    own = rows * cols
    spots = 2 * own
    ring = 2 * n_lat
    steps = ring // 2
    share = BASIS * channels // (n_z * ring * 2)
    wide = channels // 2

    lon = lax.axis_index("lon")
    lat = lax.axis_index("lat")
    seg = lax.axis_index("segment")
    z = lon // 4
    member = (lon // 2) % 2
    core = lon % 2
    pos = z * 2 + core
    y = member * n_lat + lat

    def at(z_to, member_to, core_to, lat_to, seg_to=seg):
        return {"lon": z_to * 4 + member_to * 2 + core_to, "lat": lat_to, "segment": seg_to}

    def beside(shift, lat_to):
        place = lax.rem(pos + shift + 2 * n_z, 2 * n_z)
        return at(place // 2, member, place % 2, lat_to)

    has_up = lat > 0
    has_down = lat < n_lat - 1
    is_first = seg == 0
    is_last = seg == n_seg - 1
    matched = core == member

    base = 4 * rows
    corner = base + 4 * cols
    halo = [
        (0, 2 * rows, 1, 0),
        (2 * rows, 2 * rows, -1, 0),
        (base, 2 * cols, 0, 1),
        (base + 2 * cols, 2 * cols, 0, -1),
        (corner, 8, 1, 1),
        (corner + 8, 8, -1, 1),
        (corner + 16, 8, 1, -1),
        (corner + 24, 8, -1, -1),
    ]

    def sends_to(dlat):
        return has_down if dlat > 0 else has_up

    def gets_from(dlat):
        return has_up if dlat > 0 else has_down

    ring_next = lax.rem(y + 1, ring)
    ring_prev = lax.rem(y + ring - 1, ring)

    def on_ring(place):
        return at(z, place // n_lat, core, lax.rem(place, n_lat))

    partner = at(z, member, 1 - core, lat)

    barrier = pltpu.get_barrier_semaphore()

    def greet(device):
        pl.semaphore_signal(barrier, inc=1, device_id=device, device_id_type=MESH)

    for shift in range(1, n_z):
        greet(at(lax.rem(z + shift, n_z), member, core, lat))
    greet(on_ring(ring_next))
    greet(on_ring(ring_prev))
    greet(partner)
    for _, _, shift, dlat in halo:
        if dlat == 0:
            greet(beside(shift, lat))
        else:

            @pl.when(sends_to(dlat))
            def _():
                greet(beside(shift, lat + dlat))

    for other in range(2):

        @pl.when(jnp.logical_not(matched & (member == other)))
        def _():
            greet(at(z, other, member, lat))

        @pl.when(jnp.logical_not(matched & (core == other)))
        def _():
            greet(at(z, core, other, lat))

    @pl.when(jnp.logical_not(is_first))
    def _():
        greet(at(z, member, core, lat, seg - 1))

    @pl.when(jnp.logical_not(is_last))
    def _():
        greet(at(z, member, core, lat, seg + 1))

    met = (n_z - 1) + 3 + 2 + 4
    met = met + jnp.where(has_up, 3, 0) + jnp.where(has_down, 3, 0)
    met = met - jnp.where(matched, 2, 0)
    met = met + jnp.where(is_first, 0, 1) + jnp.where(is_last, 0, 1)
    pl.semaphore_wait(barrier, met)

    def remote(src, dst, send_sem, recv_sem, device):
        return pltpu.make_async_remote_copy(
            src_ref=src,
            dst_ref=dst,
            send_sem=send_sem,
            recv_sem=recv_sem,
            device_id=device,
            device_id_type=MESH,
        )

    def slot_of(buffer, part):
        return buffer.at[pl.ds(pl.multiple_of(part * half_cells, half_cells), half_cells), :]

    def regroup(source, buffer, which):
        for to in range(2):
            there = matched & (member == to)

            @pl.when(there)
            def _():
                pltpu.make_async_copy(
                    source.at[to], slot_of(buffer, core), cin_r.at[which, core]
                ).start()

            @pl.when(jnp.logical_not(there))
            def _():
                remote(
                    source.at[to],
                    slot_of(buffer, core),
                    cin_s.at[which, to],
                    cin_r.at[which, core],
                    at(z, to, member, lat),
                ).start()

    def regroup_arrived(source, buffer, which):
        for part in range(2):
            here = matched & (core == part)

            @pl.when(here)
            def _():
                pltpu.make_async_copy(
                    source.at[0], slot_of(buffer, part), cin_r.at[which, part]
                ).wait()

            @pl.when(jnp.logical_not(here))
            def _():
                remote(
                    source.at[0],
                    slot_of(buffer, part),
                    cin_s.at[which, 0],
                    cin_r.at[which, part],
                    partner,
                ).wait_recv()

    def regroup_sent(source, buffer, which):
        for to in range(2):

            @pl.when(jnp.logical_not(matched & (member == to)))
            def _():
                remote(
                    source.at[to],
                    slot_of(buffer, core),
                    cin_s.at[which, to],
                    cin_r.at[which, core],
                    partner,
                ).wait_send()

    @pl.when(is_first)
    def _():
        regroup(in_ref, xp, 0)

    @pl.when(is_last)
    def _():
        regroup(cot_ref, gown, 1)

    for buffer in (xp, gp):

        @pl.when(jnp.logical_not(has_up))
        def _():
            buffer[pl.ds(own + base, 2 * cols), :] = jnp.zeros((2 * cols, channels), BF16)
            buffer[pl.ds(own + corner, 16), :] = jnp.zeros((16, channels), BF16)

        @pl.when(jnp.logical_not(has_down))
        def _():
            buffer[pl.ds(own + base + 2 * cols, 2 * cols), :] = jnp.zeros((2 * cols, channels), BF16)
            buffer[pl.ds(own + corner + 16, 16), :] = jnp.zeros((16, channels), BF16)

    near_rows = rows + 8
    near = table_ref[pl.ds(pl.multiple_of(lat * rows, rows), near_rows), :]
    told = jnp.dot(own_rows_ref[...], near.astype(BF16), preferred_element_type=F32)
    tap_row = told[:, :LANES].astype(jnp.int32) + own_at_ref[:, :LANES]
    tap_col = told[:, LANES : 2 * LANES].astype(jnp.int32) + own_at_ref[:, LANES:]
    in_grid = (tap_row + lat * rows >= 0) & (tap_row + lat * rows < n_lat * rows)
    source = jnp.where(in_grid, spot_of(tap_row, tap_col, rows, cols, half), -1)
    lane = lax.broadcasted_iota(jnp.int32, (own, spots), 1)
    totals = [jnp.zeros((own, spots), F32) for _ in range(BASIS)]
    for tap in range(TAPS):
        hit = lane == source[:, tap : tap + 1]
        for b in range(BASIS):
            at_lane = 2 * LANES + b * TAPS + tap
            totals[b] = totals[b] + jnp.where(hit, told[:, at_lane : at_lane + 1], 0.0)
    for b in range(BASIS):
        ahead[pl.ds(b * own, own), :] = totals[b].astype(BF16)

    told_back = jnp.dot(
        jnp.transpose(near).astype(BF16), spot_rows_ref[...], preferred_element_type=F32
    )
    spot_row = jnp.broadcast_to(spot_at_ref[0:1, :], (16, spots))
    spot_col = jnp.broadcast_to(spot_at_ref[1:2, :], (16, spots))
    to_row = told_back[:16].astype(jnp.int32) + spot_row
    to_col = told_back[LANES : LANES + 16].astype(jnp.int32) + spot_col
    lands = (to_row >= 0) & (to_row < rows) & (to_col >= 0) & (to_col < cols)
    second = (to_col >= half).astype(jnp.int32)
    target = jnp.where(
        lands, second * (rows * half) + to_row * half + to_col - second * half, -1
    )
    level = lax.broadcasted_iota(jnp.int32, (own, spots), 0)
    totals = [jnp.zeros((own, spots), F32) for _ in range(BASIS)]
    for tap in range(TAPS):
        hit = level == target[tap : tap + 1, :]
        for b in range(BASIS):
            at_row = 2 * LANES + b * TAPS + tap
            totals[b] = totals[b] + jnp.where(hit, told_back[at_row : at_row + 1, :], 0.0)
    for b in range(BASIS):
        back[:, pl.ds(b * spots, spots)] = totals[b].astype(BF16)

    def halo_copy(buffer, phase, number):
        start, size, shift, dlat = halo[number]
        return remote(
            hb.at[phase, pl.ds(start, size), :],
            buffer.at[pl.ds(own + start, size), :],
            halo_s.at[phase, number],
            halo_r.at[phase, number],
            beside(shift, lat + dlat),
        )

    def halo_start(block, buffer, phase):
        hb[phase] = jnp.dot(pick_ref[...], block, preferred_element_type=F32).astype(BF16)
        for number in (4, 5, 6, 7, 2, 3, 0, 1):
            dlat = halo[number][3]
            if dlat == 0:
                halo_copy(buffer, phase, number).start()
            else:

                @pl.when(sends_to(dlat))
                def _():
                    halo_copy(buffer, phase, number).start()

    def halo_arrived(buffer, phase):
        for number in range(8):
            dlat = halo[number][3]
            if dlat == 0:
                halo_copy(buffer, phase, number).wait_recv()
            else:

                @pl.when(gets_from(dlat))
                def _():
                    halo_copy(buffer, phase, number).wait_recv()

    def halo_sent(buffer, phase):
        for number in range(8):
            dlat = halo[number][3]
            if dlat == 0:
                halo_copy(buffer, phase, number).wait_send()
            else:

                @pl.when(sends_to(dlat))
                def _():
                    halo_copy(buffer, phase, number).wait_send()

    def restore_copy(block, output, which, part, arrives_from):
        return remote(
            block.at[pl.ds(part * half_cells, half_cells), :],
            output.at[arrives_from],
            oc_s.at[which, part],
            oc_r.at[which, arrives_from],
            at(z, core, part, lat),
        )

    def restore_start(block, output, which):
        for part in range(2):
            there = matched & (core == part)

            @pl.when(there)
            def _():
                pltpu.make_async_copy(
                    block.at[pl.ds(part * half_cells, half_cells), :],
                    output.at[member],
                    oc_r.at[which, member],
                ).start()

            @pl.when(jnp.logical_not(there))
            def _():
                restore_copy(block, output, which, part, member).start()

    def restore_finish(block, output, which):
        for part in range(2):

            @pl.when(jnp.logical_not(matched & (core == part)))
            def _():
                restore_copy(block, output, which, part, member).wait_send()

        for origin in range(2):
            here = matched & (member == origin)

            @pl.when(here)
            def _():
                pltpu.make_async_copy(
                    block.at[pl.ds(0, half_cells), :],
                    output.at[origin],
                    oc_r.at[which, origin],
                ).wait()

            @pl.when(jnp.logical_not(here))
            def _():
                restore_copy(block, output, which, 0, origin).wait_recv()

    def hop_ahead():
        return remote(
            ob, xp.at[pl.ds(0, own), :], hop_s.at[0], hop_r.at[0], at(z, member, core, lat, seg + 1)
        )

    def hop_back():
        return remote(
            gb, gown, hop_s.at[1], hop_r.at[1], at(z, member, core, lat, seg - 1)
        )

    @pl.when(is_first)
    def _():
        regroup_arrived(in_ref, xp, 0)

    @pl.when(jnp.logical_not(is_first))
    def _():
        hop_ahead().wait_recv()

    halo_start(xp[pl.ds(0, own), :], xp, 0)
    halo_arrived(xp, 0)
    widened = xp[...]
    for b in range(BASIS):
        spread[pl.ds(b * own, own), :] = jnp.dot(
            ahead[pl.ds(b * own, own), :], widened, preferred_element_type=F32
        ).astype(BF16)
    mixed = jnp.dot(spread[pl.ds(0, own), :], w_ref[0], preferred_element_type=F32)
    for b in range(1, BASIS):
        mixed = mixed + jnp.dot(
            spread[pl.ds(b * own, own), :], w_ref[b], preferred_element_type=F32
        )
    sigma = 1.0 / (1.0 + jnp.exp(-mixed))
    ob[...] = (xp[pl.ds(0, own), :].astype(F32) + mixed * sigma).astype(BF16)

    @pl.when(jnp.logical_not(is_last))
    def _():
        hop_ahead().start()

    slope[...] = sigma * (1.0 + mixed * (1.0 - sigma))
    restore_start(ob, out_ref, 0)
    pair_spread = remote(spread, spread_other, pair_s.at[0], pair_r.at[0], partner)
    pair_spread.start()

    @pl.when(is_last)
    def _():
        regroup_arrived(cot_ref, gown, 1)

    @pl.when(jnp.logical_not(is_last))
    def _():
        hop_back().wait_recv()

    gate = (gown[...].astype(F32) * slope[...]).astype(BF16)
    gp[pl.ds(0, own), :] = gate
    halo_start(gate, gp, 1)
    pair_gate = remote(gp.at[pl.ds(0, own), :], gate_other, pair_s.at[1], pair_r.at[1], partner)
    pair_gate.start()
    pair_spread.wait_recv()
    pair_gate.wait_recv()

    columns = pl.ds(pl.multiple_of(core * wide, wide), wide)
    gate_both = jnp.concatenate(
        [gp[pl.ds(0, own), columns], gate_other[:, columns]], axis=0
    )
    for b in range(BASIS):
        both = jnp.concatenate(
            [spread[pl.ds(b * own, own), :], spread_other[pl.ds(b * own, own), :]], axis=0
        )
        term = scale * lax.dot_general(
            both, gate_both, (((0,), (0,)), ((), ())), preferred_element_type=F32
        )
        for part in range(wide // LANES):
            product[part, pl.ds(b * channels, channels), :] = term[
                :, part * LANES : (part + 1) * LANES
            ]

    halo_arrived(gp, 1)
    for b in range(BASIS):
        feat[pl.ds(b * spots, spots), :] = lax.dot_general(
            gp[...], w_ref[b], (((1,), (1,)), ((), ())), preferred_element_type=F32
        ).astype(BF16)
    pulled = jnp.dot(back[...], feat[...], preferred_element_type=F32)
    gb[...] = (gown[...].astype(F32) + pulled).astype(BF16)

    @pl.when(jnp.logical_not(is_first))
    def _():
        hop_back().start()

    restore_start(gb, grad_ref, 1)

    group = share * n_z
    for place in range(ring):
        for e in range(2):
            for i in range(share):
                first = ((place // n_lat) * 2 + e) * n_lat * share + (place % n_lat) * share + i
                for part in range(wide // LANES):
                    blk[place, pl.ds(e * group + i * n_z, n_z), pl.ds(part * LANES, LANES)] = product[
                        part, pl.ds(first, n_z, stride=ring * 2 * share), :
                    ].astype(BF16)

    def ring_copy(way, step):
        lo, size = (0, 2 * group) if step else (way * group, group)
        return remote(
            ysend.at[way, step, pl.ds(lo, size), :],
            yrecv.at[way, step, pl.ds(lo, size), :],
            y_s.at[way, step],
            y_r.at[way, step],
            on_ring(ring_next if way == 0 else ring_prev),
        )

    for step in range(steps):
        for way in range(2):
            distance = steps - step
            place = lax.rem(y + (distance if way == 0 else ring - distance), ring)
            if step == 0:
                lo = way * group
                ysend[way, step, pl.ds(lo, group), :] = blk[place, pl.ds(lo, group), :]
            else:
                ring_copy(way, step - 1).wait_recv()
                if step == 1:
                    lo, rest = way * group, (1 - way) * group
                    ysend[way, step, pl.ds(lo, group), :] = (
                        blk[place, pl.ds(lo, group), :].astype(F32)
                        + yrecv[way, 0, pl.ds(lo, group), :].astype(F32)
                    ).astype(BF16)
                    ysend[way, step, pl.ds(rest, group), :] = blk[place, pl.ds(rest, group), :]
                else:
                    ysend[way, step] = (
                        blk[place].astype(F32) + yrecv[way, step - 1].astype(F32)
                    ).astype(BF16)
            ring_copy(way, step).start()
    summed = blk[y].astype(F32)
    for way in range(2):
        ring_copy(way, steps - 1).wait_recv()
        summed = summed + yrecv[way, steps - 1].astype(F32)
    for part in range(wide // LANES):
        acc[part] = summed[:, part * LANES : (part + 1) * LANES]

    def z_copy(shift):
        to = lax.rem(z + shift, n_z)
        return remote(
            zsend.at[to], zrecv.at[z], z_s.at[shift], z_r.at[shift], at(to, member, core, lat)
        )

    for to in range(n_z):
        for part in range(wide // LANES):
            zsend[to, pl.ds(0, 2 * share), pl.ds(part * LANES, LANES)] = acc[
                part, pl.ds(to, 2 * share, stride=n_z), :
            ].astype(BF16)
    for shift in range(1, n_z):
        z_copy(shift).start()
    total = zsend[z][: 2 * share].astype(F32)
    for shift in range(1, n_z):
        from_z = lax.rem(z + n_z - shift, n_z)
        remote(
            zsend.at[0], zrecv.at[from_z], z_s.at[shift], z_r.at[shift], partner
        ).wait_recv()
        total = total + zrecv[from_z][: 2 * share].astype(F32)
    mine = jnp.where(core == 0, total[:share], total[share:])
    fsend[pl.ds(0, share), :] = jnp.where(core == 0, total[share:], total[:share])
    last = remote(fsend, frecv, pair_s.at[2], pair_r.at[2], partner)
    last.start()
    last.wait_recv()
    theirs = frecv[pl.ds(0, share), :]
    wg_ref[:, :wide] = jnp.where(core == 0, mine, theirs)
    wg_ref[:, wide:] = jnp.where(core == 0, theirs, mine)

    restore_finish(ob, out_ref, 0)
    restore_finish(gb, grad_ref, 1)

    @pl.when(is_first)
    def _():
        regroup_sent(in_ref, xp, 0)

    @pl.when(is_last)
    def _():
        regroup_sent(cot_ref, gown, 1)

    @pl.when(jnp.logical_not(is_last))
    def _():
        hop_ahead().wait_send()

    @pl.when(jnp.logical_not(is_first))
    def _():
        hop_back().wait_send()

    halo_sent(xp, 0)
    halo_sent(gp, 1)
    pair_spread.wait_send()
    pair_gate.wait_send()
    last.wait_send()
    for step in range(steps):
        for way in range(2):
            ring_copy(way, step).wait_send()
    for shift in range(1, n_z):
        z_copy(shift).wait_send()


def per_device(inputs, cotangent, weights, basis_values, lat_step, lon_step):
    members, rows, half, channels = inputs.shape
    n_lon, n_lat, n_seg = (lax.axis_size(name) for name in ("lon", "lat", "segment"))
    n_z = n_lon // 4
    cols = 2 * half
    own = rows * cols
    spots = 2 * own
    ring = 2 * n_lat
    share = BASIS * channels // (n_lon * n_lat)
    wide = channels // 2
    scale = 1.0 / math.sqrt(members * rows * n_lat * half * n_lon)

    def padded(table):
        table = table.astype(F32)
        return jnp.pad(table, ((REACH, 16 - REACH), (0, LANES - table.shape[1])))

    by_basis = jnp.transpose(basis_values, (0, 2, 1)).reshape(rows * n_lat, BASIS * TAPS)
    table = jnp.concatenate([padded(lat_step), padded(lon_step), padded(by_basis)], axis=1)
    constants = [jnp.asarray(t) for t in static_tables(rows, cols, half)]
    vmem = pl.BlockSpec(memory_space=pltpu.VMEM)
    dma = pltpu.SemaphoreType.DMA
    section_out, section_grad, weight_grad = pl.pallas_call(
        functools.partial(step_kernel, (n_seg, n_lat, n_z, scale)),
        out_shape=(
            jax.ShapeDtypeStruct((2, rows * half, channels), BF16),
            jax.ShapeDtypeStruct((2, rows * half, channels), BF16),
            jax.ShapeDtypeStruct((share, channels), F32),
        ),
        in_specs=[vmem] * 9,
        out_specs=(vmem, vmem, vmem),
        scratch_shapes=[
            pltpu.VMEM((spots, channels), BF16),
            pltpu.VMEM((spots, channels), BF16),
            pltpu.VMEM((own, channels), BF16),
            pltpu.VMEM((2, own, channels), BF16),
            pltpu.VMEM((BASIS * own, spots), BF16),
            pltpu.VMEM((own, BASIS * spots), BF16),
            pltpu.VMEM((BASIS * own, channels), BF16),
            pltpu.VMEM((BASIS * own, channels), BF16),
            pltpu.VMEM((own, channels), BF16),
            pltpu.VMEM((own, channels), F32),
            pltpu.VMEM((own, channels), BF16),
            pltpu.VMEM((own, channels), BF16),
            pltpu.VMEM((BASIS * spots, channels), BF16),
            pltpu.VMEM((wide // LANES, BASIS * channels, LANES), F32),
            pltpu.VMEM((ring, 2 * share * n_z, wide), BF16),
            pltpu.VMEM((2, n_lat, 2 * share * n_z, wide), BF16),
            pltpu.VMEM((2, n_lat, 2 * share * n_z, wide), BF16),
            pltpu.VMEM((wide // LANES, 2 * share * n_z, LANES), F32),
            pltpu.VMEM((n_z, -(-2 * share // 16) * 16, wide), BF16),
            pltpu.VMEM((n_z, -(-2 * share // 16) * 16, wide), BF16),
            pltpu.VMEM((-(-share // 8) * 8, wide), F32),
            pltpu.VMEM((-(-share // 8) * 8, wide), F32),
            dma((2, 2)),
            dma((2, 2)),
            dma((2,)),
            dma((2,)),
            dma((2, 8)),
            dma((2, 8)),
            dma((2, 2)),
            dma((2, 2)),
            dma((3,)),
            dma((3,)),
            dma((2, n_lat)),
            dma((2, n_lat)),
            dma((n_z,)),
            dma((n_z,)),
        ],
        compiler_params=pltpu.CompilerParams(
            collective_id=0, has_side_effects=True, vmem_limit_bytes=48 * 1024 * 1024
        ),
        name="section_step",
    )(
        table,
        *constants,
        inputs.reshape(members, rows * half, channels),
        cotangent.reshape(members, rows * half, channels),
        weights[0],
    )
    block = (1,) + inputs.shape
    return (
        section_out.reshape(block),
        section_grad.reshape(block),
        weight_grad.reshape(1, -1),
    )


def solution(mesh):
    return jax.shard_map(
        per_device,
        mesh=mesh,
        in_specs=(
            P(None, "lat", "lon", None),
            P(None, "lat", "lon", None),
            P("segment", None, None, None),
            P(),
            P(),
            P(),
        ),
        out_specs=(
            P("segment", None, "lat", "lon", None),
            P("segment", None, "lat", "lon", None),
            P("segment", ("lon", "lat")),
        ),
        check_vma=False,
    )
```

```python
import functools
import math

import jax
import jax.numpy as jnp
from jax import lax
from jax.experimental import pallas as pl
from jax.experimental.pallas import tpu as pltpu
from jax.sharding import PartitionSpec as P

BASIS = 3
TAPS = 9
REACH = 2
LANES = 128
MESH = pl.DeviceIdType.MESH
F32 = jnp.float32
BF16 = jnp.bfloat16


def log2(number):
    power = number.bit_length() - 1
    assert 1 << power == number
    return power


def over(x, number):
    return lax.shift_right_arithmetic(x, jnp.full_like(x, log2(number)))


def rest(x, number):
    return x & (number - 1)


def halo_cell(slot, rows, cols):
    base = 4 * rows
    at = slot
    side_row = over(rest(at, 2 * rows), 2)
    side_col = rest(at, 2) + jnp.where(at < 2 * rows, -2, cols)
    at = slot - base
    far_row = over(rest(at, 2 * cols), cols) + jnp.where(at < 2 * cols, -2, rows)
    far_col = rest(at, cols)
    at = slot - base - 4 * cols
    inside = rest(at, 8)
    corner_row = over(inside, 2) + jnp.where(at < 16, -2, rows)
    corner_col = rest(inside, 2) + jnp.where(rest(over(at, 8), 2) == 0, -2, cols)
    in_side = slot < base
    in_far = slot < base + 4 * cols
    row = jnp.where(in_side, side_row, jnp.where(in_far, far_row, corner_row))
    col = jnp.where(in_side, side_col, jnp.where(in_far, far_col, corner_col))
    used = in_far | (inside < 4)
    return row, col, used


def own_cell(spot, rows, half):
    second = over(spot, rows * half)
    at = rest(spot, rows * half)
    return over(at, half), rest(at, half) + second * half


def spot_of(row, col, rows, cols, half):
    own = rows * cols
    inner = (row >= 0) & (row < rows)
    mid = (col >= 0) & (col < cols)
    side = jnp.where(col < 0, col + 2, col - cols)
    far = jnp.where(row < 0, row + 2, row - rows)
    right = (col >= cols).astype(jnp.int32)
    down = (row >= rows).astype(jnp.int32)
    second = (col >= half).astype(jnp.int32)
    at_own = second * (rows * half) + row * half + col - second * half
    at_side = own + right * (2 * rows) + row * 2 + side
    base = own + 4 * rows
    at_far = base + down * (2 * cols) + far * cols + col
    at_corner = base + 4 * cols + (down * 2 + right) * 8 + far * 2 + side
    return jnp.where(
        inner, jnp.where(mid, at_own, at_side), jnp.where(mid, at_far, at_corner)
    )


def step_kernel(
    sizes,
    lat_hbm,
    lon_hbm,
    basis_hbm,
    in_ref,
    cot_ref,
    w_hbm,
    out_ref,
    grad_ref,
    wg_ref,
    lat_ref,
    lon_ref,
    basis_ref,
    w_ref,
    raw,
    pick,
    xp,
    gp,
    gown,
    hb,
    ahead,
    back,
    spread,
    spread_other,
    gate_other,
    slope,
    ob,
    gb,
    feat,
    product,
    blk,
    ysend,
    yrecv,
    acc,
    zsend,
    zrecv,
    fsend,
    frecv,
    cin_s,
    cin_r,
    hop_s,
    hop_r,
    halo_s,
    halo_r,
    oc_s,
    oc_r,
    pair_s,
    pair_r,
    y_s,
    y_r,
    z_s,
    z_r,
    w_sem,
):
    n_seg, n_lat, n_z, scale = sizes
    rows, half, channels = in_ref.shape[1:]
    half_cells = rows * half
    cols = 2 * half
    own = rows * cols
    spots = 2 * own
    ring = 2 * n_lat
    steps = ring // 2
    share = BASIS * channels // (n_z * ring * 2)
    wide = channels // 2

    lon = lax.axis_index("lon")
    lat = lax.axis_index("lat")
    seg = lax.axis_index("segment")
    z = lon // 4
    member = (lon // 2) % 2
    core = lon % 2
    pos = z * 2 + core
    y = member * n_lat + lat

    def at(z_to, member_to, core_to, lat_to, seg_to=seg):
        return {"lon": z_to * 4 + member_to * 2 + core_to, "lat": lat_to, "segment": seg_to}

    def beside(shift, lat_to):
        place = lax.rem(pos + shift + 2 * n_z, 2 * n_z)
        return at(place // 2, member, place % 2, lat_to)

    has_up = lat > 0
    has_down = lat < n_lat - 1
    is_first = seg == 0
    is_last = seg == n_seg - 1
    matched = core == member

    base = 4 * rows
    corner = base + 4 * cols
    halo = [
        (0, 2 * rows, 1, 0),
        (2 * rows, 2 * rows, -1, 0),
        (base, 2 * cols, 0, 1),
        (base + 2 * cols, 2 * cols, 0, -1),
        (corner, 8, 1, 1),
        (corner + 8, 8, -1, 1),
        (corner + 16, 8, 1, -1),
        (corner + 24, 8, -1, -1),
    ]

    def sends_to(dlat):
        return has_down if dlat > 0 else has_up

    def gets_from(dlat):
        return has_up if dlat > 0 else has_down

    ring_next = lax.rem(y + 1, ring)
    ring_prev = lax.rem(y + ring - 1, ring)

    def on_ring(place):
        return at(z, place // n_lat, core, lax.rem(place, n_lat))

    partner = at(z, member, 1 - core, lat)

    fetch = pltpu.make_async_copy(w_hbm, w_ref, w_sem.at[0])
    tables = [
        pltpu.make_async_copy(table_hbm, table_ref, w_sem.at[1 + number])
        for number, (table_hbm, table_ref) in enumerate(
            ((lat_hbm, lat_ref), (lon_hbm, lon_ref), (basis_hbm, basis_ref))
        )
    ]
    for table in tables:
        table.start()
    fetch.start()

    barrier = pltpu.get_barrier_semaphore()

    def greet(device):
        pl.semaphore_signal(barrier, inc=1, device_id=device, device_id_type=MESH)

    for shift in range(1, n_z):
        greet(at(lax.rem(z + shift, n_z), member, core, lat))
    greet(on_ring(ring_next))
    greet(on_ring(ring_prev))
    greet(partner)
    for _, _, shift, dlat in halo:
        if dlat == 0:
            greet(beside(shift, lat))
        else:

            @pl.when(sends_to(dlat))
            def _():
                greet(beside(shift, lat + dlat))

    for other in range(2):

        @pl.when(jnp.logical_not(matched & (member == other)))
        def _():
            greet(at(z, other, member, lat))

        @pl.when(jnp.logical_not(matched & (core == other)))
        def _():
            greet(at(z, core, other, lat))

    @pl.when(jnp.logical_not(is_first))
    def _():
        greet(at(z, member, core, lat, seg - 1))

    @pl.when(jnp.logical_not(is_last))
    def _():
        greet(at(z, member, core, lat, seg + 1))

    met = (n_z - 1) + 3 + 2 + 4
    met = met + jnp.where(has_up, 3, 0) + jnp.where(has_down, 3, 0)
    met = met - jnp.where(matched, 2, 0)
    met = met + jnp.where(is_first, 0, 1) + jnp.where(is_last, 0, 1)
    pl.semaphore_wait(barrier, met)

    def remote(src, dst, send_sem, recv_sem, device):
        return pltpu.make_async_remote_copy(
            src_ref=src,
            dst_ref=dst,
            send_sem=send_sem,
            recv_sem=recv_sem,
            device_id=device,
            device_id_type=MESH,
        )

    def slot_of(buffer, part):
        return buffer.at[part]

    def regroup(source, buffer, which):
        for to in range(2):
            there = matched & (member == to)

            @pl.when(there)
            def _():
                pltpu.make_async_copy(
                    source.at[to], slot_of(buffer, core), cin_r.at[which, core]
                ).start()

            @pl.when(jnp.logical_not(there))
            def _():
                remote(
                    source.at[to],
                    slot_of(buffer, core),
                    cin_s.at[which, to],
                    cin_r.at[which, core],
                    at(z, to, member, lat),
                ).start()

    def regroup_arrived(source, buffer, which):
        for part in range(2):
            here = matched & (core == part)

            @pl.when(here)
            def _():
                pltpu.make_async_copy(
                    source.at[0], slot_of(buffer, part), cin_r.at[which, part]
                ).wait()

            @pl.when(jnp.logical_not(here))
            def _():
                remote(
                    source.at[0],
                    slot_of(buffer, part),
                    cin_s.at[which, 0],
                    cin_r.at[which, part],
                    partner,
                ).wait_recv()

    def regroup_sent(source, buffer, which):
        for to in range(2):

            @pl.when(jnp.logical_not(matched & (member == to)))
            def _():
                remote(
                    source.at[to],
                    slot_of(buffer, core),
                    cin_s.at[which, to],
                    cin_r.at[which, core],
                    partner,
                ).wait_send()

    @pl.when(is_first)
    def _():
        regroup(in_ref, raw.at[0], 0)

    @pl.when(is_last)
    def _():
        regroup(cot_ref, raw.at[1], 1)

    for buffer in (xp, gp):

        @pl.when(jnp.logical_not(has_up))
        def _():
            buffer[pl.ds(own + base, 2 * cols), :] = jnp.zeros((2 * cols, channels), BF16)
            buffer[pl.ds(own + corner, 16), :] = jnp.zeros((16, channels), BF16)

        @pl.when(jnp.logical_not(has_down))
        def _():
            buffer[pl.ds(own + base + 2 * cols, 2 * cols), :] = jnp.zeros((2 * cols, channels), BF16)
            buffer[pl.ds(own + corner + 16, 16), :] = jnp.zeros((16, channels), BF16)

    spot = lax.broadcasted_iota(jnp.int32, (16, spots), 1)
    inner_row, inner_col = own_cell(spot, rows, half)
    outer_row, outer_col, used = halo_cell(spot - own, rows, cols)
    spot_row = jnp.where(spot < own, inner_row, outer_row)
    spot_col = jnp.where(spot < own, inner_col, outer_col)
    used = (spot < own) | used
    grid_row = jnp.where(used, spot_row + lat * rows, -1)[:1]
    total_rows = n_lat * rows
    chosen = (
        lax.broadcasted_iota(jnp.int32, (total_rows, spots), 0)
        == jnp.broadcast_to(grid_row, (total_rows, spots))
    ).astype(F32).astype(BF16)

    for table in tables:
        table.wait()

    def of_spot(taps):
        return jnp.dot(taps.astype(F32).astype(BF16), chosen, preferred_element_type=F32)

    to_row = of_spot(lat_ref[...]).astype(jnp.int32) + spot_row[:TAPS]
    to_col = of_spot(lon_ref[...]).astype(jnp.int32) + spot_col[:TAPS]
    worth = [of_spot(basis_ref[:, b, :]) for b in range(BASIS)]

    lands = (to_row >= 0) & (to_row < rows) & (to_col >= 0) & (to_col < cols)
    second = (to_col >= half).astype(jnp.int32)
    target = jnp.where(
        lands, second * (rows * half) + to_row * half + to_col - second * half, -1
    )
    level = lax.broadcasted_iota(jnp.int32, (own, spots), 0)
    totals = [jnp.zeros((own, spots), F32) for _ in range(BASIS)]
    for tap in range(TAPS):
        hit = level == target[tap : tap + 1, :]
        for b in range(BASIS):
            totals[b] = totals[b] + jnp.where(hit, worth[b][tap : tap + 1, :], 0.0)
    for b in range(BASIS):
        back[:, pl.ds(b * spots, spots)] = totals[b].astype(BF16)

    tap_row, tap_col = to_row[:, :own], to_col[:, :own]
    in_grid = (tap_row + lat * rows >= 0) & (tap_row + lat * rows < total_rows)
    source = jnp.where(in_grid, spot_of(tap_row, tap_col, rows, cols, half), -1)
    level = lax.broadcasted_iota(jnp.int32, (spots, own), 0)
    totals = [jnp.zeros((spots, own), F32) for _ in range(BASIS)]
    for tap in range(TAPS):
        hit = level == source[tap : tap + 1, :]
        for b in range(BASIS):
            totals[b] = totals[b] + jnp.where(hit, worth[b][tap : tap + 1, :own], 0.0)
    for b in range(BASIS):
        ahead[pl.ds(b * own, own), :] = jnp.transpose(totals[b]).astype(BF16)

    slot = lax.broadcasted_iota(jnp.int32, (own, own), 0)
    pick_row, pick_col, used = halo_cell(slot, rows, cols)
    pick_row, pick_col = rest(pick_row, rows), rest(pick_col, cols)
    wanted = over(pick_col, half) * (rows * half) + pick_row * half + rest(pick_col, half)
    wanted = jnp.where(used, wanted, -1)
    pick[...] = (
        (lax.broadcasted_iota(jnp.int32, (own, own), 1) == wanted).astype(F32).astype(BF16)
    )

    def halo_copy(buffer, phase, number):
        start, size, shift, dlat = halo[number]
        return remote(
            hb.at[phase, pl.ds(start, size), :],
            buffer.at[pl.ds(own + start, size), :],
            halo_s.at[phase, number],
            halo_r.at[phase, number],
            beside(shift, lat + dlat),
        )

    def halo_start(block, buffer, phase):
        hb[phase] = jnp.dot(pick[...], block, preferred_element_type=F32).astype(BF16)
        for number in (4, 5, 6, 7, 2, 3, 0, 1):
            dlat = halo[number][3]
            if dlat == 0:
                halo_copy(buffer, phase, number).start()
            else:

                @pl.when(sends_to(dlat))
                def _():
                    halo_copy(buffer, phase, number).start()

    def halo_arrived(buffer, phase):
        for number in range(8):
            dlat = halo[number][3]
            if dlat == 0:
                halo_copy(buffer, phase, number).wait_recv()
            else:

                @pl.when(gets_from(dlat))
                def _():
                    halo_copy(buffer, phase, number).wait_recv()

    def halo_sent(buffer, phase):
        for number in range(8):
            dlat = halo[number][3]
            if dlat == 0:
                halo_copy(buffer, phase, number).wait_send()
            else:

                @pl.when(sends_to(dlat))
                def _():
                    halo_copy(buffer, phase, number).wait_send()

    def restore_copy(block, output, which, part, arrives_from):
        return remote(
            block.at[pl.ds(part * half_cells, half_cells), :],
            output.at[arrives_from],
            oc_s.at[which, part],
            oc_r.at[which, arrives_from],
            at(z, core, part, lat),
        )

    def restore_start(block, output, which):
        for part in range(2):
            there = matched & (core == part)

            @pl.when(there)
            def _():
                pltpu.make_async_copy(
                    block.at[pl.ds(part * half_cells, half_cells), :],
                    output.at[member],
                    oc_r.at[which, member],
                ).start()

            @pl.when(jnp.logical_not(there))
            def _():
                restore_copy(block, output, which, part, member).start()

    def restore_finish(block, output, which):
        for part in range(2):

            @pl.when(jnp.logical_not(matched & (core == part)))
            def _():
                restore_copy(block, output, which, part, member).wait_send()

        for origin in range(2):
            here = matched & (member == origin)

            @pl.when(here)
            def _():
                pltpu.make_async_copy(
                    block.at[pl.ds(0, half_cells), :],
                    output.at[origin],
                    oc_r.at[which, origin],
                ).wait()

            @pl.when(jnp.logical_not(here))
            def _():
                restore_copy(block, output, which, 0, origin).wait_recv()

    def hop_ahead():
        return remote(
            ob, xp.at[pl.ds(0, own), :], hop_s.at[0], hop_r.at[0], at(z, member, core, lat, seg + 1)
        )

    def hop_back():
        return remote(
            gb, gown, hop_s.at[1], hop_r.at[1], at(z, member, core, lat, seg - 1)
        )

    @pl.when(is_first)
    def _():
        regroup_arrived(in_ref, raw.at[0], 0)
        xp[pl.ds(0, own), :] = raw[0].reshape(own, channels)

    @pl.when(jnp.logical_not(is_first))
    def _():
        hop_ahead().wait_recv()

    halo_start(xp[pl.ds(0, own), :], xp, 0)
    halo_arrived(xp, 0)
    widened = xp[...]
    for b in range(BASIS):
        spread[pl.ds(b * own, own), :] = jnp.dot(
            ahead[pl.ds(b * own, own), :], widened, preferred_element_type=F32
        ).astype(BF16)
    fetch.wait()
    mixed = jnp.dot(spread[pl.ds(0, own), :], w_ref[0], preferred_element_type=F32)
    for b in range(1, BASIS):
        mixed = mixed + jnp.dot(
            spread[pl.ds(b * own, own), :], w_ref[b], preferred_element_type=F32
        )
    sigma = 1.0 / (1.0 + jnp.exp(-mixed))
    ob[...] = (xp[pl.ds(0, own), :].astype(F32) + mixed * sigma).astype(BF16)

    @pl.when(jnp.logical_not(is_last))
    def _():
        hop_ahead().start()

    slope[...] = sigma * (1.0 + mixed * (1.0 - sigma))
    restore_start(ob, out_ref, 0)
    pair_spread = remote(spread, spread_other, pair_s.at[0], pair_r.at[0], partner)
    pair_spread.start()

    @pl.when(is_last)
    def _():
        regroup_arrived(cot_ref, raw.at[1], 1)
        gown[...] = raw[1].reshape(own, channels)

    @pl.when(jnp.logical_not(is_last))
    def _():
        hop_back().wait_recv()

    gate = (gown[...].astype(F32) * slope[...]).astype(BF16)
    gp[pl.ds(0, own), :] = gate
    halo_start(gate, gp, 1)
    pair_gate = remote(gp.at[pl.ds(0, own), :], gate_other, pair_s.at[1], pair_r.at[1], partner)
    pair_gate.start()
    pair_spread.wait_recv()
    pair_gate.wait_recv()

    columns = pl.ds(pl.multiple_of(core * wide, wide), wide)
    gate_both = jnp.concatenate(
        [gp[pl.ds(0, own), columns], gate_other[:, columns]], axis=0
    )
    for b in range(BASIS):
        both = jnp.concatenate(
            [spread[pl.ds(b * own, own), :], spread_other[pl.ds(b * own, own), :]], axis=0
        )
        term = scale * lax.dot_general(
            both, gate_both, (((0,), (0,)), ((), ())), preferred_element_type=F32
        )
        for part in range(wide // LANES):
            product[part, pl.ds(b * channels, channels), :] = term[
                :, part * LANES : (part + 1) * LANES
            ]

    group = share * n_z

    def ring_copy(way, step, e):
        return remote(
            ysend.at[way, step, pl.ds(e * group, group), :],
            yrecv.at[way, step, pl.ds(e * group, group), :],
            y_s.at[way, step, e],
            y_r.at[way, step, e],
            on_ring(ring_next if way == 0 else ring_prev),
        )

    def ring_step(step, way, e):
        distance = steps - step
        place = lax.rem(y + (distance if way == 0 else ring - distance), ring)
        part = pl.ds(e * group, group)
        term = blk[place, part, :]
        if step > 1 or (step == 1 and e == way):
            ring_copy(way, step - 1, e).wait_recv()
            term = (term.astype(F32) + yrecv[way, step - 1, part, :].astype(F32)).astype(BF16)
        ysend[way, step, part, :] = term
        ring_copy(way, step, e).start()

    def ring_begin():
        for place in range(ring):
            for e in range(2):
                for i in range(share):
                    first = ((place // n_lat) * 2 + e) * n_lat * share + (place % n_lat) * share + i
                    for part in range(wide // LANES):
                        blk[
                            place, pl.ds(e * group + i * n_z, n_z), pl.ds(part * LANES, LANES)
                        ] = product[part, pl.ds(first, n_z, stride=ring * 2 * share), :].astype(BF16)
        for way in range(2):
            ring_step(0, way, way)
        for way in range(2):
            ring_step(1, way, 1 - way)

    pl.when(is_first)(ring_begin)

    halo_arrived(gp, 1)
    for b in range(BASIS):
        feat[pl.ds(b * spots, spots), :] = lax.dot_general(
            gp[...], w_ref[b], (((1,), (1,)), ((), ())), preferred_element_type=F32
        ).astype(BF16)
    pulled = jnp.dot(back[...], feat[...], preferred_element_type=F32)
    gb[...] = (gown[...].astype(F32) + pulled).astype(BF16)

    @pl.when(jnp.logical_not(is_first))
    def _():
        hop_back().start()

    restore_start(gb, grad_ref, 1)

    pl.when(jnp.logical_not(is_first))(ring_begin)
    for way in range(2):
        ring_step(1, way, way)
    for step in range(2, steps):
        for half_turn in range(2):
            for way in range(2):
                ring_step(step, way, way if half_turn else 1 - way)
    summed = blk[y].astype(F32)
    for way in range(2):
        for e in range(2):
            ring_copy(way, steps - 1, e).wait_recv()
        summed = summed + yrecv[way, steps - 1].astype(F32)
    for part in range(wide // LANES):
        acc[part] = summed[:, part * LANES : (part + 1) * LANES]

    def z_copy(shift):
        to = lax.rem(z + shift, n_z)
        return remote(
            zsend.at[to], zrecv.at[z], z_s.at[shift], z_r.at[shift], at(to, member, core, lat)
        )

    for to in range(n_z):
        for part in range(wide // LANES):
            zsend[to, pl.ds(0, 2 * share), pl.ds(part * LANES, LANES)] = acc[
                part, pl.ds(to, 2 * share, stride=n_z), :
            ].astype(BF16)
    for shift in range(1, n_z):
        z_copy(shift).start()
    total = zsend[z][: 2 * share].astype(F32)
    for shift in range(1, n_z):
        from_z = lax.rem(z + n_z - shift, n_z)
        remote(
            zsend.at[0], zrecv.at[from_z], z_s.at[shift], z_r.at[shift], partner
        ).wait_recv()
        total = total + zrecv[from_z][: 2 * share].astype(F32)
    mine = jnp.where(core == 0, total[:share], total[share:])
    fsend[pl.ds(0, share), :] = jnp.where(core == 0, total[share:], total[:share])
    last = remote(fsend, frecv, pair_s.at[2], pair_r.at[2], partner)
    last.start()
    last.wait_recv()
    theirs = frecv[pl.ds(0, share), :]
    wg_ref[:, :wide] = jnp.where(core == 0, mine, theirs)
    wg_ref[:, wide:] = jnp.where(core == 0, theirs, mine)

    restore_finish(ob, out_ref, 0)
    restore_finish(gb, grad_ref, 1)

    @pl.when(is_first)
    def _():
        regroup_sent(in_ref, raw.at[0], 0)

    @pl.when(is_last)
    def _():
        regroup_sent(cot_ref, raw.at[1], 1)

    @pl.when(jnp.logical_not(is_last))
    def _():
        hop_ahead().wait_send()

    @pl.when(jnp.logical_not(is_first))
    def _():
        hop_back().wait_send()

    halo_sent(xp, 0)
    halo_sent(gp, 1)
    pair_spread.wait_send()
    pair_gate.wait_send()
    last.wait_send()
    for step in range(steps):
        for way in range(2):
            for e in range(2):
                if step or e == way:
                    ring_copy(way, step, e).wait_send()
    for shift in range(1, n_z):
        z_copy(shift).wait_send()


def per_device(inputs, cotangent, weights, basis_values, lat_step, lon_step):
    members, rows, half, channels = inputs.shape
    n_lon, n_lat, n_seg = (lax.axis_size(name) for name in ("lon", "lat", "segment"))
    n_z = n_lon // 4
    cols = 2 * half
    own = rows * cols
    spots = 2 * own
    ring = 2 * n_lat
    share = BASIS * channels // (n_lon * n_lat)
    wide = channels // 2
    scale = 1.0 / math.sqrt(members * rows * n_lat * half * n_lon)

    vmem = pl.BlockSpec(memory_space=pltpu.VMEM)
    hbm = pl.BlockSpec(memory_space=pltpu.HBM)
    dma = pltpu.SemaphoreType.DMA
    section_out, section_grad, weight_grad = pl.pallas_call(
        functools.partial(step_kernel, (n_seg, n_lat, n_z, scale)),
        out_shape=(
            jax.ShapeDtypeStruct((2, rows * half, channels), BF16),
            jax.ShapeDtypeStruct((2, rows * half, channels), BF16),
            jax.ShapeDtypeStruct((share, channels), F32),
        ),
        in_specs=[hbm] * 6,
        out_specs=(hbm, hbm, vmem),
        scratch_shapes=[
            pltpu.VMEM((TAPS, rows * n_lat), jnp.int32),
            pltpu.VMEM((TAPS, rows * n_lat), jnp.int32),
            pltpu.VMEM((TAPS, BASIS, rows * n_lat), F32),
            pltpu.VMEM((BASIS, channels, channels), BF16),
            pltpu.VMEM((2, 2, rows, half, channels), BF16),
            pltpu.VMEM((own, own), BF16),
            pltpu.VMEM((spots, channels), BF16),
            pltpu.VMEM((spots, channels), BF16),
            pltpu.VMEM((own, channels), BF16),
            pltpu.VMEM((2, own, channels), BF16),
            pltpu.VMEM((BASIS * own, spots), BF16),
            pltpu.VMEM((own, BASIS * spots), BF16),
            pltpu.VMEM((BASIS * own, channels), BF16),
            pltpu.VMEM((BASIS * own, channels), BF16),
            pltpu.VMEM((own, channels), BF16),
            pltpu.VMEM((own, channels), F32),
            pltpu.VMEM((own, channels), BF16),
            pltpu.VMEM((own, channels), BF16),
            pltpu.VMEM((BASIS * spots, channels), BF16),
            pltpu.VMEM((wide // LANES, BASIS * channels, LANES), F32),
            pltpu.VMEM((ring, 2 * share * n_z, wide), BF16),
            pltpu.VMEM((2, n_lat, 2 * share * n_z, wide), BF16),
            pltpu.VMEM((2, n_lat, 2 * share * n_z, wide), BF16),
            pltpu.VMEM((wide // LANES, 2 * share * n_z, LANES), F32),
            pltpu.VMEM((n_z, -(-2 * share // 16) * 16, wide), BF16),
            pltpu.VMEM((n_z, -(-2 * share // 16) * 16, wide), BF16),
            pltpu.VMEM((-(-share // 8) * 8, wide), F32),
            pltpu.VMEM((-(-share // 8) * 8, wide), F32),
            dma((2, 2)),
            dma((2, 2)),
            dma((2,)),
            dma((2,)),
            dma((2, 8)),
            dma((2, 8)),
            dma((2, 2)),
            dma((2, 2)),
            dma((3,)),
            dma((3,)),
            dma((2, n_lat, 2)),
            dma((2, n_lat, 2)),
            dma((n_z,)),
            dma((n_z,)),
            dma((4,)),
        ],
        compiler_params=pltpu.CompilerParams(
            collective_id=0, has_side_effects=True, vmem_limit_bytes=67043328

        ),
        name="section_step",
    )(
        jnp.transpose(lat_step),
        jnp.transpose(lon_step),
        jnp.transpose(basis_values, (1, 2, 0)),
        inputs,
        cotangent,
        weights[0],
    )
    block = (1,) + inputs.shape
    return (
        section_out.reshape(block),
        section_grad.reshape(block),
        weight_grad.reshape(1, -1),
    )


def solution(mesh):
    return jax.shard_map(
        per_device,
        mesh=mesh,
        in_specs=(
            P(None, "lat", "lon", None),
            P(None, "lat", "lon", None),
            P("segment", None, None, None),
            P(),
            P(),
            P(),
        ),
        out_specs=(
            P("segment", None, "lat", "lon", None),
            P("segment", None, "lat", "lon", None),
            P("segment", ("lon", "lat")),
        ),
        check_vma=False,
    )
```

```python
import functools
import math

import jax
import jax.numpy as jnp
from jax import lax
from jax.experimental import pallas as pl
from jax.experimental.pallas import tpu as pltpu
from jax.sharding import PartitionSpec as P

BASIS = 3
TAPS = 9
REACH = 2
LANES = 128
MESH = pl.DeviceIdType.MESH
F32 = jnp.float32
BF16 = jnp.bfloat16


def log2(number):
    power = number.bit_length() - 1
    assert 1 << power == number
    return power


def over(x, number):
    return lax.shift_right_arithmetic(x, jnp.full_like(x, log2(number)))


def rest(x, number):
    return x & (number - 1)


def halo_cell(slot, rows, cols):
    base = 4 * rows
    at = slot
    side_row = over(rest(at, 2 * rows), 2)
    side_col = rest(at, 2) + jnp.where(at < 2 * rows, -2, cols)
    at = slot - base
    far_row = over(rest(at, 2 * cols), cols) + jnp.where(at < 2 * cols, -2, rows)
    far_col = rest(at, cols)
    at = slot - base - 4 * cols
    inside = rest(at, 8)
    corner_row = over(inside, 2) + jnp.where(at < 16, -2, rows)
    corner_col = rest(inside, 2) + jnp.where(rest(over(at, 8), 2) == 0, -2, cols)
    in_side = slot < base
    in_far = slot < base + 4 * cols
    row = jnp.where(in_side, side_row, jnp.where(in_far, far_row, corner_row))
    col = jnp.where(in_side, side_col, jnp.where(in_far, far_col, corner_col))
    used = in_far | (inside < 4)
    return row, col, used


def own_cell(spot, rows, half):
    second = over(spot, rows * half)
    at = rest(spot, rows * half)
    return over(at, half), rest(at, half) + second * half


def spot_of(row, col, rows, cols, half):
    own = rows * cols
    inner = (row >= 0) & (row < rows)
    mid = (col >= 0) & (col < cols)
    side = jnp.where(col < 0, col + 2, col - cols)
    far = jnp.where(row < 0, row + 2, row - rows)
    right = (col >= cols).astype(jnp.int32)
    down = (row >= rows).astype(jnp.int32)
    second = (col >= half).astype(jnp.int32)
    at_own = second * (rows * half) + row * half + col - second * half
    at_side = own + right * (2 * rows) + row * 2 + side
    base = own + 4 * rows
    at_far = base + down * (2 * cols) + far * cols + col
    at_corner = base + 4 * cols + (down * 2 + right) * 8 + far * 2 + side
    return jnp.where(
        inner, jnp.where(mid, at_own, at_side), jnp.where(mid, at_far, at_corner)
    )


def step_kernel(
    sizes,
    lat_hbm,
    lon_hbm,
    basis_hbm,
    in_ref,
    cot_ref,
    w_hbm,
    out_ref,
    grad_ref,
    wg_ref,
    lat_ref,
    lon_ref,
    basis_ref,
    w_all,
    raw,
    pick,
    xp,
    gp,
    grad,
    hb,
    ahead,
    back,
    spread,
    spread_other,
    gate_other,
    slope,
    feat,
    product,
    blk,
    ysend,
    yrecv,
    acc,
    zsend,
    zrecv,
    fsend,
    frecv,
    cin_s,
    cin_r,
    own_s,
    own_r,
    far_s,
    far_r,
    swap_s,
    swap_r,
    halo_s,
    halo_r,
    oc_s,
    oc_r,
    pair_s,
    pair_r,
    y_s,
    y_r,
    z_s,
    z_r,
    w_sem,
):
    n_seg, n_lat, n_z, scale = sizes
    rows, half, channels = in_ref.shape[1:]
    half_cells = rows * half
    cols = 2 * half
    own = rows * cols
    spots = 2 * own
    ring = 2 * n_lat
    steps = ring // 2
    share = BASIS * channels // (n_z * ring * 2)
    wide = channels // 2

    lon = lax.axis_index("lon")
    lat = lax.axis_index("lat")
    seg = lax.axis_index("segment")
    z = lon // 4
    member = (lon // 2) % 2
    core = lon % 2
    pos = z * 2 + core
    y = member * n_lat + lat

    def at(z_to, member_to, core_to, lat_to, seg_to=seg):
        return {"lon": z_to * 4 + member_to * 2 + core_to, "lat": lat_to, "segment": seg_to}

    def beside(shift, lat_to):
        place = lax.rem(pos + shift + 2 * n_z, 2 * n_z)
        return at(place // 2, member, place % 2, lat_to)

    has_up = lat > 0
    has_down = lat < n_lat - 1
    seg_next = lax.rem(seg + 1, n_seg)
    seg_prev = lax.rem(seg + n_seg - 1, n_seg)
    seg_far = lax.rem(seg + 2, n_seg)
    matched = core == member

    base = 4 * rows
    corner = base + 4 * cols
    halo = [
        (0, 2 * rows, 1, 0),
        (2 * rows, 2 * rows, -1, 0),
        (base, 2 * cols, 0, 1),
        (base + 2 * cols, 2 * cols, 0, -1),
        (corner, 8, 1, 1),
        (corner + 8, 8, -1, 1),
        (corner + 16, 8, 1, -1),
        (corner + 24, 8, -1, -1),
    ]

    def sends_to(dlat):
        return has_down if dlat > 0 else has_up

    def gets_from(dlat):
        return has_up if dlat > 0 else has_down

    ring_next = lax.rem(y + 1, ring)
    ring_prev = lax.rem(y + ring - 1, ring)

    def on_ring(place):
        return at(z, place // n_lat, core, lax.rem(place, n_lat))

    partner = at(z, member, 1 - core, lat)

    fetch = pltpu.make_async_copy(w_hbm, w_all.at[seg], w_sem.at[0])
    tables = [
        pltpu.make_async_copy(table_hbm, table_ref, w_sem.at[1 + number])
        for number, (table_hbm, table_ref) in enumerate(
            ((lat_hbm, lat_ref), (lon_hbm, lon_ref), (basis_hbm, basis_ref))
        )
    ]
    for table in tables:
        table.start()
    fetch.start()

    barrier = pltpu.get_barrier_semaphore()

    def greet(device):
        pl.semaphore_signal(barrier, inc=1, device_id=device, device_id_type=MESH)

    for shift in range(1, n_z):
        greet(at(lax.rem(z + shift, n_z), member, core, lat))
    greet(on_ring(ring_next))
    greet(on_ring(ring_prev))
    greet(partner)
    for _, _, shift, dlat in halo:
        if dlat == 0:
            greet(beside(shift, lat))
        else:

            @pl.when(sends_to(dlat))
            def _():
                greet(beside(shift, lat + dlat))

    for other in range(2):

        @pl.when(jnp.logical_not(matched & (member == other)))
        def _():
            greet(at(z, other, member, lat))

        @pl.when(jnp.logical_not(matched & (core == other)))
        def _():
            greet(at(z, core, other, lat))

    greet(at(z, member, core, lat, seg_next))
    greet(at(z, member, core, lat, seg_prev))

    met = (n_z - 1) + 3 + 2 + 4 + 2
    met = met + jnp.where(has_up, 3, 0) + jnp.where(has_down, 3, 0)
    met = met - jnp.where(matched, 2, 0)
    pl.semaphore_wait(barrier, met)

    def remote(src, dst, send_sem, recv_sem, device):
        return pltpu.make_async_remote_copy(
            src_ref=src,
            dst_ref=dst,
            send_sem=send_sem,
            recv_sem=recv_sem,
            device_id=device,
            device_id_type=MESH,
        )

    def slot_of(buffer, part):
        return buffer.at[part]

    def regroup(source, buffer, which):
        for to in range(2):
            there = matched & (member == to)

            @pl.when(there)
            def _():
                pltpu.make_async_copy(
                    source.at[to], slot_of(buffer, core), cin_r.at[which, core]
                ).start()

            @pl.when(jnp.logical_not(there))
            def _():
                remote(
                    source.at[to],
                    slot_of(buffer, core),
                    cin_s.at[which, to],
                    cin_r.at[which, core],
                    at(z, to, member, lat),
                ).start()

    def regroup_arrived(source, buffer, which):
        for part in range(2):
            here = matched & (core == part)

            @pl.when(here)
            def _():
                pltpu.make_async_copy(
                    source.at[0], slot_of(buffer, part), cin_r.at[which, part]
                ).wait()

            @pl.when(jnp.logical_not(here))
            def _():
                remote(
                    source.at[0],
                    slot_of(buffer, part),
                    cin_s.at[which, 0],
                    cin_r.at[which, part],
                    partner,
                ).wait_recv()

    def regroup_sent(source, buffer, which):
        for to in range(2):

            @pl.when(jnp.logical_not(matched & (member == to)))
            def _():
                remote(
                    source.at[to],
                    slot_of(buffer, core),
                    cin_s.at[which, to],
                    cin_r.at[which, core],
                    partner,
                ).wait_send()

    regroup(in_ref, raw.at[0], 0)

    n_pieces = 2 * BASIS
    part_rows = channels // 4
    orders = (tuple(range(n_pieces)), tuple((k + BASIS) % n_pieces for k in range(n_pieces)))

    def piece(weights, k, of_core):
        start = pl.multiple_of(of_core * (channels // 2) + (k % 2) * part_rows, part_rows)
        return weights.at[k // 2, pl.ds(start, part_rows), :]

    def own_copy(way, k):
        return remote(
            piece(w_hbm, k, core),
            piece(w_all.at[seg], k, core),
            own_s.at[way, k],
            own_r.at[way, k],
            at(z, member, core, lat, seg_prev if way else seg_next),
        )

    def own_landed(way, k):
        section = seg_next if way else seg_prev
        landing = piece(w_all.at[section], k, core)
        remote(landing, landing, own_s.at[way, k], own_r.at[way, k], partner).wait_recv()

    def far_copy(way, k):
        moved = piece(w_all.at[seg_next if way else seg_prev], k, core)
        return remote(
            moved,
            moved,
            far_s.at[k],
            far_r.at[k],
            at(z, member, core, lat, seg_prev if way else seg_next),
        )

    def far_landed(k):
        landing = piece(w_all.at[seg_far], k, core)
        remote(landing, landing, far_s.at[k], far_r.at[k], partner).wait_recv()

    def swap_copy(which, k):
        moved = piece(w_all.at[(seg_prev, seg_next, seg_far)[which]], k, core)
        return remote(moved, moved, swap_s.at[which, k], swap_r.at[which, k], partner)

    def swap_landed(which, k):
        landing = piece(w_all.at[(seg_prev, seg_next, seg_far)[which]], k, 1 - core)
        remote(landing, landing, swap_s.at[which, k], swap_r.at[which, k], partner).wait_recv()

    for step in range(n_pieces):
        for way in range(2):
            own_copy(way, orders[way][step]).start()

    def pump_near():
        for step in range(n_pieces):
            for way in range(2):
                k = orders[way][step]
                own_landed(way, k)
                swap_copy(way, k).start()
                if step < BASIS:
                    far_copy(way, k).start()
        for step in range(n_pieces):
            for way in range(2):
                swap_landed(way, orders[way][step])

    def pump_far():
        for step in range(BASIS):
            for way in range(2):
                k = orders[way][step]
                far_landed(k)
                swap_copy(2, k).start()
        for k in range(n_pieces):
            swap_landed(2, k)

    for buffer in [xp.at[s] for s in range(n_seg)] + [gp.at[s] for s in range(n_seg)]:

        @pl.when(jnp.logical_not(has_up))
        def _():
            buffer[pl.ds(own + base, 2 * cols), :] = jnp.zeros((2 * cols, channels), BF16)
            buffer[pl.ds(own + corner, 16), :] = jnp.zeros((16, channels), BF16)

        @pl.when(jnp.logical_not(has_down))
        def _():
            buffer[pl.ds(own + base + 2 * cols, 2 * cols), :] = jnp.zeros((2 * cols, channels), BF16)
            buffer[pl.ds(own + corner + 16, 16), :] = jnp.zeros((16, channels), BF16)

    spot = lax.broadcasted_iota(jnp.int32, (16, spots), 1)
    inner_row, inner_col = own_cell(spot, rows, half)
    outer_row, outer_col, used = halo_cell(spot - own, rows, cols)
    spot_row = jnp.where(spot < own, inner_row, outer_row)
    spot_col = jnp.where(spot < own, inner_col, outer_col)
    used = (spot < own) | used
    grid_row = jnp.where(used, spot_row + lat * rows, -1)[:1]
    total_rows = n_lat * rows
    chosen = (
        lax.broadcasted_iota(jnp.int32, (total_rows, spots), 0)
        == jnp.broadcast_to(grid_row, (total_rows, spots))
    ).astype(F32).astype(BF16)

    for table in tables:
        table.wait()

    def of_spot(taps):
        return jnp.dot(taps.astype(F32).astype(BF16), chosen, preferred_element_type=F32)

    to_row = of_spot(lat_ref[...]).astype(jnp.int32) + spot_row[:TAPS]
    to_col = of_spot(lon_ref[...]).astype(jnp.int32) + spot_col[:TAPS]
    worth = [of_spot(basis_ref[:, b, :]) for b in range(BASIS)]

    lands = (to_row >= 0) & (to_row < rows) & (to_col >= 0) & (to_col < cols)
    second = (to_col >= half).astype(jnp.int32)
    target = jnp.where(
        lands, second * (rows * half) + to_row * half + to_col - second * half, -1
    )
    level = lax.broadcasted_iota(jnp.int32, (own, spots), 0)
    totals = [jnp.zeros((own, spots), F32) for _ in range(BASIS)]
    for tap in range(TAPS):
        hit = level == target[tap : tap + 1, :]
        for b in range(BASIS):
            totals[b] = totals[b] + jnp.where(hit, worth[b][tap : tap + 1, :], 0.0)
    for b in range(BASIS):
        back[:, pl.ds(b * spots, spots)] = totals[b].astype(BF16)

    tap_row, tap_col = to_row[:, :own], to_col[:, :own]
    in_grid = (tap_row + lat * rows >= 0) & (tap_row + lat * rows < total_rows)
    source = jnp.where(in_grid, spot_of(tap_row, tap_col, rows, cols, half), -1)
    level = lax.broadcasted_iota(jnp.int32, (spots, own), 0)
    totals = [jnp.zeros((spots, own), F32) for _ in range(BASIS)]
    for tap in range(TAPS):
        hit = level == source[tap : tap + 1, :]
        for b in range(BASIS):
            totals[b] = totals[b] + jnp.where(hit, worth[b][tap : tap + 1, :own], 0.0)
    for b in range(BASIS):
        ahead[pl.ds(b * own, own), :] = jnp.transpose(totals[b]).astype(BF16)

    slot = lax.broadcasted_iota(jnp.int32, (own, own), 0)
    pick_row, pick_col, used = halo_cell(slot, rows, cols)
    pick_row, pick_col = rest(pick_row, rows), rest(pick_col, cols)
    wanted = over(pick_col, half) * (rows * half) + pick_row * half + rest(pick_col, half)
    wanted = jnp.where(used, wanted, -1)
    pick[...] = (
        (lax.broadcasted_iota(jnp.int32, (own, own), 1) == wanted).astype(F32).astype(BF16)
    )

    def halo_copy(buffer, phase, number):
        start, size, shift, dlat = halo[number]
        return remote(
            hb.at[phase, pl.ds(start, size), :],
            buffer.at[pl.ds(own + start, size), :],
            halo_s.at[phase, number],
            halo_r.at[phase, number],
            beside(shift, lat + dlat),
        )

    def halo_start(block, buffer, phase):
        hb[phase] = jnp.dot(pick[...], block, preferred_element_type=F32).astype(BF16)
        for number in (4, 5, 6, 7, 2, 3, 0, 1):
            dlat = halo[number][3]
            if dlat == 0:
                halo_copy(buffer, phase, number).start()
            else:

                @pl.when(sends_to(dlat))
                def _():
                    halo_copy(buffer, phase, number).start()

    def halo_arrived(buffer, phase):
        for number in range(8):
            dlat = halo[number][3]
            if dlat == 0:
                halo_copy(buffer, phase, number).wait_recv()
            else:

                @pl.when(gets_from(dlat))
                def _():
                    halo_copy(buffer, phase, number).wait_recv()

    def halo_sent(buffer, phase):
        for number in range(8):
            dlat = halo[number][3]
            if dlat == 0:
                halo_copy(buffer, phase, number).wait_send()
            else:

                @pl.when(sends_to(dlat))
                def _():
                    halo_copy(buffer, phase, number).wait_send()

    def restore_copy(block, output, which, part, arrives_from):
        return remote(
            block.at[pl.ds(part * half_cells, half_cells), :],
            output.at[arrives_from],
            oc_s.at[which, part],
            oc_r.at[which, arrives_from],
            at(z, core, part, lat),
        )

    def restore_start(block, output, which):
        for part in range(2):
            there = matched & (core == part)

            @pl.when(there)
            def _():
                pltpu.make_async_copy(
                    block.at[pl.ds(part * half_cells, half_cells), :],
                    output.at[member],
                    oc_r.at[which, member],
                ).start()

            @pl.when(jnp.logical_not(there))
            def _():
                restore_copy(block, output, which, part, member).start()

    def restore_finish(block, output, which):
        for part in range(2):

            @pl.when(jnp.logical_not(matched & (core == part)))
            def _():
                restore_copy(block, output, which, part, member).wait_send()

        for origin in range(2):
            here = matched & (member == origin)

            @pl.when(here)
            def _():
                pltpu.make_async_copy(
                    block.at[pl.ds(0, half_cells), :],
                    output.at[origin],
                    oc_r.at[which, origin],
                ).wait()

            @pl.when(jnp.logical_not(here))
            def _():
                restore_copy(block, output, which, 0, origin).wait_recv()

    pair_spread = remote(spread.at[seg], spread_other, pair_s.at[0], pair_r.at[0], partner)

    def forward(section):
        halo_arrived(xp.at[section], section)
        widened = xp[section]
        mixed = None
        for b in range(BASIS):
            picked = jnp.dot(
                ahead[pl.ds(b * own, own), :], widened, preferred_element_type=F32
            ).astype(BF16)
            spread[section, pl.ds(b * own, own), :] = picked
            term = jnp.dot(picked, w_all[section, b], preferred_element_type=F32)
            mixed = term if mixed is None else mixed + term
        sigma = 1.0 / (1.0 + jnp.exp(-mixed))
        result = (xp[section, pl.ds(0, own), :].astype(F32) + mixed * sigma).astype(BF16)
        xp[section + 1, pl.ds(0, own), :] = result
        if section + 1 < n_seg:
            halo_start(result, xp.at[section + 1], section + 1)
        slope[section] = sigma * (1.0 + mixed * (1.0 - sigma))

        @pl.when(seg == section)
        def _():
            restore_start(xp.at[section + 1], out_ref, 0)
            pair_spread.start()

    regroup_arrived(in_ref, raw.at[0], 0)
    xp[0, pl.ds(0, own), :] = raw[0].reshape(own, channels)
    halo_start(xp[0, pl.ds(0, own), :], xp.at[0], 0)
    regroup(cot_ref, raw.at[1], 1)
    fetch.wait()

    @pl.when(seg == 0)
    def _():
        forward(0)

    pump_near()
    pl.when(seg_far == 0)(pump_far)

    @pl.when(seg != 0)
    def _():
        forward(0)

    for section in range(1, n_seg):
        pl.when(seg_far == section)(pump_far)
        forward(section)

    regroup_arrived(cot_ref, raw.at[1], 1)
    grad[...] = raw[1].reshape(own, channels)

    def open_gate(section):
        gate = (grad[...].astype(F32) * slope[section]).astype(BF16)
        gp[section, pl.ds(0, own), :] = gate
        halo_start(gate, gp.at[section], n_seg + section)

    def pull(section):
        halo_arrived(gp.at[section], n_seg + section)
        for b in range(BASIS):
            feat[pl.ds(b * spots, spots), :] = lax.dot_general(
                gp[section], w_all[section, b], (((1,), (1,)), ((), ())), preferred_element_type=F32
            ).astype(BF16)
        pulled = jnp.dot(back[...], feat[...], preferred_element_type=F32)
        grad[...] = (grad[...].astype(F32) + pulled).astype(BF16)

    for section in range(n_seg - 1, 0, -1):

        @pl.when(seg < section)
        def _():
            open_gate(section)
            pull(section)

    open_gate(seg)
    pair_gate = remote(
        gp.at[seg, pl.ds(0, own), :], gate_other, pair_s.at[1], pair_r.at[1], partner
    )
    pair_gate.start()
    pair_spread.wait_recv()
    pair_gate.wait_recv()

    columns = pl.ds(pl.multiple_of(core * wide, wide), wide)
    gate_both = jnp.concatenate(
        [gp[seg, pl.ds(0, own), columns], gate_other[:, columns]], axis=0
    )
    for b in range(BASIS):
        both = jnp.concatenate(
            [spread[seg, pl.ds(b * own, own), :], spread_other[pl.ds(b * own, own), :]], axis=0
        )
        term = scale * lax.dot_general(
            both, gate_both, (((0,), (0,)), ((), ())), preferred_element_type=F32
        )
        for part in range(wide // LANES):
            product[part, pl.ds(b * channels, channels), :] = term[
                :, part * LANES : (part + 1) * LANES
            ]

    group = share * n_z

    def ring_copy(way, step, e):
        return remote(
            ysend.at[way, step, pl.ds(e * group, group), :],
            yrecv.at[way, step, pl.ds(e * group, group), :],
            y_s.at[way, step, e],
            y_r.at[way, step, e],
            on_ring(ring_next if way == 0 else ring_prev),
        )

    def ring_step(step, way, e):
        distance = steps - step
        place = lax.rem(y + (distance if way == 0 else ring - distance), ring)
        part = pl.ds(e * group, group)
        term = blk[place, part, :]
        if step > 1 or (step == 1 and e == way):
            ring_copy(way, step - 1, e).wait_recv()
            term = (term.astype(F32) + yrecv[way, step - 1, part, :].astype(F32)).astype(BF16)
        ysend[way, step, part, :] = term
        ring_copy(way, step, e).start()

    def ring_begin():
        for place in range(ring):
            for e in range(2):
                for i in range(share):
                    first = ((place // n_lat) * 2 + e) * n_lat * share + (place % n_lat) * share + i
                    for part in range(wide // LANES):
                        blk[
                            place, pl.ds(e * group + i * n_z, n_z), pl.ds(part * LANES, LANES)
                        ] = product[part, pl.ds(first, n_z, stride=ring * 2 * share), :].astype(BF16)
        for way in range(2):
            ring_step(0, way, way)
        for way in range(2):
            ring_step(1, way, 1 - way)

    ring_begin()
    pull(seg)
    restore_start(grad, grad_ref, 1)

    for way in range(2):
        ring_step(1, way, way)
    for step in range(2, steps):
        for half_turn in range(2):
            for way in range(2):
                ring_step(step, way, way if half_turn else 1 - way)
    summed = blk[y].astype(F32)
    for way in range(2):
        for e in range(2):
            ring_copy(way, steps - 1, e).wait_recv()
        summed = summed + yrecv[way, steps - 1].astype(F32)
    for part in range(wide // LANES):
        acc[part] = summed[:, part * LANES : (part + 1) * LANES]

    def z_copy(shift):
        to = lax.rem(z + shift, n_z)
        return remote(
            zsend.at[to], zrecv.at[z], z_s.at[shift], z_r.at[shift], at(to, member, core, lat)
        )

    for to in range(n_z):
        for part in range(wide // LANES):
            zsend[to, pl.ds(0, 2 * share), pl.ds(part * LANES, LANES)] = acc[
                part, pl.ds(to, 2 * share, stride=n_z), :
            ].astype(BF16)
    for shift in range(1, n_z):
        z_copy(shift).start()
    total = zsend[z][: 2 * share].astype(F32)
    for shift in range(1, n_z):
        from_z = lax.rem(z + n_z - shift, n_z)
        remote(
            zsend.at[0], zrecv.at[from_z], z_s.at[shift], z_r.at[shift], partner
        ).wait_recv()
        total = total + zrecv[from_z][: 2 * share].astype(F32)
    mine = jnp.where(core == 0, total[:share], total[share:])
    fsend[pl.ds(0, share), :] = jnp.where(core == 0, total[share:], total[:share])
    last = remote(fsend, frecv, pair_s.at[2], pair_r.at[2], partner)
    last.start()
    last.wait_recv()
    theirs = frecv[pl.ds(0, share), :]
    wg_ref[:, :wide] = jnp.where(core == 0, mine, theirs)
    wg_ref[:, wide:] = jnp.where(core == 0, theirs, mine)

    restore_finish(xp.at[seg + 1], out_ref, 0)
    restore_finish(grad, grad_ref, 1)
    regroup_sent(in_ref, raw.at[0], 0)
    regroup_sent(cot_ref, raw.at[1], 1)
    for k in range(n_pieces):
        for way in range(2):
            own_copy(way, k).wait_send()
        far_copy(k // BASIS, k).wait_send()
        for which in range(3):
            swap_copy(which, k).wait_send()
    for section in range(n_seg):
        halo_sent(xp.at[section], section)

        @pl.when(seg <= section)
        def _():
            halo_sent(gp.at[section], n_seg + section)

    pair_spread.wait_send()
    pair_gate.wait_send()
    last.wait_send()
    for step in range(steps):
        for way in range(2):
            for e in range(2):
                if step or e == way:
                    ring_copy(way, step, e).wait_send()
    for shift in range(1, n_z):
        z_copy(shift).wait_send()


def per_device(inputs, cotangent, weights, basis_values, lat_step, lon_step):
    members, rows, half, channels = inputs.shape
    n_lon, n_lat, n_seg = (lax.axis_size(name) for name in ("lon", "lat", "segment"))
    n_z = n_lon // 4
    cols = 2 * half
    own = rows * cols
    spots = 2 * own
    ring = 2 * n_lat
    share = BASIS * channels // (n_lon * n_lat)
    wide = channels // 2
    scale = 1.0 / math.sqrt(members * rows * n_lat * half * n_lon)

    vmem = pl.BlockSpec(memory_space=pltpu.VMEM)
    hbm = pl.BlockSpec(memory_space=pltpu.HBM)
    dma = pltpu.SemaphoreType.DMA
    section_out, section_grad, weight_grad = pl.pallas_call(
        functools.partial(step_kernel, (n_seg, n_lat, n_z, scale)),
        out_shape=(
            jax.ShapeDtypeStruct((2, rows * half, channels), BF16),
            jax.ShapeDtypeStruct((2, rows * half, channels), BF16),
            jax.ShapeDtypeStruct((share, channels), F32),
        ),
        in_specs=[hbm] * 6,
        out_specs=(vmem, vmem, vmem),
        scratch_shapes=[
            pltpu.VMEM((TAPS, rows * n_lat), jnp.int32),
            pltpu.VMEM((TAPS, rows * n_lat), jnp.int32),
            pltpu.VMEM((TAPS, BASIS, rows * n_lat), F32),
            pltpu.VMEM((n_seg, BASIS, channels, channels), BF16),
            pltpu.VMEM((2, 2, rows, half, channels), BF16),
            pltpu.VMEM((own, own), BF16),
            pltpu.VMEM((n_seg + 1, spots, channels), BF16),
            pltpu.VMEM((n_seg, spots, channels), BF16),
            pltpu.VMEM((own, channels), BF16),
            pltpu.VMEM((2 * n_seg, own, channels), BF16),
            pltpu.VMEM((BASIS * own, spots), BF16),
            pltpu.VMEM((own, BASIS * spots), BF16),
            pltpu.VMEM((n_seg, BASIS * own, channels), BF16),
            pltpu.VMEM((BASIS * own, channels), BF16),
            pltpu.VMEM((own, channels), BF16),
            pltpu.VMEM((n_seg, own, channels), F32),
            pltpu.VMEM((BASIS * spots, channels), BF16),
            pltpu.VMEM((wide // LANES, BASIS * channels, LANES), F32),
            pltpu.VMEM((ring, 2 * share * n_z, wide), BF16),
            pltpu.VMEM((2, n_lat, 2 * share * n_z, wide), BF16),
            pltpu.VMEM((2, n_lat, 2 * share * n_z, wide), BF16),
            pltpu.VMEM((wide // LANES, 2 * share * n_z, LANES), F32),
            pltpu.VMEM((n_z, -(-2 * share // 16) * 16, wide), BF16),
            pltpu.VMEM((n_z, -(-2 * share // 16) * 16, wide), BF16),
            pltpu.VMEM((-(-share // 8) * 8, wide), F32),
            pltpu.VMEM((-(-share // 8) * 8, wide), F32),
            dma((2, 2)),
            dma((2, 2)),
            dma((2, 2 * BASIS)),
            dma((2, 2 * BASIS)),
            dma((2 * BASIS,)),
            dma((2 * BASIS,)),
            dma((3, 2 * BASIS)),
            dma((3, 2 * BASIS)),
            dma((2 * n_seg, 8)),
            dma((2 * n_seg, 8)),
            dma((2, 2)),
            dma((2, 2)),
            dma((3,)),
            dma((3,)),
            dma((2, n_lat, 2)),
            dma((2, n_lat, 2)),
            dma((n_z,)),
            dma((n_z,)),
            dma((4,)),
        ],
        compiler_params=pltpu.CompilerParams(
            collective_id=0, has_side_effects=True, vmem_limit_bytes=50331648
        ),
        name="section_step",
    )(
        *(
            pltpu.with_memory_space_constraint(array, pltpu.HBM)
            for array in (
                jnp.transpose(lat_step),
                jnp.transpose(lon_step),
                jnp.transpose(basis_values, (1, 2, 0)),
                inputs,
                cotangent,
                weights[0],
            )
        )
    )
    block = (1,) + inputs.shape
    return (
        section_out.reshape(block),
        section_grad.reshape(block),
        weight_grad.reshape(1, -1),
    )


def solution(mesh):
    return jax.shard_map(
        per_device,
        mesh=mesh,
        in_specs=(
            P(None, "lat", "lon", None),
            P(None, "lat", "lon", None),
            P("segment", None, None, None),
            P(),
            P(),
            P(),
        ),
        out_specs=(
            P("segment", None, "lat", "lon", None),
            P("segment", None, "lat", "lon", None),
            P("segment", ("lon", "lat")),
        ),
        check_vma=False,
    )
```

```python
import functools
import math

import jax
import jax.numpy as jnp
from jax import lax
from jax.experimental import pallas as pl
from jax.experimental.pallas import tpu as pltpu
from jax.sharding import PartitionSpec as P

BASIS = 3
TAPS = 9
REACH = 2
LANES = 128
MESH = pl.DeviceIdType.MESH
F32 = jnp.float32
BF16 = jnp.bfloat16


def log2(number):
    power = number.bit_length() - 1
    assert 1 << power == number
    return power


def over(x, number):
    return lax.shift_right_arithmetic(x, jnp.full_like(x, log2(number)))


def rest(x, number):
    return x & (number - 1)


def halo_cell(slot, rows, cols):
    base = 4 * rows
    at = slot
    side_row = over(rest(at, 2 * rows), 2)
    side_col = rest(at, 2) + jnp.where(at < 2 * rows, -2, cols)
    at = slot - base
    far_row = over(rest(at, 2 * cols), cols) + jnp.where(at < 2 * cols, -2, rows)
    far_col = rest(at, cols)
    at = slot - base - 4 * cols
    inside = rest(at, 8)
    corner_row = over(inside, 2) + jnp.where(at < 16, -2, rows)
    corner_col = rest(inside, 2) + jnp.where(rest(over(at, 8), 2) == 0, -2, cols)
    in_side = slot < base
    in_far = slot < base + 4 * cols
    row = jnp.where(in_side, side_row, jnp.where(in_far, far_row, corner_row))
    col = jnp.where(in_side, side_col, jnp.where(in_far, far_col, corner_col))
    used = in_far | (inside < 4)
    return row, col, used


def own_cell(spot, rows, half):
    second = over(spot, rows * half)
    at = rest(spot, rows * half)
    return over(at, half), rest(at, half) + second * half


def spot_of(row, col, rows, cols, half):
    own = rows * cols
    inner = (row >= 0) & (row < rows)
    mid = (col >= 0) & (col < cols)
    side = jnp.where(col < 0, col + 2, col - cols)
    far = jnp.where(row < 0, row + 2, row - rows)
    right = (col >= cols).astype(jnp.int32)
    down = (row >= rows).astype(jnp.int32)
    second = (col >= half).astype(jnp.int32)
    at_own = second * (rows * half) + row * half + col - second * half
    at_side = own + right * (2 * rows) + row * 2 + side
    base = own + 4 * rows
    at_far = base + down * (2 * cols) + far * cols + col
    at_corner = base + 4 * cols + (down * 2 + right) * 8 + far * 2 + side
    return jnp.where(
        inner, jnp.where(mid, at_own, at_side), jnp.where(mid, at_far, at_corner)
    )


def step_kernel(
    sizes,
    lat_hbm,
    lon_hbm,
    basis_hbm,
    in_ref,
    cot_ref,
    w_hbm,
    out_ref,
    grad_ref,
    wg_ref,
    lat_ref,
    lon_ref,
    basis_ref,
    w_all,
    raw,
    pick,
    xp,
    gp,
    grad,
    hb,
    ahead,
    back,
    spread,
    spread_other,
    gate_other,
    slope,
    feat,
    product,
    blk,
    ysend,
    yrecv,
    acc,
    zsend,
    zrecv,
    fsend,
    frecv,
    cin_s,
    cin_r,
    own_s,
    own_r,
    far_s,
    far_r,
    side_s,
    side_r,
    swap_s,
    swap_r,
    halo_s,
    halo_r,
    oc_s,
    oc_r,
    pair_s,
    pair_r,
    y_s,
    y_r,
    z_s,
    z_r,
    w_sem,
):
    n_seg, n_lat, n_z, scale = sizes
    rows, half, channels = in_ref.shape[1:]
    half_cells = rows * half
    cols = 2 * half
    own = rows * cols
    spots = 2 * own
    ring = 2 * n_lat
    steps = ring // 2
    share = BASIS * channels // (n_z * ring * 2)
    wide = channels // 2

    lon = lax.axis_index("lon")
    lat = lax.axis_index("lat")
    seg = lax.axis_index("segment")
    z = lon // 4
    member = (lon // 2) % 2
    core = lon % 2
    pos = z * 2 + core
    y = member * n_lat + lat

    def at(z_to, member_to, core_to, lat_to, seg_to=seg):
        return {"lon": z_to * 4 + member_to * 2 + core_to, "lat": lat_to, "segment": seg_to}

    def beside(shift, lat_to):
        place = lax.rem(pos + shift + 2 * n_z, 2 * n_z)
        return at(place // 2, member, place % 2, lat_to)

    has_up = lat > 0
    has_down = lat < n_lat - 1
    seg_next = lax.rem(seg + 1, n_seg)
    seg_prev = lax.rem(seg + n_seg - 1, n_seg)
    seg_far = lax.rem(seg + 2, n_seg)
    matched = core == member

    base = 4 * rows
    corner = base + 4 * cols
    halo = [
        (0, 2 * rows, 1, 0),
        (2 * rows, 2 * rows, -1, 0),
        (base, 2 * cols, 0, 1),
        (base + 2 * cols, 2 * cols, 0, -1),
        (corner, 8, 1, 1),
        (corner + 8, 8, -1, 1),
        (corner + 16, 8, 1, -1),
        (corner + 24, 8, -1, -1),
    ]

    def sends_to(dlat):
        return has_down if dlat > 0 else has_up

    def gets_from(dlat):
        return has_up if dlat > 0 else has_down

    ring_next = lax.rem(y + 1, ring)
    ring_prev = lax.rem(y + ring - 1, ring)

    def on_ring(place):
        return at(z, place // n_lat, core, lax.rem(place, n_lat))

    partner = at(z, member, 1 - core, lat)

    fetch = pltpu.make_async_copy(w_hbm, w_all.at[seg], w_sem.at[0])
    tables = [
        pltpu.make_async_copy(table_hbm, table_ref, w_sem.at[1 + number])
        for number, (table_hbm, table_ref) in enumerate(
            ((lat_hbm, lat_ref), (lon_hbm, lon_ref), (basis_hbm, basis_ref))
        )
    ]
    for table in tables:
        table.start()
    fetch.start()

    barrier = pltpu.get_barrier_semaphore()

    def greet(device):
        pl.semaphore_signal(barrier, inc=1, device_id=device, device_id_type=MESH)

    for shift in range(1, n_z):
        greet(at(lax.rem(z + shift, n_z), member, core, lat))
    greet(on_ring(ring_next))
    greet(on_ring(ring_prev))
    greet(partner)
    for _, _, shift, dlat in halo:
        if dlat == 0:
            greet(beside(shift, lat))
        else:

            @pl.when(sends_to(dlat))
            def _():
                greet(beside(shift, lat + dlat))

    for other in range(2):

        @pl.when(jnp.logical_not(matched & (member == other)))
        def _():
            greet(at(z, other, member, lat))

        @pl.when(jnp.logical_not(matched & (core == other)))
        def _():
            greet(at(z, core, other, lat))

    greet(at(z, member, core, lat, seg_next))
    greet(at(z, member, core, lat, seg_prev))

    met = (n_z - 1) + 3 + 2 + 4 + 2
    met = met + jnp.where(has_up, 3, 0) + jnp.where(has_down, 3, 0)
    met = met - jnp.where(matched, 2, 0)
    pl.semaphore_wait(barrier, met)

    def remote(src, dst, send_sem, recv_sem, device):
        return pltpu.make_async_remote_copy(
            src_ref=src,
            dst_ref=dst,
            send_sem=send_sem,
            recv_sem=recv_sem,
            device_id=device,
            device_id_type=MESH,
        )

    def slot_of(buffer, part):
        return buffer.at[part]

    def regroup(source, buffer, which):
        for to in range(2):
            there = matched & (member == to)

            @pl.when(there)
            def _():
                pltpu.make_async_copy(
                    source.at[to], slot_of(buffer, core), cin_r.at[which, core]
                ).start()

            @pl.when(jnp.logical_not(there))
            def _():
                remote(
                    source.at[to],
                    slot_of(buffer, core),
                    cin_s.at[which, to],
                    cin_r.at[which, core],
                    at(z, to, member, lat),
                ).start()

    def regroup_arrived(source, buffer, which):
        for part in range(2):
            here = matched & (core == part)

            @pl.when(here)
            def _():
                pltpu.make_async_copy(
                    source.at[0], slot_of(buffer, part), cin_r.at[which, part]
                ).wait()

            @pl.when(jnp.logical_not(here))
            def _():
                remote(
                    source.at[0],
                    slot_of(buffer, part),
                    cin_s.at[which, 0],
                    cin_r.at[which, part],
                    partner,
                ).wait_recv()

    def regroup_sent(source, buffer, which):
        for to in range(2):

            @pl.when(jnp.logical_not(matched & (member == to)))
            def _():
                remote(
                    source.at[to],
                    slot_of(buffer, core),
                    cin_s.at[which, to],
                    cin_r.at[which, core],
                    partner,
                ).wait_send()

    regroup(in_ref, raw.at[0], 0)

    n_pieces = 2 * BASIS
    part_rows = channels // 8
    orders = (tuple(range(n_pieces)), tuple((k + BASIS) % n_pieces for k in range(n_pieces)))
    sections = (seg_prev, seg_next, seg_far)
    parity = lax.rem(z, 2)
    z_next = at(lax.rem(z + 1, n_z), member, core, lat)
    z_prev = at(lax.rem(z + n_z - 1, n_z), member, core, lat)

    def piece(weights, k, of_parity, of_core):
        start = (2 * of_parity + of_core) * (channels // 4) + (k % 2) * part_rows
        return weights.at[k // 2, pl.ds(pl.multiple_of(start, part_rows), part_rows), :]

    def own_copy(way, k):
        return remote(
            piece(w_hbm, k, parity, core),
            piece(w_all.at[seg], k, parity, core),
            own_s.at[way, k],
            own_r.at[way, k],
            at(z, member, core, lat, seg_prev if way else seg_next),
        )

    def own_landed(way, k):
        landing = piece(w_all.at[sections[way]], k, parity, core)
        remote(landing, landing, own_s.at[way, k], own_r.at[way, k], partner).wait_recv()

    def far_copy(way, k):
        moved = piece(w_all.at[sections[way]], k, parity, core)
        return remote(
            moved,
            moved,
            far_s.at[k],
            far_r.at[k],
            at(z, member, core, lat, seg_prev if way else seg_next),
        )

    def far_landed(k):
        landing = piece(w_all.at[seg_far], k, parity, core)
        remote(landing, landing, far_s.at[k], far_r.at[k], partner).wait_recv()

    def side_copy(which, k):
        moved = piece(w_all.at[sections[which]], k, parity, core)
        return remote(
            moved, moved, side_s.at[which, k], side_r.at[which, k], z_prev if k % 2 else z_next
        )

    def side_landed(which, k):
        landing = piece(w_all.at[sections[which]], k, 1 - parity, core)
        remote(landing, landing, side_s.at[which, k], side_r.at[which, k], partner).wait_recv()

    def swap_copy(which, k, other):
        moved = piece(w_all.at[sections[which]], k, 1 - parity if other else parity, core)
        return remote(
            moved, moved, swap_s.at[which, k, other], swap_r.at[which, k, other], partner
        )

    def swap_landed(which, k, other):
        landing = piece(w_all.at[sections[which]], k, 1 - parity if other else parity, 1 - core)
        remote(
            landing, landing, swap_s.at[which, k, other], swap_r.at[which, k, other], partner
        ).wait_recv()

    for step in range(n_pieces):
        for way in range(2):
            own_copy(way, orders[way][step]).start()

    def pump_near(first, last):
        for step in range(first, last):
            for way in range(2):
                k = orders[way][step]
                own_landed(way, k)
                side_copy(way, k).start()
                if step < BASIS:
                    far_copy(way, k).start()
                swap_copy(way, k, 0).start()

    def finish_near():
        for step in range(n_pieces):
            for way in range(2):
                k = orders[way][step]
                side_landed(way, k)
                swap_copy(way, k, 1).start()

    def pump_far():
        for step in range(BASIS):
            for way in range(2):
                k = orders[way][step]
                far_landed(k)
                side_copy(2, k).start()
                swap_copy(2, k, 0).start()

    def near_landed():
        for step in range(n_pieces):
            for way in range(2):
                for other in range(2):
                    swap_landed(way, orders[way][step], other)

    def finish_far():
        for k in range(n_pieces):
            side_landed(2, k)
            swap_copy(2, k, 1).start()
        for k in range(n_pieces):
            for other in range(2):
                swap_landed(2, k, other)

    for buffer in [xp.at[s] for s in range(n_seg)] + [gp.at[s] for s in range(n_seg)]:

        @pl.when(jnp.logical_not(has_up))
        def _():
            buffer[pl.ds(own + base, 2 * cols), :] = jnp.zeros((2 * cols, channels), BF16)
            buffer[pl.ds(own + corner, 16), :] = jnp.zeros((16, channels), BF16)

        @pl.when(jnp.logical_not(has_down))
        def _():
            buffer[pl.ds(own + base + 2 * cols, 2 * cols), :] = jnp.zeros((2 * cols, channels), BF16)
            buffer[pl.ds(own + corner + 16, 16), :] = jnp.zeros((16, channels), BF16)

    spot = lax.broadcasted_iota(jnp.int32, (16, spots), 1)
    inner_row, inner_col = own_cell(spot, rows, half)
    outer_row, outer_col, used = halo_cell(spot - own, rows, cols)
    spot_row = jnp.where(spot < own, inner_row, outer_row)
    spot_col = jnp.where(spot < own, inner_col, outer_col)
    used = (spot < own) | used
    grid_row = jnp.where(used, spot_row + lat * rows, -1)[:1]
    total_rows = n_lat * rows
    chosen = (
        lax.broadcasted_iota(jnp.int32, (total_rows, spots), 0)
        == jnp.broadcast_to(grid_row, (total_rows, spots))
    ).astype(F32).astype(BF16)

    for table in tables:
        table.wait()

    def of_spot(taps):
        return jnp.dot(taps.astype(F32).astype(BF16), chosen, preferred_element_type=F32)

    to_row = of_spot(lat_ref[...]).astype(jnp.int32) + spot_row[:TAPS]
    to_col = of_spot(lon_ref[...]).astype(jnp.int32) + spot_col[:TAPS]
    worth = [of_spot(basis_ref[:, b, :]) for b in range(BASIS)]

    lands = (to_row >= 0) & (to_row < rows) & (to_col >= 0) & (to_col < cols)
    second = (to_col >= half).astype(jnp.int32)
    target = jnp.where(
        lands, second * (rows * half) + to_row * half + to_col - second * half, -1
    )
    level = lax.broadcasted_iota(jnp.int32, (own, spots), 0)
    totals = [jnp.zeros((own, spots), F32) for _ in range(BASIS)]
    for tap in range(TAPS):
        hit = level == target[tap : tap + 1, :]
        for b in range(BASIS):
            totals[b] = totals[b] + jnp.where(hit, worth[b][tap : tap + 1, :], 0.0)
    for b in range(BASIS):
        back[:, pl.ds(b * spots, spots)] = totals[b].astype(BF16)

    tap_row, tap_col = to_row[:, :own], to_col[:, :own]
    in_grid = (tap_row + lat * rows >= 0) & (tap_row + lat * rows < total_rows)
    source = jnp.where(in_grid, spot_of(tap_row, tap_col, rows, cols, half), -1)
    level = lax.broadcasted_iota(jnp.int32, (spots, own), 0)
    totals = [jnp.zeros((spots, own), F32) for _ in range(BASIS)]
    for tap in range(TAPS):
        hit = level == source[tap : tap + 1, :]
        for b in range(BASIS):
            totals[b] = totals[b] + jnp.where(hit, worth[b][tap : tap + 1, :own], 0.0)
    for b in range(BASIS):
        ahead[pl.ds(b * own, own), :] = jnp.transpose(totals[b]).astype(BF16)

    slot = lax.broadcasted_iota(jnp.int32, (own, own), 0)
    pick_row, pick_col, used = halo_cell(slot, rows, cols)
    pick_row, pick_col = rest(pick_row, rows), rest(pick_col, cols)
    wanted = over(pick_col, half) * (rows * half) + pick_row * half + rest(pick_col, half)
    wanted = jnp.where(used, wanted, -1)
    pick[...] = (
        (lax.broadcasted_iota(jnp.int32, (own, own), 1) == wanted).astype(F32).astype(BF16)
    )

    def halo_copy(buffer, phase, number):
        start, size, shift, dlat = halo[number]
        return remote(
            hb.at[phase, pl.ds(start, size), :],
            buffer.at[pl.ds(own + start, size), :],
            halo_s.at[phase, number],
            halo_r.at[phase, number],
            beside(shift, lat + dlat),
        )

    def halo_start(block, buffer, phase):
        hb[phase] = jnp.dot(pick[...], block, preferred_element_type=F32).astype(BF16)
        for number in (4, 5, 6, 7, 2, 3, 0, 1):
            dlat = halo[number][3]
            if dlat == 0:
                halo_copy(buffer, phase, number).start()
            else:

                @pl.when(sends_to(dlat))
                def _():
                    halo_copy(buffer, phase, number).start()

    def halo_arrived(buffer, phase):
        for number in range(8):
            dlat = halo[number][3]
            if dlat == 0:
                halo_copy(buffer, phase, number).wait_recv()
            else:

                @pl.when(gets_from(dlat))
                def _():
                    halo_copy(buffer, phase, number).wait_recv()

    def halo_sent(buffer, phase):
        for number in range(8):
            dlat = halo[number][3]
            if dlat == 0:
                halo_copy(buffer, phase, number).wait_send()
            else:

                @pl.when(sends_to(dlat))
                def _():
                    halo_copy(buffer, phase, number).wait_send()

    def restore_copy(block, output, which, part, arrives_from):
        return remote(
            block.at[pl.ds(part * half_cells, half_cells), :],
            output.at[arrives_from],
            oc_s.at[which, part],
            oc_r.at[which, arrives_from],
            at(z, core, part, lat),
        )

    def restore_start(block, output, which):
        for part in range(2):
            there = matched & (core == part)

            @pl.when(there)
            def _():
                pltpu.make_async_copy(
                    block.at[pl.ds(part * half_cells, half_cells), :],
                    output.at[member],
                    oc_r.at[which, member],
                ).start()

            @pl.when(jnp.logical_not(there))
            def _():
                restore_copy(block, output, which, part, member).start()

    def restore_finish(block, output, which):
        for part in range(2):

            @pl.when(jnp.logical_not(matched & (core == part)))
            def _():
                restore_copy(block, output, which, part, member).wait_send()

        for origin in range(2):
            here = matched & (member == origin)

            @pl.when(here)
            def _():
                pltpu.make_async_copy(
                    block.at[pl.ds(0, half_cells), :],
                    output.at[origin],
                    oc_r.at[which, origin],
                ).wait()

            @pl.when(jnp.logical_not(here))
            def _():
                restore_copy(block, output, which, 0, origin).wait_recv()

    pair_spread = remote(spread.at[seg], spread_other, pair_s.at[0], pair_r.at[0], partner)

    def forward(section):
        halo_arrived(xp.at[section], section)
        widened = xp[section]
        mixed = None
        for b in range(BASIS):
            picked = jnp.dot(
                ahead[pl.ds(b * own, own), :], widened, preferred_element_type=F32
            ).astype(BF16)
            spread[section, pl.ds(b * own, own), :] = picked
            term = jnp.dot(picked, w_all[section, b], preferred_element_type=F32)
            mixed = term if mixed is None else mixed + term
        sigma = 1.0 / (1.0 + jnp.exp(-mixed))
        result = (xp[section, pl.ds(0, own), :].astype(F32) + mixed * sigma).astype(BF16)
        xp[section + 1, pl.ds(0, own), :] = result
        if section + 1 < n_seg:
            halo_start(result, xp.at[section + 1], section + 1)
        slope[section] = sigma * (1.0 + mixed * (1.0 - sigma))

        @pl.when(seg == section)
        def _():
            restore_start(xp.at[section + 1], out_ref, 0)
            pair_spread.start()

    pump_near(0, 4)
    regroup_arrived(in_ref, raw.at[0], 0)
    xp[0, pl.ds(0, own), :] = raw[0].reshape(own, channels)
    halo_start(xp[0, pl.ds(0, own), :], xp.at[0], 0)
    regroup(cot_ref, raw.at[1], 1)
    pump_near(4, n_pieces)
    fetch.wait()

    @pl.when(seg == 0)
    def _():
        forward(0)

    finish_near()
    pump_far()
    near_landed()
    pl.when(seg_far == 0)(finish_far)

    @pl.when(seg != 0)
    def _():
        forward(0)

    for section in range(1, n_seg):
        pl.when(seg_far == section)(finish_far)
        forward(section)

    regroup_arrived(cot_ref, raw.at[1], 1)
    grad[...] = raw[1].reshape(own, channels)

    def open_gate(section):
        gate = (grad[...].astype(F32) * slope[section]).astype(BF16)
        gp[section, pl.ds(0, own), :] = gate
        halo_start(gate, gp.at[section], n_seg + section)

    def pull(section):
        halo_arrived(gp.at[section], n_seg + section)
        for b in range(BASIS):
            feat[pl.ds(b * spots, spots), :] = lax.dot_general(
                gp[section], w_all[section, b], (((1,), (1,)), ((), ())), preferred_element_type=F32
            ).astype(BF16)
        pulled = jnp.dot(back[...], feat[...], preferred_element_type=F32)
        grad[...] = (grad[...].astype(F32) + pulled).astype(BF16)

    for section in range(n_seg - 1, 0, -1):

        @pl.when(seg < section)
        def _():
            open_gate(section)
            pull(section)

    open_gate(seg)
    pair_gate = remote(
        gp.at[seg, pl.ds(0, own), :], gate_other, pair_s.at[1], pair_r.at[1], partner
    )
    pair_gate.start()
    pair_spread.wait_recv()
    pair_gate.wait_recv()

    columns = pl.ds(pl.multiple_of(core * wide, wide), wide)
    gate_both = jnp.concatenate(
        [gp[seg, pl.ds(0, own), columns], gate_other[:, columns]], axis=0
    )
    for b in range(BASIS):
        both = jnp.concatenate(
            [spread[seg, pl.ds(b * own, own), :], spread_other[pl.ds(b * own, own), :]], axis=0
        )
        term = scale * lax.dot_general(
            both, gate_both, (((0,), (0,)), ((), ())), preferred_element_type=F32
        )
        for part in range(wide // LANES):
            product[part, pl.ds(b * channels, channels), :] = term[
                :, part * LANES : (part + 1) * LANES
            ]

    group = share * n_z

    parts = wide // LANES

    def ring_copy(way, step, part, e):
        return remote(
            ysend.at[way, step, part, pl.ds(e * group, group), :],
            yrecv.at[way, step, part, pl.ds(e * group, group), :],
            y_s.at[way, step, part, e],
            y_r.at[way, step, part, e],
            on_ring(ring_next if way == 0 else ring_prev),
        )

    def ring_step(step, way, part, e):
        distance = steps - step
        place = lax.rem(y + (distance if way == 0 else ring - distance), ring)
        span = pl.ds(e * group, group)
        term = blk[part, place, span, :]
        if step > 1 or (step == 1 and e == way):
            ring_copy(way, step - 1, part, e).wait_recv()
            term = (term.astype(F32) + yrecv[way, step - 1, part, span, :].astype(F32)).astype(
                BF16
            )
        ysend[way, step, part, span, :] = term
        ring_copy(way, step, part, e).start()

    def ring_begin():
        for part in range(parts):
            for place in range(ring):
                for e in range(2):
                    for i in range(share):
                        first = ((place // n_lat) * 2 + e) * n_lat * share
                        first = first + (place % n_lat) * share + i
                        blk[part, place, pl.ds(e * group + i * n_z, n_z), :] = product[
                            part, pl.ds(first, n_z, stride=ring * 2 * share), :
                        ].astype(BF16)
            for way in range(2):
                ring_step(0, way, part, way)
        for part in range(parts):
            for way in range(2):
                ring_step(1, way, part, 1 - way)

    ring_begin()
    pull(seg)
    restore_start(grad, grad_ref, 1)

    for part in range(parts):
        for way in range(2):
            ring_step(1, way, part, way)
    for step in range(2, steps):
        for half_turn in range(2):
            for part in range(parts):
                for way in range(2):
                    ring_step(step, way, part, way if half_turn else 1 - way)
    for part in range(parts):
        summed = blk[part, y].astype(F32)
        for way in range(2):
            for e in range(2):
                ring_copy(way, steps - 1, part, e).wait_recv()
            summed = summed + yrecv[way, steps - 1, part].astype(F32)
        acc[pl.ds(part * 2 * group, 2 * group), :] = summed

    def z_copy(shift):
        to = lax.rem(z + shift, n_z)
        return remote(
            zsend.at[to], zrecv.at[z], z_s.at[shift], z_r.at[shift], at(to, member, core, lat)
        )

    slab = parts * 2 * share
    for to in range(n_z):
        zsend[to] = acc[pl.ds(to, slab, stride=n_z), :].astype(BF16)
    for shift in range(1, n_z):
        z_copy(shift).start()
    total = zsend[z].astype(F32)
    for shift in range(1, n_z):
        from_z = lax.rem(z + n_z - shift, n_z)
        remote(
            zsend.at[0], zrecv.at[from_z], z_s.at[shift], z_r.at[shift], partner
        ).wait_recv()
        total = total + zrecv[from_z].astype(F32)

    def rows_for(e):
        return jnp.concatenate(
            [
                total[(2 * part + e) * share : (2 * part + e + 1) * share]
                for part in range(parts)
            ],
            axis=1,
        )

    mine = jnp.where(core == 0, rows_for(0), rows_for(1))
    fsend[pl.ds(0, share), :] = jnp.where(core == 0, rows_for(1), rows_for(0))
    last = remote(fsend, frecv, pair_s.at[2], pair_r.at[2], partner)
    last.start()
    last.wait_recv()
    theirs = frecv[pl.ds(0, share), :]
    wg_ref[:, :wide] = jnp.where(core == 0, mine, theirs)
    wg_ref[:, wide:] = jnp.where(core == 0, theirs, mine)

    restore_finish(xp.at[seg + 1], out_ref, 0)
    restore_finish(grad, grad_ref, 1)
    regroup_sent(in_ref, raw.at[0], 0)
    regroup_sent(cot_ref, raw.at[1], 1)
    for k in range(n_pieces):
        for way in range(2):
            own_copy(way, k).wait_send()
        far_copy(k // BASIS, k).wait_send()
        for which in range(3):
            side_copy(which, k).wait_send()
            for other in range(2):
                swap_copy(which, k, other).wait_send()
    for section in range(n_seg):
        halo_sent(xp.at[section], section)

        @pl.when(seg <= section)
        def _():
            halo_sent(gp.at[section], n_seg + section)

    pair_spread.wait_send()
    pair_gate.wait_send()
    last.wait_send()
    for step in range(steps):
        for way in range(2):
            for part in range(parts):
                for e in range(2):
                    if step or e == way:
                        ring_copy(way, step, part, e).wait_send()
    for shift in range(1, n_z):
        z_copy(shift).wait_send()


def per_device(inputs, cotangent, weights, basis_values, lat_step, lon_step):
    members, rows, half, channels = inputs.shape
    n_lon, n_lat, n_seg = (lax.axis_size(name) for name in ("lon", "lat", "segment"))
    n_z = n_lon // 4
    cols = 2 * half
    own = rows * cols
    spots = 2 * own
    ring = 2 * n_lat
    share = BASIS * channels // (n_lon * n_lat)
    wide = channels // 2
    parts = wide // LANES
    scale = 1.0 / math.sqrt(members * rows * n_lat * half * n_lon)

    vmem = pl.BlockSpec(memory_space=pltpu.VMEM)
    hbm = pl.BlockSpec(memory_space=pltpu.HBM)
    dma = pltpu.SemaphoreType.DMA
    section_out, section_grad, weight_grad = pl.pallas_call(
        functools.partial(step_kernel, (n_seg, n_lat, n_z, scale)),
        out_shape=(
            jax.ShapeDtypeStruct((2, rows * half, channels), BF16),
            jax.ShapeDtypeStruct((2, rows * half, channels), BF16),
            jax.ShapeDtypeStruct((share, channels), F32),
        ),
        in_specs=[hbm] * 6,
        out_specs=(vmem, vmem, vmem),
        scratch_shapes=[
            pltpu.VMEM((TAPS, rows * n_lat), jnp.int32),
            pltpu.VMEM((TAPS, rows * n_lat), jnp.int32),
            pltpu.VMEM((TAPS, BASIS, rows * n_lat), F32),
            pltpu.VMEM((n_seg, BASIS, channels, channels), BF16),
            pltpu.VMEM((2, 2, rows, half, channels), BF16),
            pltpu.VMEM((own, own), BF16),
            pltpu.VMEM((n_seg + 1, spots, channels), BF16),
            pltpu.VMEM((n_seg, spots, channels), BF16),
            pltpu.VMEM((own, channels), BF16),
            pltpu.VMEM((2 * n_seg, own, channels), BF16),
            pltpu.VMEM((BASIS * own, spots), BF16),
            pltpu.VMEM((own, BASIS * spots), BF16),
            pltpu.VMEM((n_seg, BASIS * own, channels), BF16),
            pltpu.VMEM((BASIS * own, channels), BF16),
            pltpu.VMEM((own, channels), BF16),
            pltpu.VMEM((n_seg, own, channels), F32),
            pltpu.VMEM((BASIS * spots, channels), BF16),
            pltpu.VMEM((wide // LANES, BASIS * channels, LANES), F32),
            pltpu.VMEM((parts, ring, 2 * share * n_z, LANES), BF16),
            pltpu.VMEM((2, n_lat, parts, 2 * share * n_z, LANES), BF16),
            pltpu.VMEM((2, n_lat, parts, 2 * share * n_z, LANES), BF16),
            pltpu.VMEM((parts * 2 * share * n_z, LANES), F32),
            pltpu.VMEM((n_z, parts * 2 * share, LANES), BF16),
            pltpu.VMEM((n_z, parts * 2 * share, LANES), BF16),
            pltpu.VMEM((-(-share // 8) * 8, wide), F32),
            pltpu.VMEM((-(-share // 8) * 8, wide), F32),
            dma((2, 2)),
            dma((2, 2)),
            dma((2, 2 * BASIS)),
            dma((2, 2 * BASIS)),
            dma((2 * BASIS,)),
            dma((2 * BASIS,)),
            dma((3, 2 * BASIS)),
            dma((3, 2 * BASIS)),
            dma((3, 2 * BASIS, 2)),
            dma((3, 2 * BASIS, 2)),
            dma((2 * n_seg, 8)),
            dma((2 * n_seg, 8)),
            dma((2, 2)),
            dma((2, 2)),
            dma((3,)),
            dma((3,)),
            dma((2, n_lat, parts, 2)),
            dma((2, n_lat, parts, 2)),
            dma((n_z,)),
            dma((n_z,)),
            dma((4,)),
        ],
        compiler_params=pltpu.CompilerParams(
            collective_id=0, has_side_effects=True, vmem_limit_bytes=50331648
        ),
        name="section_step",
    )(
        *(
            pltpu.with_memory_space_constraint(array, pltpu.HBM)
            for array in (
                jnp.transpose(lat_step),
                jnp.transpose(lon_step),
                jnp.transpose(basis_values, (1, 2, 0)),
                inputs,
                cotangent,
                weights[0],
            )
        )
    )
    block = (1,) + inputs.shape
    return (
        section_out.reshape(block),
        section_grad.reshape(block),
        weight_grad.reshape(1, -1),
    )


def solution(mesh):
    return jax.shard_map(
        per_device,
        mesh=mesh,
        in_specs=(
            P(None, "lat", "lon", None),
            P(None, "lat", "lon", None),
            P("segment", None, None, None),
            P(),
            P(),
            P(),
        ),
        out_specs=(
            P("segment", None, "lat", "lon", None),
            P("segment", None, "lat", "lon", None),
            P("segment", ("lon", "lat")),
        ),
        check_vma=False,
    )
```

```python
import functools
import math

import jax
import jax.numpy as jnp
from jax import lax
from jax.experimental import pallas as pl
from jax.experimental.pallas import tpu as pltpu
from jax.sharding import PartitionSpec as P

BASIS = 3
TAPS = 9
REACH = 2
LANES = 128
MESH = pl.DeviceIdType.MESH
F32 = jnp.float32
BF16 = jnp.bfloat16


def log2(number):
    power = number.bit_length() - 1
    assert 1 << power == number
    return power


def over(x, number):
    return lax.shift_right_arithmetic(x, jnp.full_like(x, log2(number)))


def rest(x, number):
    return x & (number - 1)


def halo_cell(slot, rows, cols):
    base = 4 * rows
    at = slot
    side_row = over(rest(at, 2 * rows), 2)
    side_col = rest(at, 2) + jnp.where(at < 2 * rows, -2, cols)
    at = slot - base
    far_row = over(rest(at, 2 * cols), cols) + jnp.where(at < 2 * cols, -2, rows)
    far_col = rest(at, cols)
    at = slot - base - 4 * cols
    inside = rest(at, 8)
    corner_row = over(inside, 2) + jnp.where(at < 16, -2, rows)
    corner_col = rest(inside, 2) + jnp.where(rest(over(at, 8), 2) == 0, -2, cols)
    in_side = slot < base
    in_far = slot < base + 4 * cols
    row = jnp.where(in_side, side_row, jnp.where(in_far, far_row, corner_row))
    col = jnp.where(in_side, side_col, jnp.where(in_far, far_col, corner_col))
    used = in_far | (inside < 4)
    return row, col, used


def own_cell(spot, rows, half):
    second = over(spot, rows * half)
    at = rest(spot, rows * half)
    return over(at, half), rest(at, half) + second * half


def spot_of(row, col, rows, cols, half):
    own = rows * cols
    inner = (row >= 0) & (row < rows)
    mid = (col >= 0) & (col < cols)
    side = jnp.where(col < 0, col + 2, col - cols)
    far = jnp.where(row < 0, row + 2, row - rows)
    right = (col >= cols).astype(jnp.int32)
    down = (row >= rows).astype(jnp.int32)
    second = (col >= half).astype(jnp.int32)
    at_own = second * (rows * half) + row * half + col - second * half
    at_side = own + right * (2 * rows) + row * 2 + side
    base = own + 4 * rows
    at_far = base + down * (2 * cols) + far * cols + col
    at_corner = base + 4 * cols + (down * 2 + right) * 8 + far * 2 + side
    return jnp.where(
        inner, jnp.where(mid, at_own, at_side), jnp.where(mid, at_far, at_corner)
    )


def step_kernel(
    sizes,
    lat_hbm,
    lon_hbm,
    basis_hbm,
    in_ref,
    cot_ref,
    w_hbm,
    out_ref,
    grad_ref,
    wg_ref,
    lat_ref,
    lon_ref,
    basis_ref,
    w_all,
    raw,
    pick,
    xp,
    gp,
    grad,
    hb,
    ahead,
    back,
    spread,
    spread_other,
    gate_other,
    slope,
    feat,
    product,
    blk,
    ysend,
    yrecv,
    acc,
    zsend,
    zrecv,
    fsend,
    frecv,
    cin_s,
    cin_r,
    own_s,
    own_r,
    far_s,
    far_r,
    side_s,
    side_r,
    swap_s,
    swap_r,
    halo_s,
    halo_r,
    oc_s,
    oc_r,
    pair_s,
    pair_r,
    y_s,
    y_r,
    z_s,
    z_r,
    w_sem,
):
    n_seg, n_lat, n_z, scale = sizes
    rows, half, channels = in_ref.shape[1:]
    half_cells = rows * half
    cols = 2 * half
    own = rows * cols
    spots = 2 * own
    ring = 2 * n_lat
    steps = ring // 2
    share = BASIS * channels // (n_z * ring * 2)
    wide = channels // 2

    lon = lax.axis_index("lon")
    lat = lax.axis_index("lat")
    seg = lax.axis_index("segment")
    z = lon // 4
    member = (lon // 2) % 2
    core = lon % 2
    pos = z * 2 + core
    y = member * n_lat + lat

    def at(z_to, member_to, core_to, lat_to, seg_to=seg):
        return {"lon": z_to * 4 + member_to * 2 + core_to, "lat": lat_to, "segment": seg_to}

    def beside(shift, lat_to):
        place = lax.rem(pos + shift + 2 * n_z, 2 * n_z)
        return at(place // 2, member, place % 2, lat_to)

    has_up = lat > 0
    has_down = lat < n_lat - 1
    seg_next = lax.rem(seg + 1, n_seg)
    seg_prev = lax.rem(seg + n_seg - 1, n_seg)
    seg_far = lax.rem(seg + 2, n_seg)
    matched = core == member

    base = 4 * rows
    corner = base + 4 * cols
    halo = [
        (0, 2 * rows, 1, 0),
        (2 * rows, 2 * rows, -1, 0),
        (base, 2 * cols, 0, 1),
        (base + 2 * cols, 2 * cols, 0, -1),
        (corner, 8, 1, 1),
        (corner + 8, 8, -1, 1),
        (corner + 16, 8, 1, -1),
        (corner + 24, 8, -1, -1),
    ]

    def sends_to(dlat):
        return has_down if dlat > 0 else has_up

    def gets_from(dlat):
        return has_up if dlat > 0 else has_down

    ring_next = lax.rem(y + 1, ring)
    ring_prev = lax.rem(y + ring - 1, ring)

    def on_ring(place):
        return at(z, place // n_lat, core, lax.rem(place, n_lat))

    partner = at(z, member, 1 - core, lat)

    fetch = pltpu.make_async_copy(w_hbm, w_all.at[seg], w_sem.at[0])
    tables = [
        pltpu.make_async_copy(table_hbm, table_ref, w_sem.at[1 + number])
        for number, (table_hbm, table_ref) in enumerate(
            ((lat_hbm, lat_ref), (lon_hbm, lon_ref), (basis_hbm, basis_ref))
        )
    ]
    for table in tables:
        table.start()
    fetch.start()

    barrier = pltpu.get_barrier_semaphore()

    def greet(device):
        pl.semaphore_signal(barrier, inc=1, device_id=device, device_id_type=MESH)

    for shift in range(1, n_z):
        greet(at(lax.rem(z + shift, n_z), member, core, lat))
    greet(on_ring(ring_next))
    greet(on_ring(ring_prev))
    greet(partner)
    for _, _, shift, dlat in halo:
        if dlat == 0:
            greet(beside(shift, lat))
        else:

            @pl.when(sends_to(dlat))
            def _():
                greet(beside(shift, lat + dlat))

    for other in range(2):

        @pl.when(jnp.logical_not(matched & (member == other)))
        def _():
            greet(at(z, other, member, lat))

        @pl.when(jnp.logical_not(matched & (core == other)))
        def _():
            greet(at(z, core, other, lat))

    greet(at(z, member, core, lat, seg_next))
    greet(at(z, member, core, lat, seg_prev))

    met = (n_z - 1) + 3 + 2 + 4 + 2
    met = met + jnp.where(has_up, 3, 0) + jnp.where(has_down, 3, 0)
    met = met - jnp.where(matched, 2, 0)
    pl.semaphore_wait(barrier, met)

    def remote(src, dst, send_sem, recv_sem, device):
        return pltpu.make_async_remote_copy(
            src_ref=src,
            dst_ref=dst,
            send_sem=send_sem,
            recv_sem=recv_sem,
            device_id=device,
            device_id_type=MESH,
        )

    def slot_of(buffer, part):
        return buffer.at[part]

    def regroup(source, buffer, which):
        for to in range(2):
            there = matched & (member == to)

            @pl.when(there)
            def _():
                pltpu.make_async_copy(
                    source.at[to], slot_of(buffer, core), cin_r.at[which, core]
                ).start()

            @pl.when(jnp.logical_not(there))
            def _():
                remote(
                    source.at[to],
                    slot_of(buffer, core),
                    cin_s.at[which, to],
                    cin_r.at[which, core],
                    at(z, to, member, lat),
                ).start()

    def regroup_arrived(source, buffer, which):
        for part in range(2):
            here = matched & (core == part)

            @pl.when(here)
            def _():
                pltpu.make_async_copy(
                    source.at[0], slot_of(buffer, part), cin_r.at[which, part]
                ).wait()

            @pl.when(jnp.logical_not(here))
            def _():
                remote(
                    source.at[0],
                    slot_of(buffer, part),
                    cin_s.at[which, 0],
                    cin_r.at[which, part],
                    partner,
                ).wait_recv()

    def regroup_sent(source, buffer, which):
        for to in range(2):

            @pl.when(jnp.logical_not(matched & (member == to)))
            def _():
                remote(
                    source.at[to],
                    slot_of(buffer, core),
                    cin_s.at[which, to],
                    cin_r.at[which, core],
                    partner,
                ).wait_send()

    regroup(in_ref, raw.at[0], 0)

    n_pieces = 2 * BASIS
    part_rows = channels // 8
    orders = (tuple(range(n_pieces)), tuple((k + BASIS) % n_pieces for k in range(n_pieces)))
    sections = (seg_prev, seg_next, seg_far)
    parities = (lax.rem(y, 2), lax.rem(z, 2))
    sides = (
        (on_ring(ring_next), on_ring(ring_prev)),
        (
            at(lax.rem(z + 1, n_z), member, core, lat),
            at(lax.rem(z + n_z - 1, n_z), member, core, lat),
        ),
    )

    def axis_of(which, k):
        return which if which < 2 else k // BASIS

    def piece(weights, k, of_parity, of_core):
        start = (2 * of_parity + of_core) * (channels // 4) + (k % 2) * part_rows
        return weights.at[k // 2, pl.ds(pl.multiple_of(start, part_rows), part_rows), :]

    def own_copy(way, k):
        return remote(
            piece(w_hbm, k, parities[way], core),
            piece(w_all.at[seg], k, parities[way], core),
            own_s.at[way, k],
            own_r.at[way, k],
            at(z, member, core, lat, seg_prev if way else seg_next),
        )

    def own_landed(way, k):
        landing = piece(w_all.at[sections[way]], k, parities[way], core)
        remote(landing, landing, own_s.at[way, k], own_r.at[way, k], partner).wait_recv()

    def far_copy(way, k):
        moved = piece(w_all.at[sections[way]], k, parities[way], core)
        return remote(
            moved,
            moved,
            far_s.at[k],
            far_r.at[k],
            at(z, member, core, lat, seg_prev if way else seg_next),
        )

    def far_landed(k):
        landing = piece(w_all.at[seg_far], k, parities[axis_of(2, k)], core)
        remote(landing, landing, far_s.at[k], far_r.at[k], partner).wait_recv()

    def side_copy(which, k):
        axis = axis_of(which, k)
        moved = piece(w_all.at[sections[which]], k, parities[axis], core)
        return remote(
            moved, moved, side_s.at[which, k], side_r.at[which, k], sides[axis][k % 2]
        )

    def side_landed(which, k):
        landing = piece(w_all.at[sections[which]], k, 1 - parities[axis_of(which, k)], core)
        remote(landing, landing, side_s.at[which, k], side_r.at[which, k], partner).wait_recv()

    def swap_of(which, k, other, of_core):
        parity = parities[axis_of(which, k)]
        return piece(w_all.at[sections[which]], k, 1 - parity if other else parity, of_core)

    def swap_copy(which, k, other):
        moved = swap_of(which, k, other, core)
        return remote(
            moved, moved, swap_s.at[which, k, other], swap_r.at[which, k, other], partner
        )

    def swap_landed(which, k, other):
        landing = swap_of(which, k, other, 1 - core)
        remote(
            landing, landing, swap_s.at[which, k, other], swap_r.at[which, k, other], partner
        ).wait_recv()

    for step in range(n_pieces):
        for way in range(2):
            own_copy(way, orders[way][step]).start()

    def pump_near(first, last, both):
        for step in range(first, last):
            for way in (1, 0):
                k = orders[way][step]
                own_landed(way, k)
                if way or both:
                    side_copy(way, k).start()
                if step < BASIS:
                    far_copy(way, k).start()
                swap_copy(way, k, 0).start()

    def pump_far():
        for step in range(BASIS):
            for way in range(2):
                k = orders[way][step]
                far_landed(k)
                side_copy(2, k).start()
                swap_copy(2, k, 0).start()

    def sides_landed(which):
        order = orders[which] if which < 2 else range(n_pieces)
        for k in order:
            side_landed(which, k)
            swap_copy(which, k, 1).start()

    def swaps_landed(which):
        for k in range(n_pieces):
            for other in range(2):
                swap_landed(which, k, other)

    def weights_here(section):
        @pl.when(seg_far == section)
        def _():
            sides_landed(2)
            swaps_landed(2)

        for which in range(2):

            @pl.when(sections[which] == section)
            def _():
                swaps_landed(which)

    for buffer in [xp.at[s] for s in range(n_seg)] + [gp.at[s] for s in range(n_seg)]:

        @pl.when(jnp.logical_not(has_up))
        def _():
            buffer[pl.ds(own + base, 2 * cols), :] = jnp.zeros((2 * cols, channels), BF16)
            buffer[pl.ds(own + corner, 16), :] = jnp.zeros((16, channels), BF16)

        @pl.when(jnp.logical_not(has_down))
        def _():
            buffer[pl.ds(own + base + 2 * cols, 2 * cols), :] = jnp.zeros((2 * cols, channels), BF16)
            buffer[pl.ds(own + corner + 16, 16), :] = jnp.zeros((16, channels), BF16)

    spot = lax.broadcasted_iota(jnp.int32, (16, spots), 1)
    inner_row, inner_col = own_cell(spot, rows, half)
    outer_row, outer_col, used = halo_cell(spot - own, rows, cols)
    spot_row = jnp.where(spot < own, inner_row, outer_row)
    spot_col = jnp.where(spot < own, inner_col, outer_col)
    used = (spot < own) | used
    grid_row = jnp.where(used, spot_row + lat * rows, -1)[:1]
    total_rows = n_lat * rows
    chosen = (
        lax.broadcasted_iota(jnp.int32, (total_rows, spots), 0)
        == jnp.broadcast_to(grid_row, (total_rows, spots))
    ).astype(F32).astype(BF16)

    for table in tables:
        table.wait()

    def of_spot(taps):
        return jnp.dot(taps.astype(F32).astype(BF16), chosen, preferred_element_type=F32)

    to_row = of_spot(lat_ref[...]).astype(jnp.int32) + spot_row[:TAPS]
    to_col = of_spot(lon_ref[...]).astype(jnp.int32) + spot_col[:TAPS]
    worth = [of_spot(basis_ref[:, b, :]) for b in range(BASIS)]

    lands = (to_row >= 0) & (to_row < rows) & (to_col >= 0) & (to_col < cols)
    second = (to_col >= half).astype(jnp.int32)
    target = jnp.where(
        lands, second * (rows * half) + to_row * half + to_col - second * half, -1
    )
    level = lax.broadcasted_iota(jnp.int32, (own, spots), 0)
    totals = [jnp.zeros((own, spots), F32) for _ in range(BASIS)]
    for tap in range(TAPS):
        hit = level == target[tap : tap + 1, :]
        for b in range(BASIS):
            totals[b] = totals[b] + jnp.where(hit, worth[b][tap : tap + 1, :], 0.0)
    for b in range(BASIS):
        back[:, pl.ds(b * spots, spots)] = totals[b].astype(BF16)

    tap_row, tap_col = to_row[:, :own], to_col[:, :own]
    in_grid = (tap_row + lat * rows >= 0) & (tap_row + lat * rows < total_rows)
    source = jnp.where(in_grid, spot_of(tap_row, tap_col, rows, cols, half), -1)
    level = lax.broadcasted_iota(jnp.int32, (spots, own), 0)
    totals = [jnp.zeros((spots, own), F32) for _ in range(BASIS)]
    for tap in range(TAPS):
        hit = level == source[tap : tap + 1, :]
        for b in range(BASIS):
            totals[b] = totals[b] + jnp.where(hit, worth[b][tap : tap + 1, :own], 0.0)
    for b in range(BASIS):
        ahead[pl.ds(b * own, own), :] = jnp.transpose(totals[b]).astype(BF16)

    slot = lax.broadcasted_iota(jnp.int32, (own, own), 0)
    pick_row, pick_col, used = halo_cell(slot, rows, cols)
    pick_row, pick_col = rest(pick_row, rows), rest(pick_col, cols)
    wanted = over(pick_col, half) * (rows * half) + pick_row * half + rest(pick_col, half)
    wanted = jnp.where(used, wanted, -1)
    pick[...] = (
        (lax.broadcasted_iota(jnp.int32, (own, own), 1) == wanted).astype(F32).astype(BF16)
    )

    def halo_copy(buffer, phase, number):
        start, size, shift, dlat = halo[number]
        return remote(
            hb.at[phase, pl.ds(start, size), :],
            buffer.at[pl.ds(own + start, size), :],
            halo_s.at[phase, number],
            halo_r.at[phase, number],
            beside(shift, lat + dlat),
        )

    def halo_start(block, buffer, phase):
        hb[phase] = jnp.dot(pick[...], block, preferred_element_type=F32).astype(BF16)
        for number in (4, 5, 6, 7, 2, 3, 0, 1):
            dlat = halo[number][3]
            if dlat == 0:
                halo_copy(buffer, phase, number).start()
            else:

                @pl.when(sends_to(dlat))
                def _():
                    halo_copy(buffer, phase, number).start()

    def halo_arrived(buffer, phase):
        for number in range(8):
            dlat = halo[number][3]
            if dlat == 0:
                halo_copy(buffer, phase, number).wait_recv()
            else:

                @pl.when(gets_from(dlat))
                def _():
                    halo_copy(buffer, phase, number).wait_recv()

    def halo_sent(buffer, phase):
        for number in range(8):
            dlat = halo[number][3]
            if dlat == 0:
                halo_copy(buffer, phase, number).wait_send()
            else:

                @pl.when(sends_to(dlat))
                def _():
                    halo_copy(buffer, phase, number).wait_send()

    def restore_copy(block, output, which, part, arrives_from):
        return remote(
            block.at[pl.ds(part * half_cells, half_cells), :],
            output.at[arrives_from],
            oc_s.at[which, part],
            oc_r.at[which, arrives_from],
            at(z, core, part, lat),
        )

    def restore_start(block, output, which):
        for part in range(2):
            there = matched & (core == part)

            @pl.when(there)
            def _():
                pltpu.make_async_copy(
                    block.at[pl.ds(part * half_cells, half_cells), :],
                    output.at[member],
                    oc_r.at[which, member],
                ).start()

            @pl.when(jnp.logical_not(there))
            def _():
                restore_copy(block, output, which, part, member).start()

    def restore_finish(block, output, which):
        for part in range(2):

            @pl.when(jnp.logical_not(matched & (core == part)))
            def _():
                restore_copy(block, output, which, part, member).wait_send()

        for origin in range(2):
            here = matched & (member == origin)

            @pl.when(here)
            def _():
                pltpu.make_async_copy(
                    block.at[pl.ds(0, half_cells), :],
                    output.at[origin],
                    oc_r.at[which, origin],
                ).wait()

            @pl.when(jnp.logical_not(here))
            def _():
                restore_copy(block, output, which, 0, origin).wait_recv()

    pair_spread = remote(spread.at[seg], spread_other, pair_s.at[0], pair_r.at[0], partner)

    def forward(section):
        halo_arrived(xp.at[section], section)
        widened = xp[section]
        mixed = None
        for b in range(BASIS):
            picked = jnp.dot(
                ahead[pl.ds(b * own, own), :], widened, preferred_element_type=F32
            ).astype(BF16)
            spread[section, pl.ds(b * own, own), :] = picked
            term = jnp.dot(picked, w_all[section, b], preferred_element_type=F32)
            mixed = term if mixed is None else mixed + term
        sigma = 1.0 / (1.0 + jnp.exp(-mixed))
        result = (xp[section, pl.ds(0, own), :].astype(F32) + mixed * sigma).astype(BF16)
        xp[section + 1, pl.ds(0, own), :] = result
        if section + 1 < n_seg:
            halo_start(result, xp.at[section + 1], section + 1)
        slope[section] = sigma * (1.0 + mixed * (1.0 - sigma))

        @pl.when(seg == section)
        def _():
            restore_start(xp.at[section + 1], out_ref, 0)
            pair_spread.start()

    early = 4
    pump_near(0, early, False)
    regroup_arrived(in_ref, raw.at[0], 0)
    xp[0, pl.ds(0, own), :] = raw[0].reshape(own, channels)
    halo_start(xp[0, pl.ds(0, own), :], xp.at[0], 0)
    for step in range(early):
        side_copy(0, orders[0][step]).start()
    pump_near(early, n_pieces, True)
    fetch.wait()

    @pl.when(seg == 0)
    def _():
        forward(0)

    sides_landed(1)
    pump_far()
    sides_landed(0)

    @pl.when(seg != 0)
    def _():
        weights_here(0)
        forward(0)

    regroup(cot_ref, raw.at[1], 1)
    for section in range(1, n_seg):
        weights_here(section)
        forward(section)

    regroup_arrived(cot_ref, raw.at[1], 1)
    grad[...] = raw[1].reshape(own, channels)

    def open_gate(section):
        gate = (grad[...].astype(F32) * slope[section]).astype(BF16)
        gp[section, pl.ds(0, own), :] = gate
        halo_start(gate, gp.at[section], n_seg + section)

    def pull(section):
        halo_arrived(gp.at[section], n_seg + section)
        for b in range(BASIS):
            feat[pl.ds(b * spots, spots), :] = lax.dot_general(
                gp[section], w_all[section, b], (((1,), (1,)), ((), ())), preferred_element_type=F32
            ).astype(BF16)
        pulled = jnp.dot(back[...], feat[...], preferred_element_type=F32)
        grad[...] = (grad[...].astype(F32) + pulled).astype(BF16)

    for section in range(n_seg - 1, 0, -1):

        @pl.when(seg < section)
        def _():
            open_gate(section)
            pull(section)

    open_gate(seg)
    pair_gate = remote(
        gp.at[seg, pl.ds(0, own), :], gate_other, pair_s.at[1], pair_r.at[1], partner
    )
    pair_gate.start()
    pair_spread.wait_recv()
    pair_gate.wait_recv()

    columns = pl.ds(pl.multiple_of(core * wide, wide), wide)
    gate_both = jnp.concatenate(
        [gp[seg, pl.ds(0, own), columns], gate_other[:, columns]], axis=0
    )
    for b in range(BASIS):
        both = jnp.concatenate(
            [spread[seg, pl.ds(b * own, own), :], spread_other[pl.ds(b * own, own), :]], axis=0
        )
        term = scale * lax.dot_general(
            both, gate_both, (((0,), (0,)), ((), ())), preferred_element_type=F32
        )
        for part in range(wide // LANES):
            product[part, pl.ds(b * channels, channels), :] = term[
                :, part * LANES : (part + 1) * LANES
            ]

    group = share * n_z

    parts = wide // LANES

    def ring_copy(way, step, part, e):
        return remote(
            ysend.at[way, step, part, pl.ds(e * group, group), :],
            yrecv.at[way, step, part, pl.ds(e * group, group), :],
            y_s.at[way, step, part, e],
            y_r.at[way, step, part, e],
            on_ring(ring_next if way == 0 else ring_prev),
        )

    def ring_step(step, way, part, e):
        distance = steps - step
        place = lax.rem(y + (distance if way == 0 else ring - distance), ring)
        span = pl.ds(e * group, group)
        term = blk[part, place, span, :]
        if step > 1 or (step == 1 and e == way):
            ring_copy(way, step - 1, part, e).wait_recv()
            term = (term.astype(F32) + yrecv[way, step - 1, part, span, :].astype(F32)).astype(
                BF16
            )
        ysend[way, step, part, span, :] = term
        ring_copy(way, step, part, e).start()

    def ring_begin():
        for part in range(parts):
            for place in range(ring):
                for e in range(2):
                    for i in range(share):
                        first = ((place // n_lat) * 2 + e) * n_lat * share
                        first = first + (place % n_lat) * share + i
                        blk[part, place, pl.ds(e * group + i * n_z, n_z), :] = product[
                            part, pl.ds(first, n_z, stride=ring * 2 * share), :
                        ].astype(BF16)
            for way in range(2):
                ring_step(0, way, part, way)
        for part in range(parts):
            for way in range(2):
                ring_step(1, way, part, 1 - way)

    ring_begin()
    pull(seg)
    restore_start(grad, grad_ref, 1)

    for part in range(parts):
        for way in range(2):
            ring_step(1, way, part, way)
    for step in range(2, steps):
        for half_turn in range(2):
            for part in range(parts):
                for way in range(2):
                    ring_step(step, way, part, way if half_turn else 1 - way)
    for part in range(parts):
        summed = blk[part, y].astype(F32)
        for way in range(2):
            for e in range(2):
                ring_copy(way, steps - 1, part, e).wait_recv()
            summed = summed + yrecv[way, steps - 1, part].astype(F32)
        acc[pl.ds(part * 2 * group, 2 * group), :] = summed

    def z_copy(shift):
        to = lax.rem(z + shift, n_z)
        return remote(
            zsend.at[to], zrecv.at[z], z_s.at[shift], z_r.at[shift], at(to, member, core, lat)
        )

    slab = parts * 2 * share
    for to in range(n_z):
        zsend[to] = acc[pl.ds(to, slab, stride=n_z), :].astype(BF16)
    for shift in range(1, n_z):
        z_copy(shift).start()
    total = zsend[z].astype(F32)
    for shift in range(1, n_z):
        from_z = lax.rem(z + n_z - shift, n_z)
        remote(
            zsend.at[0], zrecv.at[from_z], z_s.at[shift], z_r.at[shift], partner
        ).wait_recv()
        total = total + zrecv[from_z].astype(F32)

    def rows_for(e):
        return jnp.concatenate(
            [
                total[(2 * part + e) * share : (2 * part + e + 1) * share]
                for part in range(parts)
            ],
            axis=1,
        )

    mine = jnp.where(core == 0, rows_for(0), rows_for(1))
    fsend[pl.ds(0, share), :] = jnp.where(core == 0, rows_for(1), rows_for(0))
    last = remote(fsend, frecv, pair_s.at[2], pair_r.at[2], partner)
    last.start()
    last.wait_recv()
    theirs = frecv[pl.ds(0, share), :]
    wg_ref[:, :wide] = jnp.where(core == 0, mine, theirs)
    wg_ref[:, wide:] = jnp.where(core == 0, theirs, mine)

    restore_finish(xp.at[seg + 1], out_ref, 0)
    restore_finish(grad, grad_ref, 1)
    regroup_sent(in_ref, raw.at[0], 0)
    regroup_sent(cot_ref, raw.at[1], 1)
    for k in range(n_pieces):
        for way in range(2):
            own_copy(way, k).wait_send()
        far_copy(k // BASIS, k).wait_send()
        for which in range(3):
            side_copy(which, k).wait_send()
            for other in range(2):
                swap_copy(which, k, other).wait_send()
    for section in range(n_seg):
        halo_sent(xp.at[section], section)

        @pl.when(seg <= section)
        def _():
            halo_sent(gp.at[section], n_seg + section)

    pair_spread.wait_send()
    pair_gate.wait_send()
    last.wait_send()
    for step in range(steps):
        for way in range(2):
            for part in range(parts):
                for e in range(2):
                    if step or e == way:
                        ring_copy(way, step, part, e).wait_send()
    for shift in range(1, n_z):
        z_copy(shift).wait_send()


def per_device(inputs, cotangent, weights, basis_values, lat_step, lon_step):
    members, rows, half, channels = inputs.shape
    n_lon, n_lat, n_seg = (lax.axis_size(name) for name in ("lon", "lat", "segment"))
    n_z = n_lon // 4
    cols = 2 * half
    own = rows * cols
    spots = 2 * own
    ring = 2 * n_lat
    share = BASIS * channels // (n_lon * n_lat)
    wide = channels // 2
    parts = wide // LANES
    scale = 1.0 / math.sqrt(members * rows * n_lat * half * n_lon)

    vmem = pl.BlockSpec(memory_space=pltpu.VMEM)
    hbm = pl.BlockSpec(memory_space=pltpu.HBM)
    dma = pltpu.SemaphoreType.DMA
    section_out, section_grad, weight_grad = pl.pallas_call(
        functools.partial(step_kernel, (n_seg, n_lat, n_z, scale)),
        out_shape=(
            jax.ShapeDtypeStruct((2, rows * half, channels), BF16),
            jax.ShapeDtypeStruct((2, rows * half, channels), BF16),
            jax.ShapeDtypeStruct((share, channels), F32),
        ),
        in_specs=[hbm] * 6,
        out_specs=(vmem, vmem, vmem),
        scratch_shapes=[
            pltpu.VMEM((TAPS, rows * n_lat), jnp.int32),
            pltpu.VMEM((TAPS, rows * n_lat), jnp.int32),
            pltpu.VMEM((TAPS, BASIS, rows * n_lat), F32),
            pltpu.VMEM((n_seg, BASIS, channels, channels), BF16),
            pltpu.VMEM((2, 2, rows, half, channels), BF16),
            pltpu.VMEM((own, own), BF16),
            pltpu.VMEM((n_seg + 1, spots, channels), BF16),
            pltpu.VMEM((n_seg, spots, channels), BF16),
            pltpu.VMEM((own, channels), BF16),
            pltpu.VMEM((2 * n_seg, own, channels), BF16),
            pltpu.VMEM((BASIS * own, spots), BF16),
            pltpu.VMEM((own, BASIS * spots), BF16),
            pltpu.VMEM((n_seg, BASIS * own, channels), BF16),
            pltpu.VMEM((BASIS * own, channels), BF16),
            pltpu.VMEM((own, channels), BF16),
            pltpu.VMEM((n_seg, own, channels), F32),
            pltpu.VMEM((BASIS * spots, channels), BF16),
            pltpu.VMEM((wide // LANES, BASIS * channels, LANES), F32),
            pltpu.VMEM((parts, ring, 2 * share * n_z, LANES), BF16),
            pltpu.VMEM((2, n_lat, parts, 2 * share * n_z, LANES), BF16),
            pltpu.VMEM((2, n_lat, parts, 2 * share * n_z, LANES), BF16),
            pltpu.VMEM((parts * 2 * share * n_z, LANES), F32),
            pltpu.VMEM((n_z, parts * 2 * share, LANES), BF16),
            pltpu.VMEM((n_z, parts * 2 * share, LANES), BF16),
            pltpu.VMEM((-(-share // 8) * 8, wide), F32),
            pltpu.VMEM((-(-share // 8) * 8, wide), F32),
            dma((2, 2)),
            dma((2, 2)),
            dma((2, 2 * BASIS)),
            dma((2, 2 * BASIS)),
            dma((2 * BASIS,)),
            dma((2 * BASIS,)),
            dma((3, 2 * BASIS)),
            dma((3, 2 * BASIS)),
            dma((3, 2 * BASIS, 2)),
            dma((3, 2 * BASIS, 2)),
            dma((2 * n_seg, 8)),
            dma((2 * n_seg, 8)),
            dma((2, 2)),
            dma((2, 2)),
            dma((3,)),
            dma((3,)),
            dma((2, n_lat, parts, 2)),
            dma((2, n_lat, parts, 2)),
            dma((n_z,)),
            dma((n_z,)),
            dma((4,)),
        ],
        compiler_params=pltpu.CompilerParams(
            collective_id=0, has_side_effects=True, vmem_limit_bytes=50331648
        ),
        name="section_step",
    )(
        *(
            pltpu.with_memory_space_constraint(array, pltpu.HBM)
            for array in (
                jnp.transpose(lat_step),
                jnp.transpose(lon_step),
                jnp.transpose(basis_values, (1, 2, 0)),
                inputs,
                cotangent,
                weights[0],
            )
        )
    )
    block = (1,) + inputs.shape
    return (
        section_out.reshape(block),
        section_grad.reshape(block),
        weight_grad.reshape(1, -1),
    )


def solution(mesh):
    return jax.shard_map(
        per_device,
        mesh=mesh,
        in_specs=(
            P(None, "lat", "lon", None),
            P(None, "lat", "lon", None),
            P("segment", None, None, None),
            P(),
            P(),
            P(),
        ),
        out_specs=(
            P("segment", None, "lat", "lon", None),
            P("segment", None, "lat", "lon", None),
            P("segment", ("lon", "lat")),
        ),
        check_vma=False,
    )
```

```python
import functools
import math

import jax
import jax.numpy as jnp
from jax import lax
from jax.experimental import pallas as pl
from jax.experimental.pallas import tpu as pltpu
from jax.sharding import PartitionSpec as P

BASIS = 3
TAPS = 9
REACH = 2
LANES = 128
MESH = pl.DeviceIdType.MESH
F32 = jnp.float32
BF16 = jnp.bfloat16


def log2(number):
    power = number.bit_length() - 1
    assert 1 << power == number
    return power


def over(x, number):
    return lax.shift_right_arithmetic(x, jnp.full_like(x, log2(number)))


def rest(x, number):
    return x & (number - 1)


def halo_cell(slot, rows, cols):
    base = 4 * rows
    at = slot
    side_row = over(rest(at, 2 * rows), 2)
    side_col = rest(at, 2) + jnp.where(at < 2 * rows, -2, cols)
    at = slot - base
    far_row = over(rest(at, 2 * cols), cols) + jnp.where(at < 2 * cols, -2, rows)
    far_col = rest(at, cols)
    at = slot - base - 4 * cols
    inside = rest(at, 8)
    corner_row = over(inside, 2) + jnp.where(at < 16, -2, rows)
    corner_col = rest(inside, 2) + jnp.where(rest(over(at, 8), 2) == 0, -2, cols)
    in_side = slot < base
    in_far = slot < base + 4 * cols
    row = jnp.where(in_side, side_row, jnp.where(in_far, far_row, corner_row))
    col = jnp.where(in_side, side_col, jnp.where(in_far, far_col, corner_col))
    used = in_far | (inside < 4)
    return row, col, used


def own_cell(spot, rows, half):
    second = over(spot, rows * half)
    at = rest(spot, rows * half)
    return over(at, half), rest(at, half) + second * half


def spot_of(row, col, rows, cols, half):
    own = rows * cols
    inner = (row >= 0) & (row < rows)
    mid = (col >= 0) & (col < cols)
    side = jnp.where(col < 0, col + 2, col - cols)
    far = jnp.where(row < 0, row + 2, row - rows)
    right = (col >= cols).astype(jnp.int32)
    down = (row >= rows).astype(jnp.int32)
    second = (col >= half).astype(jnp.int32)
    at_own = second * (rows * half) + row * half + col - second * half
    at_side = own + right * (2 * rows) + row * 2 + side
    base = own + 4 * rows
    at_far = base + down * (2 * cols) + far * cols + col
    at_corner = base + 4 * cols + (down * 2 + right) * 8 + far * 2 + side
    return jnp.where(
        inner, jnp.where(mid, at_own, at_side), jnp.where(mid, at_far, at_corner)
    )


def step_kernel(
    sizes,
    lat_hbm,
    lon_hbm,
    basis_hbm,
    in_ref,
    cot_ref,
    w_hbm,
    out_ref,
    grad_ref,
    wg_ref,
    lat_ref,
    lon_ref,
    basis_ref,
    w_all,
    raw,
    pick,
    xp,
    gp,
    grad,
    hb,
    ahead,
    back,
    spread,
    spread_other,
    gate_other,
    slope,
    feat,
    product,
    blk,
    ysend,
    yrecv,
    acc,
    zsend,
    zrecv,
    fsend,
    frecv,
    cin_s,
    cin_r,
    own_s,
    own_r,
    far_s,
    far_r,
    side_s,
    side_r,
    swap_s,
    swap_r,
    halo_s,
    halo_r,
    oc_s,
    oc_r,
    pair_s,
    pair_r,
    y_s,
    y_r,
    z_s,
    z_r,
    w_sem,
    tokens,
):
    n_seg, n_lat, n_z, scale = sizes
    rows, half, channels = in_ref.shape[1:]
    half_cells = rows * half
    cols = 2 * half
    own = rows * cols
    spots = 2 * own
    ring = 2 * n_lat
    steps = ring // 2
    share = BASIS * channels // (n_z * ring * 2)
    wide = channels // 2

    lon = lax.axis_index("lon")
    lat = lax.axis_index("lat")
    seg = lax.axis_index("segment")
    z = lon // 4
    member = (lon // 2) % 2
    core = lon % 2
    pos = z * 2 + core
    y = member * n_lat + lat

    def at(z_to, member_to, core_to, lat_to, seg_to=seg):
        return {"lon": z_to * 4 + member_to * 2 + core_to, "lat": lat_to, "segment": seg_to}

    def beside(shift, lat_to):
        place = lax.rem(pos + shift + 2 * n_z, 2 * n_z)
        return at(place // 2, member, place % 2, lat_to)

    has_up = lat > 0
    has_down = lat < n_lat - 1
    seg_next = lax.rem(seg + 1, n_seg)
    seg_prev = lax.rem(seg + n_seg - 1, n_seg)
    seg_far = lax.rem(seg + 2, n_seg)
    matched = core == member

    base = 4 * rows
    corner = base + 4 * cols
    halo = [
        (0, 2 * rows, 1, 0),
        (2 * rows, 2 * rows, -1, 0),
        (base, 2 * cols, 0, 1),
        (base + 2 * cols, 2 * cols, 0, -1),
        (corner, 8, 1, 1),
        (corner + 8, 8, -1, 1),
        (corner + 16, 8, 1, -1),
        (corner + 24, 8, -1, -1),
    ]

    def sends_to(dlat):
        return has_down if dlat > 0 else has_up

    def gets_from(dlat):
        return has_up if dlat > 0 else has_down

    ring_next = lax.rem(y + 1, ring)
    ring_prev = lax.rem(y + ring - 1, ring)

    def on_ring(place):
        return at(z, place // n_lat, core, lax.rem(place, n_lat))

    partner = at(z, member, 1 - core, lat)

    fetch = pltpu.make_async_copy(w_hbm, w_all.at[seg], w_sem.at[0])
    tables = [
        pltpu.make_async_copy(table_hbm, table_ref, w_sem.at[1 + number])
        for number, (table_hbm, table_ref) in enumerate(
            ((lat_hbm, lat_ref), (lon_hbm, lon_ref), (basis_hbm, basis_ref))
        )
    ]
    for table in tables:
        table.start()
    fetch.start()

    barrier = pltpu.get_barrier_semaphore()

    def greet(device):
        pl.semaphore_signal(barrier, inc=1, device_id=device, device_id_type=MESH)

    z_next = at(lax.rem(z + 1, n_z), member, core, lat)
    z_prev = at(lax.rem(z + n_z - 1, n_z), member, core, lat)
    greet(z_next)
    greet(z_prev)
    greet(on_ring(ring_next))
    greet(on_ring(ring_prev))
    greet(partner)
    for _, _, shift, dlat in halo:
        if dlat == 0:
            greet(beside(shift, lat))
        else:

            @pl.when(sends_to(dlat))
            def _():
                greet(beside(shift, lat + dlat))

    for other in range(2):

        @pl.when(jnp.logical_not(matched & (member == other)))
        def _():
            greet(at(z, other, member, lat))

        @pl.when(jnp.logical_not(matched & (core == other)))
        def _():
            greet(at(z, core, other, lat))

    greet(at(z, member, core, lat, seg_next))
    greet(at(z, member, core, lat, seg_prev))

    met = 2 + 3 + 2 + 4 + 2
    met = met + jnp.where(has_up, 3, 0) + jnp.where(has_down, 3, 0)
    met = met - jnp.where(matched, 2, 0)
    pl.semaphore_wait(barrier, met)

    def remote(src, dst, send_sem, recv_sem, device):
        return pltpu.make_async_remote_copy(
            src_ref=src,
            dst_ref=dst,
            send_sem=send_sem,
            recv_sem=recv_sem,
            device_id=device,
            device_id_type=MESH,
        )

    def slot_of(buffer, part):
        return buffer.at[part]

    def regroup(source, buffer, which):
        for to in range(2):
            there = matched & (member == to)

            @pl.when(there)
            def _():
                pltpu.make_async_copy(
                    source.at[to], slot_of(buffer, core), cin_r.at[which, core]
                ).start()

            @pl.when(jnp.logical_not(there))
            def _():
                remote(
                    source.at[to],
                    slot_of(buffer, core),
                    cin_s.at[which, to],
                    cin_r.at[which, core],
                    at(z, to, member, lat),
                ).start()

    def regroup_arrived(source, buffer, which):
        for part in range(2):
            here = matched & (core == part)

            @pl.when(here)
            def _():
                pltpu.make_async_copy(
                    source.at[0], slot_of(buffer, part), cin_r.at[which, part]
                ).wait()

            @pl.when(jnp.logical_not(here))
            def _():
                remote(
                    source.at[0],
                    slot_of(buffer, part),
                    cin_s.at[which, 0],
                    cin_r.at[which, part],
                    partner,
                ).wait_recv()

    def regroup_sent(source, buffer, which):
        for to in range(2):

            @pl.when(jnp.logical_not(matched & (member == to)))
            def _():
                remote(
                    source.at[to],
                    slot_of(buffer, core),
                    cin_s.at[which, to],
                    cin_r.at[which, core],
                    partner,
                ).wait_send()

    regroup(in_ref, raw.at[0], 0)

    rounds = n_z // 2 - 1

    def token(number):
        if 1 < number <= rounds + 1:
            for way in range(2):
                pl.semaphore_wait(tokens.at[way, number - 2], 1)
        if number <= rounds:
            for way, neighbour in enumerate((z_next, z_prev)):
                pl.semaphore_signal(
                    tokens.at[way, number - 1],
                    inc=1,
                    device_id=neighbour,
                    device_id_type=MESH,
                )

    token(1)

    n_pieces = 2 * BASIS
    part_rows = channels // 8
    orders = (tuple(range(n_pieces)), tuple((k + BASIS) % n_pieces for k in range(n_pieces)))
    sections = (seg_prev, seg_next, seg_far)
    parity = lax.rem(z, 2)

    def piece(weights, k, of_parity, of_core):
        start = (2 * of_parity + of_core) * (channels // 4) + (k % 2) * part_rows
        return weights.at[k // 2, pl.ds(pl.multiple_of(start, part_rows), part_rows), :]

    def own_copy(way, k):
        return remote(
            piece(w_hbm, k, parity, core),
            piece(w_all.at[seg], k, parity, core),
            own_s.at[way, k],
            own_r.at[way, k],
            at(z, member, core, lat, seg_prev if way else seg_next),
        )

    def own_landed(way, k):
        landing = piece(w_all.at[sections[way]], k, parity, core)
        remote(landing, landing, own_s.at[way, k], own_r.at[way, k], partner).wait_recv()

    def far_copy(way, k):
        moved = piece(w_all.at[sections[way]], k, parity, core)
        return remote(
            moved,
            moved,
            far_s.at[k],
            far_r.at[k],
            at(z, member, core, lat, seg_prev if way else seg_next),
        )

    def far_landed(k):
        landing = piece(w_all.at[seg_far], k, parity, core)
        remote(landing, landing, far_s.at[k], far_r.at[k], partner).wait_recv()

    def side_copy(which, k):
        moved = piece(w_all.at[sections[which]], k, parity, core)
        return remote(
            moved, moved, side_s.at[which, k], side_r.at[which, k], z_prev if k % 2 else z_next
        )

    def side_landed(which, k):
        landing = piece(w_all.at[sections[which]], k, 1 - parity, core)
        remote(landing, landing, side_s.at[which, k], side_r.at[which, k], partner).wait_recv()

    def swap_copy(which, k, other):
        moved = piece(w_all.at[sections[which]], k, 1 - parity if other else parity, core)
        return remote(
            moved, moved, swap_s.at[which, k, other], swap_r.at[which, k, other], partner
        )

    def swap_landed(which, k, other):
        landing = piece(w_all.at[sections[which]], k, 1 - parity if other else parity, 1 - core)
        remote(
            landing, landing, swap_s.at[which, k, other], swap_r.at[which, k, other], partner
        ).wait_recv()

    for step in range(n_pieces):
        for way in range(2):
            own_copy(way, orders[way][step]).start()

    def pump_near(first, last):
        for step in range(first, last):
            for way in range(2):
                k = orders[way][step]
                own_landed(way, k)
                side_copy(way, k).start()
                if step < BASIS:
                    far_copy(way, k).start()
                swap_copy(way, k, 0).start()

    def finish_near():
        for step in range(n_pieces):
            for way in (1, 0):
                k = orders[way][step]
                side_landed(way, k)
                swap_copy(way, k, 1).start()

    def pump_far():
        for step in range(BASIS):
            for way in range(2):
                k = orders[way][step]
                far_landed(k)
                side_copy(2, k).start()
                swap_copy(2, k, 0).start()

    def near_landed(way):
        for k in orders[way]:
            for other in range(2):
                swap_landed(way, k, other)

    def weights_here(section):
        pl.when(seg_far == section)(finish_far)
        for way in range(2):

            @pl.when(sections[way] == section)
            def _():
                near_landed(way)

    def finish_far():
        for k in range(n_pieces):
            side_landed(2, k)
            swap_copy(2, k, 1).start()
        for k in range(n_pieces):
            for other in range(2):
                swap_landed(2, k, other)

    for buffer in [xp.at[s] for s in range(n_seg)] + [gp.at[s] for s in range(n_seg)]:

        @pl.when(jnp.logical_not(has_up))
        def _():
            buffer[pl.ds(own + base, 2 * cols), :] = jnp.zeros((2 * cols, channels), BF16)
            buffer[pl.ds(own + corner, 16), :] = jnp.zeros((16, channels), BF16)

        @pl.when(jnp.logical_not(has_down))
        def _():
            buffer[pl.ds(own + base + 2 * cols, 2 * cols), :] = jnp.zeros((2 * cols, channels), BF16)
            buffer[pl.ds(own + corner + 16, 16), :] = jnp.zeros((16, channels), BF16)

    spot = lax.broadcasted_iota(jnp.int32, (16, spots), 1)
    inner_row, inner_col = own_cell(spot, rows, half)
    outer_row, outer_col, used = halo_cell(spot - own, rows, cols)
    spot_row = jnp.where(spot < own, inner_row, outer_row)
    spot_col = jnp.where(spot < own, inner_col, outer_col)
    used = (spot < own) | used
    grid_row = jnp.where(used, spot_row + lat * rows, -1)[:1]
    total_rows = n_lat * rows
    chosen = (
        lax.broadcasted_iota(jnp.int32, (total_rows, spots), 0)
        == jnp.broadcast_to(grid_row, (total_rows, spots))
    ).astype(F32).astype(BF16)

    for table in tables:
        table.wait()

    def of_spot(taps):
        return jnp.dot(taps.astype(F32).astype(BF16), chosen, preferred_element_type=F32)

    to_row = of_spot(lat_ref[...]).astype(jnp.int32) + spot_row[:TAPS]
    to_col = of_spot(lon_ref[...]).astype(jnp.int32) + spot_col[:TAPS]
    worth = [of_spot(basis_ref[:, b, :]) for b in range(BASIS)]

    lands = (to_row >= 0) & (to_row < rows) & (to_col >= 0) & (to_col < cols)
    second = (to_col >= half).astype(jnp.int32)
    target = jnp.where(
        lands, second * (rows * half) + to_row * half + to_col - second * half, -1
    )
    level = lax.broadcasted_iota(jnp.int32, (own, spots), 0)
    totals = [jnp.zeros((own, spots), F32) for _ in range(BASIS)]
    for tap in range(TAPS):
        hit = level == target[tap : tap + 1, :]
        for b in range(BASIS):
            totals[b] = totals[b] + jnp.where(hit, worth[b][tap : tap + 1, :], 0.0)
    for b in range(BASIS):
        back[:, pl.ds(b * spots, spots)] = totals[b].astype(BF16)

    tap_row, tap_col = to_row[:, :own], to_col[:, :own]
    in_grid = (tap_row + lat * rows >= 0) & (tap_row + lat * rows < total_rows)
    source = jnp.where(in_grid, spot_of(tap_row, tap_col, rows, cols, half), -1)
    level = lax.broadcasted_iota(jnp.int32, (spots, own), 0)
    totals = [jnp.zeros((spots, own), F32) for _ in range(BASIS)]
    for tap in range(TAPS):
        hit = level == source[tap : tap + 1, :]
        for b in range(BASIS):
            totals[b] = totals[b] + jnp.where(hit, worth[b][tap : tap + 1, :own], 0.0)
    for b in range(BASIS):
        ahead[pl.ds(b * own, own), :] = jnp.transpose(totals[b]).astype(BF16)

    slot = lax.broadcasted_iota(jnp.int32, (own, own), 0)
    pick_row, pick_col, used = halo_cell(slot, rows, cols)
    pick_row, pick_col = rest(pick_row, rows), rest(pick_col, cols)
    wanted = over(pick_col, half) * (rows * half) + pick_row * half + rest(pick_col, half)
    wanted = jnp.where(used, wanted, -1)
    pick[...] = (
        (lax.broadcasted_iota(jnp.int32, (own, own), 1) == wanted).astype(F32).astype(BF16)
    )

    def halo_copy(buffer, phase, number):
        start, size, shift, dlat = halo[number]
        return remote(
            hb.at[phase, pl.ds(start, size), :],
            buffer.at[pl.ds(own + start, size), :],
            halo_s.at[phase, number],
            halo_r.at[phase, number],
            beside(shift, lat + dlat),
        )

    def halo_start(block, buffer, phase):
        hb[phase] = jnp.dot(pick[...], block, preferred_element_type=F32).astype(BF16)
        for number in (4, 5, 6, 7, 2, 3, 0, 1):
            dlat = halo[number][3]
            if dlat == 0:
                halo_copy(buffer, phase, number).start()
            else:

                @pl.when(sends_to(dlat))
                def _():
                    halo_copy(buffer, phase, number).start()

    def halo_arrived(buffer, phase):
        for number in range(8):
            dlat = halo[number][3]
            if dlat == 0:
                halo_copy(buffer, phase, number).wait_recv()
            else:

                @pl.when(gets_from(dlat))
                def _():
                    halo_copy(buffer, phase, number).wait_recv()

    def halo_sent(buffer, phase):
        for number in range(8):
            dlat = halo[number][3]
            if dlat == 0:
                halo_copy(buffer, phase, number).wait_send()
            else:

                @pl.when(sends_to(dlat))
                def _():
                    halo_copy(buffer, phase, number).wait_send()

    def restore_copy(block, output, which, part, arrives_from):
        return remote(
            block.at[pl.ds(part * half_cells, half_cells), :],
            output.at[arrives_from],
            oc_s.at[which, part],
            oc_r.at[which, arrives_from],
            at(z, core, part, lat),
        )

    def restore_start(block, output, which):
        for part in range(2):
            there = matched & (core == part)

            @pl.when(there)
            def _():
                pltpu.make_async_copy(
                    block.at[pl.ds(part * half_cells, half_cells), :],
                    output.at[member],
                    oc_r.at[which, member],
                ).start()

            @pl.when(jnp.logical_not(there))
            def _():
                restore_copy(block, output, which, part, member).start()

    def restore_finish(block, output, which):
        for part in range(2):

            @pl.when(jnp.logical_not(matched & (core == part)))
            def _():
                restore_copy(block, output, which, part, member).wait_send()

        for origin in range(2):
            here = matched & (member == origin)

            @pl.when(here)
            def _():
                pltpu.make_async_copy(
                    block.at[pl.ds(0, half_cells), :],
                    output.at[origin],
                    oc_r.at[which, origin],
                ).wait()

            @pl.when(jnp.logical_not(here))
            def _():
                restore_copy(block, output, which, 0, origin).wait_recv()

    pair_spread = remote(spread.at[seg], spread_other, pair_s.at[0], pair_r.at[0], partner)

    def forward(section):
        halo_arrived(xp.at[section], section)
        widened = xp[section]
        mixed = None
        for b in range(BASIS):
            picked = jnp.dot(
                ahead[pl.ds(b * own, own), :], widened, preferred_element_type=F32
            ).astype(BF16)
            spread[section, pl.ds(b * own, own), :] = picked
            term = jnp.dot(picked, w_all[section, b], preferred_element_type=F32)
            mixed = term if mixed is None else mixed + term
        sigma = 1.0 / (1.0 + jnp.exp(-mixed))
        result = (xp[section, pl.ds(0, own), :].astype(F32) + mixed * sigma).astype(BF16)
        xp[section + 1, pl.ds(0, own), :] = result
        if section + 1 < n_seg:
            halo_start(result, xp.at[section + 1], section + 1)
        slope[section] = sigma * (1.0 + mixed * (1.0 - sigma))

        @pl.when(seg == section)
        def _():
            restore_start(xp.at[section + 1], out_ref, 0)
            pair_spread.start()

    pump_near(0, 4)
    regroup_arrived(in_ref, raw.at[0], 0)
    xp[0, pl.ds(0, own), :] = raw[0].reshape(own, channels)
    token(2)
    halo_start(xp[0, pl.ds(0, own), :], xp.at[0], 0)
    token(3)
    regroup(cot_ref, raw.at[1], 1)
    pump_near(4, n_pieces)
    fetch.wait()

    @pl.when(seg == 0)
    def _():
        forward(0)

    finish_near()
    pump_far()
    @pl.when(seg != 0)
    def _():
        weights_here(0)
        forward(0)

    for section in range(1, n_seg):
        token(section + 3)
        weights_here(section)
        forward(section)
    for number in range(n_seg + 3, rounds + 1):
        token(number)

    regroup_arrived(cot_ref, raw.at[1], 1)
    grad[...] = raw[1].reshape(own, channels)

    def open_gate(section, then=None):
        gate = (grad[...].astype(F32) * slope[section]).astype(BF16)
        gp[section, pl.ds(0, own), :] = gate
        if then is not None:
            then()
        halo_start(gate, gp.at[section], n_seg + section)

    def pull(section):
        halo_arrived(gp.at[section], n_seg + section)
        for b in range(BASIS):
            feat[pl.ds(b * spots, spots), :] = lax.dot_general(
                gp[section], w_all[section, b], (((1,), (1,)), ((), ())), preferred_element_type=F32
            ).astype(BF16)
        pulled = jnp.dot(back[...], feat[...], preferred_element_type=F32)
        grad[...] = (grad[...].astype(F32) + pulled).astype(BF16)

    for section in range(n_seg - 1, 0, -1):

        @pl.when(seg < section)
        def _():
            open_gate(section)
            pull(section)

    pair_gate = remote(
        gp.at[seg, pl.ds(0, own), :], gate_other, pair_s.at[1], pair_r.at[1], partner
    )
    open_gate(seg, pair_gate.start)
    pair_spread.wait_recv()
    pair_gate.wait_recv()

    columns = pl.ds(pl.multiple_of(core * wide, wide), wide)
    gate_both = jnp.concatenate(
        [gp[seg, pl.ds(0, own), columns], gate_other[:, columns]], axis=0
    )
    for b in range(BASIS):
        both = jnp.concatenate(
            [spread[seg, pl.ds(b * own, own), :], spread_other[pl.ds(b * own, own), :]], axis=0
        )
        term = scale * lax.dot_general(
            both, gate_both, (((0,), (0,)), ((), ())), preferred_element_type=F32
        )
        for part in range(wide // LANES):
            product[part, pl.ds(b * channels, channels), :] = term[
                :, part * LANES : (part + 1) * LANES
            ]

    group = share * n_z

    parts = wide // LANES

    def ring_copy(way, step, part, e):
        return remote(
            ysend.at[way, step, part, pl.ds(e * group, group), :],
            yrecv.at[way, step, part, pl.ds(e * group, group), :],
            y_s.at[way, step, part, e],
            y_r.at[way, step, part, e],
            on_ring(ring_next if way == 0 else ring_prev),
        )

    def ring_step(step, way, part, e):
        distance = steps - step
        place = lax.rem(y + (distance if way == 0 else ring - distance), ring)
        span = pl.ds(e * group, group)
        term = blk[part, place, span, :]
        if step > 1 or (step == 1 and e == way):
            ring_copy(way, step - 1, part, e).wait_recv()
            term = (term.astype(F32) + yrecv[way, step - 1, part, span, :].astype(F32)).astype(
                BF16
            )
        ysend[way, step, part, span, :] = term
        ring_copy(way, step, part, e).start()

    def ring_begin():
        for part in range(parts):
            for place in range(ring):
                for e in range(2):
                    for i in range(share):
                        first = ((place // n_lat) * 2 + e) * n_lat * share
                        first = first + (place % n_lat) * share + i
                        blk[part, place, pl.ds(e * group + i * n_z, n_z), :] = product[
                            part, pl.ds(first, n_z, stride=ring * 2 * share), :
                        ].astype(BF16)
            for way in range(2):
                ring_step(0, way, part, way)
        for part in range(parts):
            for way in range(2):
                ring_step(1, way, part, 1 - way)

    ring_begin()
    for part in range(parts):
        for way in range(2):
            ring_step(1, way, part, way)
    pull(seg)
    restore_start(grad, grad_ref, 1)
    for step in range(2, steps):
        for half_turn in range(2):
            for part in range(parts):
                for way in range(2):
                    ring_step(step, way, part, way if half_turn else 1 - way)
    for part in range(parts):
        summed = blk[part, y].astype(F32)
        for way in range(2):
            for e in range(2):
                ring_copy(way, steps - 1, part, e).wait_recv()
            summed = summed + yrecv[way, steps - 1, part].astype(F32)
        acc[pl.ds(part * 2 * group, 2 * group), :] = summed

    def z_copy(shift):
        to = lax.rem(z + shift, n_z)
        return remote(
            zsend.at[to], zrecv.at[z], z_s.at[shift], z_r.at[shift], at(to, member, core, lat)
        )

    slab = parts * 2 * share
    for to in range(n_z):
        zsend[to] = acc[pl.ds(to, slab, stride=n_z), :].astype(BF16)
    token(rounds + 1)
    for shift in range(1, n_z):
        z_copy(shift).start()
    total = zsend[z].astype(F32)
    for shift in range(1, n_z):
        from_z = lax.rem(z + n_z - shift, n_z)
        remote(
            zsend.at[0], zrecv.at[from_z], z_s.at[shift], z_r.at[shift], partner
        ).wait_recv()
        total = total + zrecv[from_z].astype(F32)

    def rows_for(e):
        return jnp.concatenate(
            [
                total[(2 * part + e) * share : (2 * part + e + 1) * share]
                for part in range(parts)
            ],
            axis=1,
        )

    mine = jnp.where(core == 0, rows_for(0), rows_for(1))
    fsend[pl.ds(0, share), :] = jnp.where(core == 0, rows_for(1), rows_for(0))
    last = remote(fsend, frecv, pair_s.at[2], pair_r.at[2], partner)
    last.start()
    last.wait_recv()
    theirs = frecv[pl.ds(0, share), :]
    wg_ref[:, :wide] = jnp.where(core == 0, mine, theirs)
    wg_ref[:, wide:] = jnp.where(core == 0, theirs, mine)

    restore_finish(xp.at[seg + 1], out_ref, 0)
    restore_finish(grad, grad_ref, 1)
    regroup_sent(in_ref, raw.at[0], 0)
    regroup_sent(cot_ref, raw.at[1], 1)
    for k in range(n_pieces):
        for way in range(2):
            own_copy(way, k).wait_send()
        far_copy(k // BASIS, k).wait_send()
        for which in range(3):
            side_copy(which, k).wait_send()
            for other in range(2):
                swap_copy(which, k, other).wait_send()
    for section in range(n_seg):
        halo_sent(xp.at[section], section)

        @pl.when(seg <= section)
        def _():
            halo_sent(gp.at[section], n_seg + section)

    pair_spread.wait_send()
    pair_gate.wait_send()
    last.wait_send()
    for step in range(steps):
        for way in range(2):
            for part in range(parts):
                for e in range(2):
                    if step or e == way:
                        ring_copy(way, step, part, e).wait_send()
    for shift in range(1, n_z):
        z_copy(shift).wait_send()


def per_device(inputs, cotangent, weights, basis_values, lat_step, lon_step):
    members, rows, half, channels = inputs.shape
    n_lon, n_lat, n_seg = (lax.axis_size(name) for name in ("lon", "lat", "segment"))
    n_z = n_lon // 4
    cols = 2 * half
    own = rows * cols
    spots = 2 * own
    ring = 2 * n_lat
    share = BASIS * channels // (n_lon * n_lat)
    wide = channels // 2
    parts = wide // LANES
    scale = 1.0 / math.sqrt(members * rows * n_lat * half * n_lon)

    vmem = pl.BlockSpec(memory_space=pltpu.VMEM)
    hbm = pl.BlockSpec(memory_space=pltpu.HBM)
    dma = pltpu.SemaphoreType.DMA
    section_out, section_grad, weight_grad = pl.pallas_call(
        functools.partial(step_kernel, (n_seg, n_lat, n_z, scale)),
        out_shape=(
            jax.ShapeDtypeStruct((2, rows * half, channels), BF16),
            jax.ShapeDtypeStruct((2, rows * half, channels), BF16),
            jax.ShapeDtypeStruct((share, channels), F32),
        ),
        in_specs=[hbm] * 6,
        out_specs=(vmem, vmem, vmem),
        scratch_shapes=[
            pltpu.VMEM((TAPS, rows * n_lat), jnp.int32),
            pltpu.VMEM((TAPS, rows * n_lat), jnp.int32),
            pltpu.VMEM((TAPS, BASIS, rows * n_lat), F32),
            pltpu.VMEM((n_seg, BASIS, channels, channels), BF16),
            pltpu.VMEM((2, 2, rows, half, channels), BF16),
            pltpu.VMEM((own, own), BF16),
            pltpu.VMEM((n_seg + 1, spots, channels), BF16),
            pltpu.VMEM((n_seg, spots, channels), BF16),
            pltpu.VMEM((own, channels), BF16),
            pltpu.VMEM((2 * n_seg, own, channels), BF16),
            pltpu.VMEM((BASIS * own, spots), BF16),
            pltpu.VMEM((own, BASIS * spots), BF16),
            pltpu.VMEM((n_seg, BASIS * own, channels), BF16),
            pltpu.VMEM((BASIS * own, channels), BF16),
            pltpu.VMEM((own, channels), BF16),
            pltpu.VMEM((n_seg, own, channels), F32),
            pltpu.VMEM((BASIS * spots, channels), BF16),
            pltpu.VMEM((wide // LANES, BASIS * channels, LANES), F32),
            pltpu.VMEM((parts, ring, 2 * share * n_z, LANES), BF16),
            pltpu.VMEM((2, n_lat, parts, 2 * share * n_z, LANES), BF16),
            pltpu.VMEM((2, n_lat, parts, 2 * share * n_z, LANES), BF16),
            pltpu.VMEM((parts * 2 * share * n_z, LANES), F32),
            pltpu.VMEM((n_z, parts * 2 * share, LANES), BF16),
            pltpu.VMEM((n_z, parts * 2 * share, LANES), BF16),
            pltpu.VMEM((-(-share // 8) * 8, wide), F32),
            pltpu.VMEM((-(-share // 8) * 8, wide), F32),
            dma((2, 2)),
            dma((2, 2)),
            dma((2, 2 * BASIS)),
            dma((2, 2 * BASIS)),
            dma((2 * BASIS,)),
            dma((2 * BASIS,)),
            dma((3, 2 * BASIS)),
            dma((3, 2 * BASIS)),
            dma((3, 2 * BASIS, 2)),
            dma((3, 2 * BASIS, 2)),
            dma((2 * n_seg, 8)),
            dma((2 * n_seg, 8)),
            dma((2, 2)),
            dma((2, 2)),
            dma((3,)),
            dma((3,)),
            dma((2, n_lat, parts, 2)),
            dma((2, n_lat, parts, 2)),
            dma((n_z,)),
            dma((n_z,)),
            dma((4,)),
            pltpu.SemaphoreType.REGULAR((2, max(n_z // 2 - 1, 1))),
        ],
        compiler_params=pltpu.CompilerParams(
            collective_id=0, has_side_effects=True, vmem_limit_bytes=50331648
        ),
        name="section_step",
    )(
        *(
            pltpu.with_memory_space_constraint(array, pltpu.HBM)
            for array in (
                jnp.transpose(lat_step),
                jnp.transpose(lon_step),
                jnp.transpose(basis_values, (1, 2, 0)),
                inputs,
                cotangent,
                weights[0],
            )
        )
    )
    block = (1,) + inputs.shape
    return (
        section_out.reshape(block),
        section_grad.reshape(block),
        weight_grad.reshape(1, -1),
    )


def solution(mesh):
    return jax.shard_map(
        per_device,
        mesh=mesh,
        in_specs=(
            P(None, "lat", "lon", None),
            P(None, "lat", "lon", None),
            P("segment", None, None, None),
            P(),
            P(),
            P(),
        ),
        out_specs=(
            P("segment", None, "lat", "lon", None),
            P("segment", None, "lat", "lon", None),
            P("segment", ("lon", "lat")),
        ),
        check_vma=False,
    )
```

```python
import functools
import math

import jax
import jax.numpy as jnp
from jax import lax
from jax.experimental import pallas as pl
from jax.experimental.pallas import tpu as pltpu
from jax.sharding import PartitionSpec as P

BASIS = 3
TAPS = 9
REACH = 2
LANES = 128
MESH = pl.DeviceIdType.MESH
F32 = jnp.float32
BF16 = jnp.bfloat16


def log2(number):
    power = number.bit_length() - 1
    assert 1 << power == number
    return power


def over(x, number):
    return lax.shift_right_arithmetic(x, jnp.full_like(x, log2(number)))


def rest(x, number):
    return x & (number - 1)


def halo_cell(slot, rows, cols):
    base = 4 * rows
    at = slot
    side_row = over(rest(at, 2 * rows), 2)
    side_col = rest(at, 2) + jnp.where(at < 2 * rows, -2, cols)
    at = slot - base
    far_row = over(rest(at, 2 * cols), cols) + jnp.where(at < 2 * cols, -2, rows)
    far_col = rest(at, cols)
    at = slot - base - 4 * cols
    inside = rest(at, 8)
    corner_row = over(inside, 2) + jnp.where(at < 16, -2, rows)
    corner_col = rest(inside, 2) + jnp.where(rest(over(at, 8), 2) == 0, -2, cols)
    in_side = slot < base
    in_far = slot < base + 4 * cols
    row = jnp.where(in_side, side_row, jnp.where(in_far, far_row, corner_row))
    col = jnp.where(in_side, side_col, jnp.where(in_far, far_col, corner_col))
    used = in_far | (inside < 4)
    return row, col, used


def own_cell(spot, rows, half):
    second = over(spot, rows * half)
    at = rest(spot, rows * half)
    return over(at, half), rest(at, half) + second * half


def spot_of(row, col, rows, cols, half):
    own = rows * cols
    inner = (row >= 0) & (row < rows)
    mid = (col >= 0) & (col < cols)
    side = jnp.where(col < 0, col + 2, col - cols)
    far = jnp.where(row < 0, row + 2, row - rows)
    right = (col >= cols).astype(jnp.int32)
    down = (row >= rows).astype(jnp.int32)
    second = (col >= half).astype(jnp.int32)
    at_own = second * (rows * half) + row * half + col - second * half
    at_side = own + right * (2 * rows) + row * 2 + side
    base = own + 4 * rows
    at_far = base + down * (2 * cols) + far * cols + col
    at_corner = base + 4 * cols + (down * 2 + right) * 8 + far * 2 + side
    return jnp.where(
        inner, jnp.where(mid, at_own, at_side), jnp.where(mid, at_far, at_corner)
    )


def step_kernel(
    sizes,
    lat_hbm,
    lon_hbm,
    basis_hbm,
    in_ref,
    cot_ref,
    w_hbm,
    out_ref,
    grad_ref,
    wg_ref,
    lat_ref,
    lon_ref,
    basis_ref,
    w_all,
    raw,
    restored,
    pick,
    xp,
    gp,
    grad,
    hb,
    ahead,
    back,
    spread,
    spread_other,
    gate_other,
    slope,
    feat,
    product,
    blk,
    ysend,
    yrecv,
    acc,
    zsend,
    zrecv,
    fsend,
    frecv,
    cin_s,
    cin_r,
    own_s,
    own_r,
    far_s,
    far_r,
    side_s,
    side_r,
    swap_s,
    swap_r,
    halo_s,
    halo_r,
    oc_s,
    oc_r,
    pair_s,
    pair_r,
    y_s,
    y_r,
    z_s,
    z_r,
    w_sem,
    tokens,
):
    n_seg, n_lat, n_z, scale = sizes
    rows, half, channels = in_ref.shape[1:]
    half_cells = rows * half
    cols = 2 * half
    own = rows * cols
    spots = 2 * own
    ring = 2 * n_lat
    steps = ring // 2
    share = BASIS * channels // (n_z * ring * 2)
    wide = channels // 2

    lon = lax.axis_index("lon")
    lat = lax.axis_index("lat")
    seg = lax.axis_index("segment")
    z = lon // 4
    member = (lon // 2) % 2
    core = lon % 2
    pos = z * 2 + core
    y = member * n_lat + lat

    def at(z_to, member_to, core_to, lat_to, seg_to=seg):
        return {"lon": z_to * 4 + member_to * 2 + core_to, "lat": lat_to, "segment": seg_to}

    def beside(shift, lat_to):
        place = lax.rem(pos + shift + 2 * n_z, 2 * n_z)
        return at(place // 2, member, place % 2, lat_to)

    has_up = lat > 0
    has_down = lat < n_lat - 1
    seg_next = lax.rem(seg + 1, n_seg)
    seg_prev = lax.rem(seg + n_seg - 1, n_seg)
    seg_far = lax.rem(seg + 2, n_seg)
    matched = core == member

    base = 4 * rows
    corner = base + 4 * cols
    halo = [
        (0, 2 * rows, 1, 0),
        (2 * rows, 2 * rows, -1, 0),
        (base, 2 * cols, 0, 1),
        (base + 2 * cols, 2 * cols, 0, -1),
        (corner, 8, 1, 1),
        (corner + 8, 8, -1, 1),
        (corner + 16, 8, 1, -1),
        (corner + 24, 8, -1, -1),
    ]

    def sends_to(dlat):
        return has_down if dlat > 0 else has_up

    def gets_from(dlat):
        return has_up if dlat > 0 else has_down

    ring_next = lax.rem(y + 1, ring)
    ring_prev = lax.rem(y + ring - 1, ring)

    def on_ring(place):
        return at(z, place // n_lat, core, lax.rem(place, n_lat))

    partner = at(z, member, 1 - core, lat)

    fetch = pltpu.make_async_copy(w_hbm, w_all.at[seg], w_sem.at[0])
    tables = [
        pltpu.make_async_copy(table_hbm, table_ref, w_sem.at[1 + number])
        for number, (table_hbm, table_ref) in enumerate(
            ((lat_hbm, lat_ref), (lon_hbm, lon_ref), (basis_hbm, basis_ref))
        )
    ]
    for table in tables:
        table.start()
    fetch.start()

    barrier = pltpu.get_barrier_semaphore()

    def greet(device):
        pl.semaphore_signal(barrier, inc=1, device_id=device, device_id_type=MESH)

    z_next = at(lax.rem(z + 1, n_z), member, core, lat)
    z_prev = at(lax.rem(z + n_z - 1, n_z), member, core, lat)
    greet(z_next)
    greet(z_prev)
    greet(on_ring(ring_next))
    greet(on_ring(ring_prev))
    greet(partner)
    for _, _, shift, dlat in halo:
        if dlat == 0:
            greet(beside(shift, lat))
        else:

            @pl.when(sends_to(dlat))
            def _():
                greet(beside(shift, lat + dlat))

    for other in range(2):

        @pl.when(jnp.logical_not(matched & (member == other)))
        def _():
            greet(at(z, other, member, lat))

        @pl.when(jnp.logical_not(matched & (core == other)))
        def _():
            greet(at(z, core, other, lat))

    greet(at(z, member, core, lat, seg_next))
    greet(at(z, member, core, lat, seg_prev))

    met = 2 + 3 + 2 + 4 + 2
    met = met + jnp.where(has_up, 3, 0) + jnp.where(has_down, 3, 0)
    met = met - jnp.where(matched, 2, 0)
    pl.semaphore_wait(barrier, met)

    def remote(src, dst, send_sem, recv_sem, device):
        return pltpu.make_async_remote_copy(
            src_ref=src,
            dst_ref=dst,
            send_sem=send_sem,
            recv_sem=recv_sem,
            device_id=device,
            device_id_type=MESH,
        )

    def slot_of(buffer, part):
        return buffer.at[part]

    def regroup(source, buffer, which):
        for to in range(2):
            there = matched & (member == to)

            @pl.when(there)
            def _():
                pltpu.make_async_copy(
                    source.at[to], slot_of(buffer, core), cin_r.at[which, core]
                ).start()

            @pl.when(jnp.logical_not(there))
            def _():
                remote(
                    source.at[to],
                    slot_of(buffer, core),
                    cin_s.at[which, to],
                    cin_r.at[which, core],
                    at(z, to, member, lat),
                ).start()

    def regroup_arrived(source, buffer, which):
        for part in range(2):
            here = matched & (core == part)

            @pl.when(here)
            def _():
                pltpu.make_async_copy(
                    source.at[0], slot_of(buffer, part), cin_r.at[which, part]
                ).wait()

            @pl.when(jnp.logical_not(here))
            def _():
                remote(
                    source.at[0],
                    slot_of(buffer, part),
                    cin_s.at[which, 0],
                    cin_r.at[which, part],
                    partner,
                ).wait_recv()

    def regroup_sent(source, buffer, which):
        for to in range(2):

            @pl.when(jnp.logical_not(matched & (member == to)))
            def _():
                remote(
                    source.at[to],
                    slot_of(buffer, core),
                    cin_s.at[which, to],
                    cin_r.at[which, core],
                    partner,
                ).wait_send()

    regroup(in_ref, raw.at[0], 0)

    rounds = n_z // 2 - 1

    def token(number):
        if 1 < number <= rounds + 1:
            for way in range(2):
                pl.semaphore_wait(tokens.at[way, number - 2], 1)
        if number <= rounds:
            for way, neighbour in enumerate((z_next, z_prev)):
                pl.semaphore_signal(
                    tokens.at[way, number - 1],
                    inc=1,
                    device_id=neighbour,
                    device_id_type=MESH,
                )

    token(1)

    n_pieces = 2 * BASIS
    part_rows = channels // 8
    orders = (tuple(range(n_pieces)), tuple((k + BASIS) % n_pieces for k in range(n_pieces)))
    sections = (seg_prev, seg_next, seg_far)
    parity = lax.rem(z, 2)

    def piece(weights, k, of_parity, of_core):
        start = (2 * of_parity + of_core) * (channels // 4) + (k % 2) * part_rows
        return weights.at[k // 2, pl.ds(pl.multiple_of(start, part_rows), part_rows), :]

    def own_copy(way, k):
        return remote(
            piece(w_hbm, k, parity, core),
            piece(w_all.at[seg], k, parity, core),
            own_s.at[way, k],
            own_r.at[way, k],
            at(z, member, core, lat, seg_prev if way else seg_next),
        )

    def own_landed(way, k):
        landing = piece(w_all.at[sections[way]], k, parity, core)
        remote(landing, landing, own_s.at[way, k], own_r.at[way, k], partner).wait_recv()

    def far_copy(way, k):
        moved = piece(w_all.at[sections[way]], k, parity, core)
        return remote(
            moved,
            moved,
            far_s.at[k],
            far_r.at[k],
            at(z, member, core, lat, seg_prev if way else seg_next),
        )

    def far_landed(k):
        landing = piece(w_all.at[seg_far], k, parity, core)
        remote(landing, landing, far_s.at[k], far_r.at[k], partner).wait_recv()

    def side_copy(which, k):
        moved = piece(w_all.at[sections[which]], k, parity, core)
        return remote(
            moved, moved, side_s.at[which, k], side_r.at[which, k], z_prev if k % 2 else z_next
        )

    def side_landed(which, k):
        landing = piece(w_all.at[sections[which]], k, 1 - parity, core)
        remote(landing, landing, side_s.at[which, k], side_r.at[which, k], partner).wait_recv()

    def swap_copy(which, k, other):
        moved = piece(w_all.at[sections[which]], k, 1 - parity if other else parity, core)
        return remote(
            moved, moved, swap_s.at[which, k, other], swap_r.at[which, k, other], partner
        )

    def swap_landed(which, k, other):
        landing = piece(w_all.at[sections[which]], k, 1 - parity if other else parity, 1 - core)
        remote(
            landing, landing, swap_s.at[which, k, other], swap_r.at[which, k, other], partner
        ).wait_recv()

    for step in range(n_pieces):
        for way in range(2):
            own_copy(way, orders[way][step]).start()

    def pump_near(first, last):
        for step in range(first, last):
            for way in range(2):
                k = orders[way][step]
                own_landed(way, k)
                side_copy(way, k).start()
                if step < BASIS:
                    far_copy(way, k).start()
                swap_copy(way, k, 0).start()

    def finish_near():
        for step in range(n_pieces):
            for way in (1, 0):
                k = orders[way][step]
                side_landed(way, k)
                swap_copy(way, k, 1).start()

    def pump_far():
        for step in range(BASIS):
            for way in range(2):
                k = orders[way][step]
                far_landed(k)
                side_copy(2, k).start()
                swap_copy(2, k, 0).start()

    def near_landed(way):
        for k in orders[way]:
            for other in range(2):
                swap_landed(way, k, other)

    def weights_here(section):
        pl.when(seg_far == section)(finish_far)
        for way in range(2):

            @pl.when(sections[way] == section)
            def _():
                near_landed(way)

    def finish_far():
        for k in range(n_pieces):
            side_landed(2, k)
            swap_copy(2, k, 1).start()
        for k in range(n_pieces):
            for other in range(2):
                swap_landed(2, k, other)

    for buffer in [xp.at[s] for s in range(n_seg)] + [gp.at[s] for s in range(n_seg)]:

        @pl.when(jnp.logical_not(has_up))
        def _():
            buffer[pl.ds(own + base, 2 * cols), :] = jnp.zeros((2 * cols, channels), BF16)
            buffer[pl.ds(own + corner, 16), :] = jnp.zeros((16, channels), BF16)

        @pl.when(jnp.logical_not(has_down))
        def _():
            buffer[pl.ds(own + base + 2 * cols, 2 * cols), :] = jnp.zeros((2 * cols, channels), BF16)
            buffer[pl.ds(own + corner + 16, 16), :] = jnp.zeros((16, channels), BF16)

    spot = lax.broadcasted_iota(jnp.int32, (16, spots), 1)
    inner_row, inner_col = own_cell(spot, rows, half)
    outer_row, outer_col, used = halo_cell(spot - own, rows, cols)
    spot_row = jnp.where(spot < own, inner_row, outer_row)
    spot_col = jnp.where(spot < own, inner_col, outer_col)
    used = (spot < own) | used
    grid_row = jnp.where(used, spot_row + lat * rows, -1)[:1]
    total_rows = n_lat * rows
    chosen = (
        lax.broadcasted_iota(jnp.int32, (total_rows, spots), 0)
        == jnp.broadcast_to(grid_row, (total_rows, spots))
    ).astype(F32).astype(BF16)

    for table in tables:
        table.wait()

    def of_spot(taps):
        return jnp.dot(taps.astype(F32).astype(BF16), chosen, preferred_element_type=F32)

    to_row = of_spot(lat_ref[...]).astype(jnp.int32) + spot_row[:TAPS]
    to_col = of_spot(lon_ref[...]).astype(jnp.int32) + spot_col[:TAPS]
    worth = [of_spot(basis_ref[:, b, :]) for b in range(BASIS)]

    lands = (to_row >= 0) & (to_row < rows) & (to_col >= 0) & (to_col < cols)
    second = (to_col >= half).astype(jnp.int32)
    target = jnp.where(
        lands, second * (rows * half) + to_row * half + to_col - second * half, -1
    )
    level = lax.broadcasted_iota(jnp.int32, (own, spots), 0)
    totals = [jnp.zeros((own, spots), F32) for _ in range(BASIS)]
    for tap in range(TAPS):
        hit = level == target[tap : tap + 1, :]
        for b in range(BASIS):
            totals[b] = totals[b] + jnp.where(hit, worth[b][tap : tap + 1, :], 0.0)
    for b in range(BASIS):
        back[:, pl.ds(b * spots, spots)] = totals[b].astype(BF16)

    tap_row, tap_col = to_row[:, :own], to_col[:, :own]
    in_grid = (tap_row + lat * rows >= 0) & (tap_row + lat * rows < total_rows)
    source = jnp.where(in_grid, spot_of(tap_row, tap_col, rows, cols, half), -1)
    level = lax.broadcasted_iota(jnp.int32, (spots, own), 0)
    totals = [jnp.zeros((spots, own), F32) for _ in range(BASIS)]
    for tap in range(TAPS):
        hit = level == source[tap : tap + 1, :]
        for b in range(BASIS):
            totals[b] = totals[b] + jnp.where(hit, worth[b][tap : tap + 1, :own], 0.0)
    for b in range(BASIS):
        ahead[pl.ds(b * own, own), :] = jnp.transpose(totals[b]).astype(BF16)

    slot = lax.broadcasted_iota(jnp.int32, (own, own), 0)
    pick_row, pick_col, used = halo_cell(slot, rows, cols)
    pick_row, pick_col = rest(pick_row, rows), rest(pick_col, cols)
    wanted = over(pick_col, half) * (rows * half) + pick_row * half + rest(pick_col, half)
    wanted = jnp.where(used, wanted, -1)
    pick[...] = (
        (lax.broadcasted_iota(jnp.int32, (own, own), 1) == wanted).astype(F32).astype(BF16)
    )

    def halo_copy(buffer, phase, number):
        start, size, shift, dlat = halo[number]
        return remote(
            hb.at[phase, pl.ds(start, size), :],
            buffer.at[pl.ds(own + start, size), :],
            halo_s.at[phase, number],
            halo_r.at[phase, number],
            beside(shift, lat + dlat),
        )

    def halo_start(block, buffer, phase):
        hb[phase] = jnp.dot(pick[...], block, preferred_element_type=F32).astype(BF16)
        for number in (4, 5, 6, 7, 2, 3, 0, 1):
            dlat = halo[number][3]
            if dlat == 0:
                halo_copy(buffer, phase, number).start()
            else:

                @pl.when(sends_to(dlat))
                def _():
                    halo_copy(buffer, phase, number).start()

    def halo_arrived(buffer, phase):
        for number in range(8):
            dlat = halo[number][3]
            if dlat == 0:
                halo_copy(buffer, phase, number).wait_recv()
            else:

                @pl.when(gets_from(dlat))
                def _():
                    halo_copy(buffer, phase, number).wait_recv()

    def halo_sent(buffer, phase):
        for number in range(8):
            dlat = halo[number][3]
            if dlat == 0:
                halo_copy(buffer, phase, number).wait_send()
            else:

                @pl.when(sends_to(dlat))
                def _():
                    halo_copy(buffer, phase, number).wait_send()

    def restore_copy(output, which, part, arrives_from):
        return remote(
            restored.at[which, part],
            output.at[arrives_from],
            oc_s.at[which, part],
            oc_r.at[which, arrives_from],
            at(z, core, part, lat),
        )

    def restore_start(block, output, which):
        for part in range(2):
            restored[which, part] = block[pl.ds(part * half_cells, half_cells), :].reshape(
                rows, half, channels
            )
            there = matched & (core == part)

            @pl.when(there)
            def _():
                pltpu.make_async_copy(
                    restored.at[which, part], output.at[member], oc_r.at[which, member]
                ).start()

            @pl.when(jnp.logical_not(there))
            def _():
                restore_copy(output, which, part, member).start()

    def restore_finish(output, which):
        for part in range(2):

            @pl.when(jnp.logical_not(matched & (core == part)))
            def _():
                restore_copy(output, which, part, member).wait_send()

        for origin in range(2):
            here = matched & (member == origin)

            @pl.when(here)
            def _():
                pltpu.make_async_copy(
                    restored.at[which, 0], output.at[origin], oc_r.at[which, origin]
                ).wait()

            @pl.when(jnp.logical_not(here))
            def _():
                restore_copy(output, which, 0, origin).wait_recv()

    pair_spread = remote(spread.at[seg], spread_other, pair_s.at[0], pair_r.at[0], partner)

    def forward(section):
        halo_arrived(xp.at[section], section)
        widened = xp[section]
        mixed = None
        for b in range(BASIS):
            picked = jnp.dot(
                ahead[pl.ds(b * own, own), :], widened, preferred_element_type=F32
            ).astype(BF16)
            spread[section, pl.ds(b * own, own), :] = picked
            term = jnp.dot(picked, w_all[section, b], preferred_element_type=F32)
            mixed = term if mixed is None else mixed + term
        sigma = 1.0 / (1.0 + jnp.exp(-mixed))
        result = (xp[section, pl.ds(0, own), :].astype(F32) + mixed * sigma).astype(BF16)
        xp[section + 1, pl.ds(0, own), :] = result
        if section + 1 < n_seg:
            halo_start(result, xp.at[section + 1], section + 1)
        slope[section] = sigma * (1.0 + mixed * (1.0 - sigma))

        @pl.when(seg == section)
        def _():
            restore_start(xp.at[section + 1], out_ref, 0)
            pair_spread.start()

    pump_near(0, 4)
    regroup_arrived(in_ref, raw.at[0], 0)
    xp[0, pl.ds(0, own), :] = raw[0].reshape(own, channels)
    token(2)
    halo_start(xp[0, pl.ds(0, own), :], xp.at[0], 0)
    token(3)
    regroup(cot_ref, raw.at[1], 1)
    pump_near(4, n_pieces)
    fetch.wait()

    @pl.when(seg == 0)
    def _():
        forward(0)

    finish_near()
    pump_far()
    @pl.when(seg != 0)
    def _():
        weights_here(0)
        forward(0)

    for section in range(1, n_seg):
        token(section + 3)
        weights_here(section)
        forward(section)
    for number in range(n_seg + 3, rounds + 1):
        token(number)

    regroup_arrived(cot_ref, raw.at[1], 1)
    grad[...] = raw[1].reshape(own, channels)

    def open_gate(section, then=None):
        gate = (grad[...].astype(F32) * slope[section]).astype(BF16)
        gp[section, pl.ds(0, own), :] = gate
        if then is not None:
            then()
        halo_start(gate, gp.at[section], n_seg + section)

    def pull(section):
        halo_arrived(gp.at[section], n_seg + section)
        for b in range(BASIS):
            feat[pl.ds(b * spots, spots), :] = lax.dot_general(
                gp[section], w_all[section, b], (((1,), (1,)), ((), ())), preferred_element_type=F32
            ).astype(BF16)
        pulled = jnp.dot(back[...], feat[...], preferred_element_type=F32)
        grad[...] = (grad[...].astype(F32) + pulled).astype(BF16)

    for section in range(n_seg - 1, 0, -1):

        @pl.when(seg < section)
        def _():
            open_gate(section)
            pull(section)

    pair_gate = remote(
        gp.at[seg, pl.ds(0, own), :], gate_other, pair_s.at[1], pair_r.at[1], partner
    )
    open_gate(seg, pair_gate.start)
    pair_spread.wait_recv()
    pair_gate.wait_recv()

    columns = pl.ds(pl.multiple_of(core * wide, wide), wide)
    gate_both = jnp.concatenate(
        [gp[seg, pl.ds(0, own), columns], gate_other[:, columns]], axis=0
    )
    for b in range(BASIS):
        both = jnp.concatenate(
            [spread[seg, pl.ds(b * own, own), :], spread_other[pl.ds(b * own, own), :]], axis=0
        )
        term = scale * lax.dot_general(
            both, gate_both, (((0,), (0,)), ((), ())), preferred_element_type=F32
        )
        for part in range(wide // LANES):
            product[part, pl.ds(b * channels, channels), :] = term[
                :, part * LANES : (part + 1) * LANES
            ]

    group = share * n_z

    parts = wide // LANES

    def ring_copy(way, step, part, e):
        return remote(
            ysend.at[way, step, part, pl.ds(e * group, group), :],
            yrecv.at[way, step, part, pl.ds(e * group, group), :],
            y_s.at[way, step, part, e],
            y_r.at[way, step, part, e],
            on_ring(ring_next if way == 0 else ring_prev),
        )

    def ring_step(step, way, part, e):
        distance = steps - step
        place = lax.rem(y + (distance if way == 0 else ring - distance), ring)
        span = pl.ds(e * group, group)
        term = blk[part, place, span, :]
        if step > 1 or (step == 1 and e == way):
            ring_copy(way, step - 1, part, e).wait_recv()
            term = (term.astype(F32) + yrecv[way, step - 1, part, span, :].astype(F32)).astype(
                BF16
            )
        ysend[way, step, part, span, :] = term
        ring_copy(way, step, part, e).start()

    def ring_begin():
        for part in range(parts):
            for place in range(ring):
                for e in range(2):
                    for i in range(share):
                        first = ((place // n_lat) * 2 + e) * n_lat * share
                        first = first + (place % n_lat) * share + i
                        blk[part, place, pl.ds(e * group + i * n_z, n_z), :] = product[
                            part, pl.ds(first, n_z, stride=ring * 2 * share), :
                        ].astype(BF16)
            for way in range(2):
                ring_step(0, way, part, way)
        for part in range(parts):
            for way in range(2):
                ring_step(1, way, part, 1 - way)

    ring_begin()
    for part in range(parts):
        for way in range(2):
            ring_step(1, way, part, way)
    pull(seg)
    restore_start(grad, grad_ref, 1)
    for step in range(2, steps):
        for half_turn in range(2):
            for part in range(parts):
                for way in range(2):
                    ring_step(step, way, part, way if half_turn else 1 - way)
    for part in range(parts):
        summed = blk[part, y].astype(F32)
        for way in range(2):
            for e in range(2):
                ring_copy(way, steps - 1, part, e).wait_recv()
            summed = summed + yrecv[way, steps - 1, part].astype(F32)
        acc[pl.ds(part * 2 * group, 2 * group), :] = summed

    def z_copy(shift):
        to = lax.rem(z + shift, n_z)
        return remote(
            zsend.at[to], zrecv.at[z], z_s.at[shift], z_r.at[shift], at(to, member, core, lat)
        )

    slab = parts * 2 * share
    for to in range(n_z):
        zsend[to] = acc[pl.ds(to, slab, stride=n_z), :].astype(BF16)
    token(rounds + 1)
    nearest = sorted(range(1, n_z), key=lambda shift: min(shift, n_z - shift))
    for shift in reversed(nearest):
        z_copy(shift).start()
    total = zsend[z].astype(F32)
    for shift in nearest:
        from_z = lax.rem(z + n_z - shift, n_z)
        remote(
            zsend.at[0], zrecv.at[from_z], z_s.at[shift], z_r.at[shift], partner
        ).wait_recv()
        total = total + zrecv[from_z].astype(F32)

    def rows_for(e):
        return jnp.concatenate(
            [
                total[(2 * part + e) * share : (2 * part + e + 1) * share]
                for part in range(parts)
            ],
            axis=1,
        )

    mine = jnp.where(core == 0, rows_for(0), rows_for(1))
    fsend[pl.ds(0, share), :] = jnp.where(core == 0, rows_for(1), rows_for(0))
    last = remote(fsend, frecv, pair_s.at[2], pair_r.at[2], partner)
    last.start()
    last.wait_recv()
    theirs = frecv[pl.ds(0, share), :]
    wg_ref[:, :wide] = jnp.where(core == 0, mine, theirs)
    wg_ref[:, wide:] = jnp.where(core == 0, theirs, mine)

    restore_finish(out_ref, 0)
    restore_finish(grad_ref, 1)
    regroup_sent(in_ref, raw.at[0], 0)
    regroup_sent(cot_ref, raw.at[1], 1)
    for k in range(n_pieces):
        for way in range(2):
            own_copy(way, k).wait_send()
        far_copy(k // BASIS, k).wait_send()
        for which in range(3):
            side_copy(which, k).wait_send()
            for other in range(2):
                swap_copy(which, k, other).wait_send()
    for section in range(n_seg):
        halo_sent(xp.at[section], section)

        @pl.when(seg <= section)
        def _():
            halo_sent(gp.at[section], n_seg + section)

    pair_spread.wait_send()
    pair_gate.wait_send()
    last.wait_send()
    for step in range(steps):
        for way in range(2):
            for part in range(parts):
                for e in range(2):
                    if step or e == way:
                        ring_copy(way, step, part, e).wait_send()
    for shift in range(1, n_z):
        z_copy(shift).wait_send()


def per_device(inputs, cotangent, weights, basis_values, lat_step, lon_step):
    members, rows, half, channels = inputs.shape
    n_lon, n_lat, n_seg = (lax.axis_size(name) for name in ("lon", "lat", "segment"))
    n_z = n_lon // 4
    cols = 2 * half
    own = rows * cols
    spots = 2 * own
    ring = 2 * n_lat
    share = BASIS * channels // (n_lon * n_lat)
    wide = channels // 2
    parts = wide // LANES
    scale = 1.0 / math.sqrt(members * rows * n_lat * half * n_lon)

    vmem = pl.BlockSpec(memory_space=pltpu.VMEM)
    hbm = pl.BlockSpec(memory_space=pltpu.HBM)
    dma = pltpu.SemaphoreType.DMA
    section_out, section_grad, weight_grad = pl.pallas_call(
        functools.partial(step_kernel, (n_seg, n_lat, n_z, scale)),
        out_shape=(
            jax.ShapeDtypeStruct((2, rows, half, channels), BF16),
            jax.ShapeDtypeStruct((2, rows, half, channels), BF16),
            jax.ShapeDtypeStruct((share, channels), F32),
        ),
        in_specs=[hbm] * 6,
        out_specs=(vmem, vmem, vmem),
        scratch_shapes=[
            pltpu.VMEM((TAPS, rows * n_lat), jnp.int32),
            pltpu.VMEM((TAPS, rows * n_lat), jnp.int32),
            pltpu.VMEM((TAPS, BASIS, rows * n_lat), F32),
            pltpu.VMEM((n_seg, BASIS, channels, channels), BF16),
            pltpu.VMEM((2, 2, rows, half, channels), BF16),
            pltpu.VMEM((2, 2, rows, half, channels), BF16),
            pltpu.VMEM((own, own), BF16),
            pltpu.VMEM((n_seg + 1, spots, channels), BF16),
            pltpu.VMEM((n_seg, spots, channels), BF16),
            pltpu.VMEM((own, channels), BF16),
            pltpu.VMEM((2 * n_seg, own, channels), BF16),
            pltpu.VMEM((BASIS * own, spots), BF16),
            pltpu.VMEM((own, BASIS * spots), BF16),
            pltpu.VMEM((n_seg, BASIS * own, channels), BF16),
            pltpu.VMEM((BASIS * own, channels), BF16),
            pltpu.VMEM((own, channels), BF16),
            pltpu.VMEM((n_seg, own, channels), F32),
            pltpu.VMEM((BASIS * spots, channels), BF16),
            pltpu.VMEM((wide // LANES, BASIS * channels, LANES), F32),
            pltpu.VMEM((parts, ring, 2 * share * n_z, LANES), BF16),
            pltpu.VMEM((2, n_lat, parts, 2 * share * n_z, LANES), BF16),
            pltpu.VMEM((2, n_lat, parts, 2 * share * n_z, LANES), BF16),
            pltpu.VMEM((parts * 2 * share * n_z, LANES), F32),
            pltpu.VMEM((n_z, parts * 2 * share, LANES), BF16),
            pltpu.VMEM((n_z, parts * 2 * share, LANES), BF16),
            pltpu.VMEM((-(-share // 8) * 8, wide), F32),
            pltpu.VMEM((-(-share // 8) * 8, wide), F32),
            dma((2, 2)),
            dma((2, 2)),
            dma((2, 2 * BASIS)),
            dma((2, 2 * BASIS)),
            dma((2 * BASIS,)),
            dma((2 * BASIS,)),
            dma((3, 2 * BASIS)),
            dma((3, 2 * BASIS)),
            dma((3, 2 * BASIS, 2)),
            dma((3, 2 * BASIS, 2)),
            dma((2 * n_seg, 8)),
            dma((2 * n_seg, 8)),
            dma((2, 2)),
            dma((2, 2)),
            dma((3,)),
            dma((3,)),
            dma((2, n_lat, parts, 2)),
            dma((2, n_lat, parts, 2)),
            dma((n_z,)),
            dma((n_z,)),
            dma((4,)),
            pltpu.SemaphoreType.REGULAR((2, max(n_z // 2 - 1, 1))),
        ],
        compiler_params=pltpu.CompilerParams(
            collective_id=0, has_side_effects=True, vmem_limit_bytes=50331648
        ),
        name="section_step",
    )(
        *(
            pltpu.with_memory_space_constraint(array, pltpu.HBM)
            for array in (
                jnp.transpose(lat_step),
                jnp.transpose(lon_step),
                jnp.transpose(basis_values, (1, 2, 0)),
                inputs,
                cotangent,
                weights[0],
            )
        )
    )
    block = (1,) + inputs.shape
    return (
        section_out.reshape(block),
        section_grad.reshape(block),
        weight_grad.reshape(1, -1),
    )


def solution(mesh):
    return jax.shard_map(
        per_device,
        mesh=mesh,
        in_specs=(
            P(None, "lat", "lon", None),
            P(None, "lat", "lon", None),
            P("segment", None, None, None),
            P(),
            P(),
            P(),
        ),
        out_specs=(
            P("segment", None, "lat", "lon", None),
            P("segment", None, "lat", "lon", None),
            P("segment", ("lon", "lat")),
        ),
        check_vma=False,
    )
```
